32 devices in a mesh: items: 8 (over z, x), patch: 4 (over y, core).
Axes of the slice: x: 2, y: 2, z: 4, core: 2. Of those that a mesh axis runs over, the one named last changes fastest.
Arguments:
- text: bfloat16 [10240, 768], P(('items', 'patch')), may hold values from -6 to 6
- cotangent: bfloat16 [10240, 768], P(('items', 'patch')), may hold values from -6 to 6
- patches: bfloat16 [256, 148, 1024], P('items', 'patch'), may hold values from -6 to 6
- text_lengths: int32 [256], P(('items', 'patch')), may hold values from 4 to 40
- patch_mask: int32 [256, 148], P('items', 'patch'), may hold values 0 or 1
- w_qkv: float32 [768, 2304], P(('items', 'patch')), may hold values from -0.21875 to 0.21875
- w_out: float32 [768, 768], P(('items', 'patch')), may hold values from -0.875 to 0.875
- w_cross_q: float32 [768, 768], P(('items', 'patch')), may hold values from -0.21875 to 0.21875
- w_cross_kv: float32 [1024, 1536], P(('items', 'patch')), may hold values from -0.1875 to 0.1875
- w_cross_out: float32 [768, 768], P(('items', 'patch')), may hold values from -1.75 to 1.75
- w_inner: float32 [768, 3072], P(('items', 'patch')), may hold values from -0.21875 to 0.21875
- w_outer: float32 [3072, 768], P(('items', 'patch')), may hold values from -0.109375 to 0.109375
- norm_rows: float32 [6, 768], P(None, ('items', 'patch')), may hold values from -0.4 to 1.4, as said below
- first_qkv: float32 [768, 2304], P(('items', 'patch')), may hold values from -32 to 32
- first_out: float32 [768, 768], P(('items', 'patch')), may hold values from -32 to 32
- first_cross_q: float32 [768, 768], P(('items', 'patch')), may hold values from -20 to 20
- first_cross_kv: float32 [1024, 1536], P(('items', 'patch')), may hold values from -64 to 64
- first_cross_out: float32 [768, 768], P(('items', 'patch')), may hold values from -14 to 14
- first_inner: float32 [768, 3072], P(('items', 'patch')), may hold values from -20 to 20
- first_outer: float32 [3072, 768], P(('items', 'patch')), may hold values from -40 to 40
- first_norms: float32 [6, 768], P(None, ('items', 'patch')), may hold values from -64 to 64
- second_qkv: float32 [768, 2304], P(('items', 'patch')), may hold values from 2.56 to 10.24
- second_out: float32 [768, 768], P(('items', 'patch')), may hold values from 2.56 to 10.24
- second_cross_q: float32 [768, 768], P(('items', 'patch')), may hold values from 0.9216 to 3.6864
- second_cross_kv: float32 [1024, 1536], P(('items', 'patch')), may hold values from 9.472 to 37.888
- second_cross_out: float32 [768, 768], P(('items', 'patch')), may hold values from 0.4096 to 1.6384
- second_inner: float32 [768, 3072], P(('items', 'patch')), may hold values from 0.9216 to 3.6864
- second_outer: float32 [3072, 768], P(('items', 'patch')), may hold values from 3.6864 to 14.7456
- second_norms: float32 [6, 768], P(None, ('items', 'patch')), may hold values from 10.24 to 40.96
Outputs:
- block_output: bfloat16 [10240, 768], P(('items', 'patch'))
- text_grad: float32 [10240, 768], P(('items', 'patch'))
- patch_grad: float32 [256, 148, 1024], P('items', 'patch')
- new_w_qkv: float32 [768, 2304], P(('items', 'patch'))
- new_w_out: float32 [768, 768], P(('items', 'patch'))
- new_w_cross_q: float32 [768, 768], P(('items', 'patch'))
- new_w_cross_kv: float32 [1024, 1536], P(('items', 'patch'))
- new_w_cross_out: float32 [768, 768], P(('items', 'patch'))
- new_w_inner: float32 [768, 3072], P(('items', 'patch'))
- new_w_outer: float32 [3072, 768], P(('items', 'patch'))
- new_norm_rows: float32 [6, 768], P(None, ('items', 'patch'))
- new_first_qkv: float32 [768, 2304], P(('items', 'patch'))
- new_first_out: float32 [768, 768], P(('items', 'patch'))
- new_first_cross_q: float32 [768, 768], P(('items', 'patch'))
- new_first_cross_kv: float32 [1024, 1536], P(('items', 'patch'))
- new_first_cross_out: float32 [768, 768], P(('items', 'patch'))
- new_first_inner: float32 [768, 3072], P(('items', 'patch'))
- new_first_outer: float32 [3072, 768], P(('items', 'patch'))
- new_first_norms: float32 [6, 768], P(None, ('items', 'patch'))
- new_second_qkv: float32 [768, 2304], P(('items', 'patch'))
- new_second_out: float32 [768, 768], P(('items', 'patch'))
- new_second_cross_q: float32 [768, 768], P(('items', 'patch'))
- new_second_cross_kv: float32 [1024, 1536], P(('items', 'patch'))
- new_second_cross_out: float32 [768, 768], P(('items', 'patch'))
- new_second_inner: float32 [768, 3072], P(('items', 'patch'))
- new_second_outer: float32 [3072, 768], P(('items', 'patch'))
- new_second_norms: float32 [6, 768], P(None, ('items', 'patch'))
The draws below stay inside these ranges and needn't reach their ends.
Inputs may be any that keep to these rules, and one draw needn't show every extreme that they name: `norm_rows`: rows 0, 2 and 4 are gains near one, rows 1, 3 and 5 biases near zero.
All inputs are finite; a program needn't handle non-finite values. No bound on the sum of `patch_mask` on one device may be relied on, other than what follows from the above.
Results may differ from the reference program's by a relative error of at most 0.033.
Values may be sent and summed in bfloat16 or wider, within the bound.
A program may use at most 256 MiB of HBM per device.

```python
import math
import jax
import jax.numpy as jnp
from jax import lax

D = 768
HEADS = 12
HEAD_DIM = 64
FF = 3072
ENC = 1024
TEXT = 40
PATCHES = 148
VALID = 145
ITEMS = 256
N_ITEMS = 8


def draw_norm_rows(key, part):
    gain_key, shift_key = jax.random.split(jax.random.fold_in(key, 17))
    gains = 1.0 + 0.1 * jnp.clip(jax.random.normal(gain_key, (3, D), jnp.float32), -4.0, 4.0)
    shifts = 0.1 * jnp.clip(jax.random.normal(shift_key, (3, D), jnp.float32), -4.0, 4.0)
    return jnp.stack([gains, shifts], axis=1).reshape(6, D)


def plant(drawn, rng, least, top_value):
    extent = drawn.shape
    place = [jax.random.randint(jax.random.fold_in(rng, axis), (), 0, extent[axis]) for axis in range(len(extent))]
    drawn = drawn.at[tuple(place)].set(least)
    longest = extent.index(max(extent))
    place[longest] = (place[longest] + 1) % extent[longest]
    return drawn.at[tuple(place)].set(top_value)


def shard_levels(own_key, shape, cuts, smallest, top_value):
    level = 1.0
    for axis_at, shards_of in cuts:
        draws = jax.random.uniform(jax.random.fold_in(jax.random.fold_in(own_key, 6), axis_at), (shards_of,), jnp.float32, smallest / len(cuts), top_value / len(cuts))
        level = level * jnp.repeat(jnp.exp(draws), shape[axis_at] // shards_of).reshape((-1,) + (1,) * (len(shape) - 1 - axis_at))
    return level


def bell_draw(own_key, extent, scale, most, cuts=(), kind=jnp.bfloat16):
    loudness = shard_levels(own_key, extent, cuts, -0.22, 0.18) if cuts else 1.0
    drawn = jax.random.normal(own_key, extent, jnp.float32) * scale * loudness
    return jnp.minimum(jnp.maximum(drawn, -most), most).astype(kind)


def setup_inputs(seed: int = 0) -> dict:
    keys = jax.random.split(jax.random.key(seed), 30)
    text = bell_draw(keys[0], (ITEMS * TEXT, D), 1.0, 6.0, ((0, 32),))
    cotangent = bell_draw(keys[1], (ITEMS * TEXT, D), 1.0, 6.0, ((0, 32),))
    patches = bell_draw(keys[2], (ITEMS, PATCHES, ENC), 1.0, 6.0, ((0, 8), (1, 4)))
    text_lengths = plant(jax.random.randint(keys[3], (ITEMS,), 4, TEXT + 1), jax.random.fold_in(keys[3], 1), 4, TEXT).astype(jnp.int32)
    patch_mask = plant((jax.random.randint(keys[4], (ITEMS, PATCHES), 0, 8) < 7).astype(jnp.int32), jax.random.fold_in(keys[4], 1), 0, 1)
    w_qkv = bell_draw(keys[5], (D, 3 * D), D ** -0.5, 0.21875, ((0, 32),), jnp.float32)
    w_out = bell_draw(keys[6], (D, D), (D // 16) ** -0.5, 0.875, ((0, 32),), jnp.float32)
    w_cross_q = bell_draw(keys[7], (D, D), D ** -0.5, 0.21875, ((0, 32),), jnp.float32)
    w_cross_kv = bell_draw(keys[8], (ENC, 2 * D), ENC ** -0.5, 0.1875, ((0, 32),), jnp.float32)
    w_cross_out = bell_draw(keys[9], (D, D), (D // 64) ** -0.5, 1.75, ((0, 32),), jnp.float32)
    w_inner = bell_draw(keys[10], (D, FF), D ** -0.5, 0.21875, ((0, 32),), jnp.float32)
    w_outer = bell_draw(keys[11], (FF, D), FF ** -0.5, 0.109375, ((0, 32),), jnp.float32)
    norm_rows = draw_norm_rows(jax.random.fold_in(keys[29], 71), 0)
    first_qkv = bell_draw(keys[13], (D, 3 * D), (0.055 * (ITEMS * TEXT) ** 0.5), 32.0, ((0, 32),), jnp.float32)
    first_out = bell_draw(keys[14], (D, D), (0.055 * (ITEMS * TEXT) ** 0.5), 32.0, ((0, 32),), jnp.float32)
    first_cross_q = bell_draw(keys[15], (D, D), (0.033 * (ITEMS * TEXT) ** 0.5), 20.0, ((0, 32),), jnp.float32)
    first_cross_kv = bell_draw(keys[16], (ENC, 2 * D), (0.055 * (ITEMS * PATCHES) ** 0.5), 64.0, ((0, 32),), jnp.float32)
    first_cross_out = bell_draw(keys[17], (D, D), (0.022 * (ITEMS * TEXT) ** 0.5), 14.0, ((0, 32),), jnp.float32)
    first_inner = bell_draw(keys[18], (D, FF), (0.033 * (ITEMS * TEXT) ** 0.5), 20.0, ((0, 32),), jnp.float32)
    first_outer = bell_draw(keys[19], (FF, D), (0.066 * (ITEMS * TEXT) ** 0.5), 40.0, ((0, 32),), jnp.float32)
    first_norms = bell_draw(keys[20], (6, D), (0.11 * (ITEMS * TEXT) ** 0.5), 64.0, ((1, 32),), jnp.float32)
    second_qkv = jnp.clip(jnp.exp(math.log(10.24) - 1.3862944 * jax.random.uniform(keys[21], (D, 3 * D), jnp.float32) ** shard_levels(keys[21], (D, 3 * D), ((0, 32),), -0.2, 0.2)), 2.56, 10.24)
    second_out = jnp.clip(jnp.exp(math.log(10.24) - 1.3862944 * jax.random.uniform(keys[22], (D, D), jnp.float32) ** shard_levels(keys[22], (D, D), ((0, 32),), -0.2, 0.2)), 2.56, 10.24)
    second_cross_q = jnp.clip(jnp.exp(math.log(3.6864) - 1.3862944 * jax.random.uniform(keys[23], (D, D), jnp.float32) ** shard_levels(keys[23], (D, D), ((0, 32),), -0.2, 0.2)), 0.9216, 3.6864)
    second_cross_kv = jnp.clip(jnp.exp(math.log(37.888) - 1.3862944 * jax.random.uniform(keys[24], (ENC, 2 * D), jnp.float32) ** shard_levels(keys[24], (ENC, 2 * D), ((0, 32),), -0.2, 0.2)), 9.472, 37.888)
    second_cross_out = jnp.clip(jnp.exp(math.log(1.6384) - 1.3862944 * jax.random.uniform(keys[25], (D, D), jnp.float32) ** shard_levels(keys[25], (D, D), ((0, 32),), -0.2, 0.2)), 0.4096, 1.6384)
    second_inner = jnp.clip(jnp.exp(math.log(3.6864) - 1.3862944 * jax.random.uniform(keys[26], (D, FF), jnp.float32) ** shard_levels(keys[26], (D, FF), ((0, 32),), -0.2, 0.2)), 0.9216, 3.6864)
    second_outer = jnp.clip(jnp.exp(math.log(14.7456) - 1.3862944 * jax.random.uniform(keys[27], (FF, D), jnp.float32) ** shard_levels(keys[27], (FF, D), ((0, 32),), -0.2, 0.2)), 3.6864, 14.7456)
    second_norms = jnp.clip(jnp.exp(math.log(40.96) - 1.3862944 * jax.random.uniform(keys[28], (6, D), jnp.float32) ** shard_levels(keys[28], (6, D), ((1, 32),), -0.2, 0.2)), 10.24, 40.96)
    return dict(text=text, cotangent=cotangent, patches=patches, text_lengths=text_lengths, patch_mask=patch_mask, w_qkv=w_qkv, w_out=w_out, w_cross_q=w_cross_q, w_cross_kv=w_cross_kv, w_cross_out=w_cross_out, w_inner=w_inner, w_outer=w_outer, norm_rows=norm_rows, first_qkv=first_qkv, first_out=first_out, first_cross_q=first_cross_q, first_cross_kv=first_cross_kv, first_cross_out=first_cross_out, first_inner=first_inner, first_outer=first_outer, first_norms=first_norms, second_qkv=second_qkv, second_out=second_out, second_cross_q=second_cross_q, second_cross_kv=second_cross_kv, second_cross_out=second_cross_out, second_inner=second_inner, second_outer=second_outer, second_norms=second_norms)


@jax.custom_vjp
def low(v):
    return lax.optimization_barrier(v.astype(jnp.bfloat16)).astype(jnp.float32)

@jax.custom_vjp
def low_back(v):
    return v

def low_keep(v):
    return (low(v), None)

def low_pass(kept, grad):
    return (grad,)

def back_keep(v):
    return (v, None)

def back_low(kept, grad):
    return (low(grad),)
low.defvjp(low_keep, low_pass)
low_back.defvjp(back_keep, back_low)
step_rates = (0.05, 0.15, 0.05, 0.05, 0.3, 0.05, 0.05, 0.5)
step_decays = (0.01, 0.01, 0.01, 0.01, 0.01, 0.01, 0.01, 0.0)

def dense(left_side, right_side):
    return jnp.dot(left_side, right_side, precision=lax.Precision.HIGHEST, preferred_element_type=jnp.float32)

def layer_norm(values, norm_gain, norm_shift):
    center = values - lax.optimization_barrier(jnp.mean(values, axis=-1, keepdims=True))
    spread = lax.optimization_barrier(jnp.mean(center * center, axis=-1, keepdims=True))
    return center * lax.rsqrt(spread + 1e-12) * norm_gain + norm_shift

def attend(query_rows, key_rows, value_rows, key_bias):
    scores = jnp.einsum('bqhe,bkhe->bhqk', query_rows, key_rows, precision=lax.Precision.HIGHEST)
    scores = low_back(scores * HEAD_DIM ** (-0.5) + key_bias[:, None, None, :])
    probs_low = low(jax.nn.softmax(scores, axis=-1))
    return jnp.einsum('bhqk,bkhe->bqhe', probs_low, value_rows, precision=lax.Precision.HIGHEST)

def forward(weights, text_rows, image_rows, self_bias, patch_bias):
    w_qkv, w_out, w_cross_q, w_cross_kv, w_cross_out, w_inner, w_outer, norm_rows = weights
    item_count = self_bias.shape[0]
    mixed_rows = low_back(low(dense(text_rows, w_qkv))).reshape(item_count, TEXT, 3, HEADS, HEAD_DIM)
    self_ctx = attend(mixed_rows[:, :, 0], mixed_rows[:, :, 1], mixed_rows[:, :, 2], self_bias)
    self_ctx = low_back(low(self_ctx.reshape(item_count * TEXT, D)))
    after_self = layer_norm(text_rows + low_back(dense(self_ctx, w_out)), norm_rows[0], norm_rows[1])
    cross_query = low_back(low(dense(low(after_self), w_cross_q))).reshape(item_count, TEXT, HEADS, HEAD_DIM)
    memory = low_back(low(dense(image_rows, w_cross_kv))).reshape(item_count, PATCHES, 2, HEADS, HEAD_DIM)
    cross_ctx = attend(cross_query, memory[:, :, 0], memory[:, :, 1], patch_bias)
    cross_ctx = low_back(low(cross_ctx.reshape(item_count * TEXT, D)))
    after_cross = layer_norm(after_self + low_back(dense(cross_ctx, w_cross_out)), norm_rows[2], norm_rows[3])
    inner_pre = low_back(dense(low(after_cross), w_inner))
    hidden = low(jax.nn.gelu(inner_pre, approximate=False))
    return layer_norm(after_cross + low_back(dense(hidden, w_outer)), norm_rows[4], norm_rows[5])

def adamw_step(master, gradient, first_moment, second_moment, rate, decay):
    first_new = 0.9 * first_moment + 0.1 * gradient
    second_new = 0.999 * second_moment + 0.001 * gradient * gradient
    step_size = first_new / (1.0 - 0.9 ** 10) / (jnp.sqrt(second_new / (1.0 - 0.999 ** 10)) + 1e-08)
    return (master - rate * (step_size + decay * master), first_new, second_new)

def add_pair(running, addend):
    return running + addend

def reference(text, cotangent, patches, text_lengths, patch_mask, w_qkv, w_out, w_cross_q, w_cross_kv, w_cross_out, w_inner, w_outer, norm_rows, first_qkv, first_out, first_cross_q, first_cross_kv, first_cross_out, first_inner, first_outer, first_norms, second_qkv, second_out, second_cross_q, second_cross_kv, second_cross_out, second_inner, second_outer, second_norms):
    masters = (w_qkv, w_out, w_cross_q, w_cross_kv, w_cross_out, w_inner, w_outer, norm_rows)
    firsts = (first_qkv, first_out, first_cross_q, first_cross_kv, first_cross_out, first_inner, first_outer, first_norms)
    seconds = (second_qkv, second_out, second_cross_q, second_cross_kv, second_cross_out, second_inner, second_outer, second_norms)
    params = tuple((low(master) for master in masters))
    group_items = ITEMS // N_ITEMS
    positions = jnp.arange(TEXT, dtype=jnp.int32)
    self_bias = jnp.where(positions[None, :] < text_lengths[:, None], 0.0, -10000.0).astype(jnp.float32)
    patch_index = jnp.arange(PATCHES, dtype=jnp.int32)
    patch_valid = (patch_mask > 0) & (patch_index[None, :] < VALID)
    patch_bias = jnp.where(patch_valid, 0.0, -10000.0).astype(jnp.float32)
    blocks = (text.reshape(N_ITEMS, group_items * TEXT, D), cotangent.reshape(N_ITEMS, group_items * TEXT, D), patches.reshape(N_ITEMS, group_items * PATCHES, ENC), self_bias.reshape(N_ITEMS, group_items, TEXT), patch_bias.reshape(N_ITEMS, group_items, PATCHES))
    zero_grads = tuple((jnp.zeros(master.shape, jnp.float32) for master in masters))

    def one_block(running, block_data):
        text_block, cot_block, image_block, self_part, patch_part = block_data

        def apply_layer(weights, text_in, image_in):
            return forward(weights, text_in, image_in, self_part, patch_part)
        result, pullback = jax.vjp(apply_layer, params, text_block.astype(jnp.float32), image_block.astype(jnp.float32))
        weight_grads, text_part, image_part = pullback(cot_block.astype(jnp.float32))
        running = jax.tree.map(add_pair, running, weight_grads)
        return (running, (result.astype(jnp.bfloat16), text_part, image_part))
    weight_grads, (outputs, text_grads, image_grads) = lax.scan(one_block, zero_grads, blocks)
    block_output = outputs.reshape(ITEMS * TEXT, D)
    text_grad = text_grads.reshape(ITEMS * TEXT, D)
    patch_grad = image_grads.reshape(ITEMS, PATCHES, ENC)
    new_masters = []
    new_firsts = []
    new_seconds = []
    for position in range(8):
        updated = adamw_step(masters[position], weight_grads[position], firsts[position], seconds[position], step_rates[position], step_decays[position])
        new_masters.append(updated[0])
        new_firsts.append(updated[1])
        new_seconds.append(updated[2])
    return (block_output, text_grad, patch_grad, new_masters[0], new_masters[1], new_masters[2], new_masters[3], new_masters[4], new_masters[5], new_masters[6], new_masters[7], new_firsts[0], new_firsts[1], new_firsts[2], new_firsts[3], new_firsts[4], new_firsts[5], new_firsts[6], new_firsts[7], new_seconds[0], new_seconds[1], new_seconds[2], new_seconds[3], new_seconds[4], new_seconds[5], new_seconds[6], new_seconds[7])
```

```python
import functools

import jax
import jax.numpy as jnp
from jax import lax
from jax.experimental import pallas as pl
from jax.experimental.pallas import tpu as pltpu
from jax.sharding import PartitionSpec as P

D = 768
HEADS = 12
HEAD_DIM = 64
ENC = 1024
TEXT = 40
VALID = 145
PAIR = 2 * HEAD_DIM
PAIRS = HEADS // 2
SCALE = HEAD_DIM ** (-0.5)
OUTSIDE = -1e30
bf16, f32 = jnp.bfloat16, jnp.float32


def dot(a, b):
    return jnp.dot(a, b, preferred_element_type=f32)


def dot_nt(a, b):
    return lax.dot_general(a, b, (((1,), (1,)), ((), ())), preferred_element_type=f32)


def dot_tn(a, b):
    return lax.dot_general(a, b, (((0,), (0,)), ((), ())), preferred_element_type=f32)


def tiles(total, step, body):
    def run(k, carry):
        body(pl.ds(pl.multiple_of(k * step, step), step))
        return carry

    lax.fori_loop(0, total // step, run, 0)


def norm_forward(values):
    center = values - jnp.mean(values, axis=-1, keepdims=True)
    inverse = lax.rsqrt(jnp.mean(center * center, axis=-1, keepdims=True) + 1e-12)
    return center * inverse, inverse


def norm_backward(grad_out, normed, inverse, gain):
    grad_gain = jnp.sum(grad_out * normed, axis=0, keepdims=True)
    grad_shift = jnp.sum(grad_out, axis=0, keepdims=True)
    scaled = grad_out * gain
    grad_values = inverse * (
        scaled
        - jnp.mean(scaled, axis=-1, keepdims=True)
        - normed * jnp.mean(scaled * normed, axis=-1, keepdims=True)
    )
    return grad_values, grad_gain, grad_shift


def low_half():
    return lax.broadcasted_iota(jnp.int32, (TEXT, PAIR), 1) < HEAD_DIM


def expand(rows):
    low = low_half()
    return jnp.concatenate(
        [jnp.where(low, rows, 0.0), jnp.where(low, 0.0, rows)], axis=0
    ).astype(bf16)


def fold(rows):
    return jnp.where(low_half(), rows[:TEXT], rows[TEXT:])


def softmax(scores):
    top = jnp.max(scores, axis=-1, keepdims=True)
    powers = jnp.exp(scores - top)
    return powers / jnp.sum(powers, axis=-1, keepdims=True)


def pair_cols(j, start=0):
    return slice(start + PAIR * j, start + PAIR * (j + 1))


def pair_rows(j):
    return slice(2 * TEXT * j, 2 * TEXT * (j + 1))


def attend_forward(query, keys, values, bias, probs, item, context, rows):
    js = range(PAIRS)
    scores = [dot_nt(expand(query(j)), keys(j)) * SCALE + bias for j in js]
    weights = [softmax(s) for s in scores]
    for j in js:
        probs[item, pair_rows(j), :] = weights[j]
    parts = [dot(weights[j].astype(bf16), values(j)) for j in js]
    for j in js:
        context[rows, pair_cols(j)] = fold(parts[j])


def attend_backward(query, keys, values, probs, item, grad_context, put_q, put_k, put_v):
    js = range(PAIRS)
    outer = [expand(grad_context(j)) for j in js]
    grads = [dot_nt(outer[j], values(j)) for j in js]
    inner = []
    for j in js:
        weights = probs[item, pair_rows(j), :]
        delta = jnp.sum(weights * grads[j], axis=-1, keepdims=True)
        inner.append((weights * (grads[j] - delta)).astype(bf16))
    for j in js:
        put_v(j, dot_tn(probs[item, pair_rows(j), :].astype(bf16), outer[j]))
    for j in js:
        put_q(j, fold(dot(inner[j], keys(j))) * SCALE)
    for j in js:
        put_k(j, dot_tn(inner[j], expand(query(j))) * SCALE)


def self_forward(lengths, text, w_qkv, w_out, norms, mixed, probs, ctx, normed, inverse, mix, context):
    def project(cols):
        got = dot(text[...], w_qkv[:, cols]).astype(bf16)
        mixed[:, cols] = got
        mix[:, cols] = got.astype(f32)

    tiles(3 * D, 256, project)
    position = lax.broadcasted_iota(jnp.int32, (1, TEXT), 1)

    def one(item, carry):
        rows = pl.ds(pl.multiple_of(item * TEXT, 8), TEXT)
        bias = jnp.where(position < lengths[item], 0.0, -10000.0).astype(f32)
        attend_forward(
            lambda j: mix[rows, pair_cols(j)],
            lambda j: mix[rows, pair_cols(j, D)].astype(bf16),
            lambda j: mix[rows, pair_cols(j, 2 * D)].astype(bf16),
            bias, probs, item, context, rows,
        )
        return carry

    lax.fori_loop(0, probs.shape[0], one, 0)
    ctx[...] = context[...].astype(bf16)
    pre = text[...].astype(f32) + dot(ctx[...], w_out[...])
    n, r = norm_forward(pre)
    normed[...] = n
    inverse[...] = r


def self_backward(text, mixed, probs, ctx, normed, inverse, grad_after, w_qkv, w_out, norms,
                  g_qkv, g_out, text_grad, g_norm, mix, grad_ctx, grad_mix, low_mix):
    grad_pre, grad_gain, grad_shift = norm_backward(grad_after[...], normed[...], inverse[...], norms[0:1, :])
    g_norm[0:1, :] = grad_gain
    g_norm[1:2, :] = grad_shift
    low = grad_pre.astype(bf16)
    g_out[...] = dot_tn(ctx[...], low).astype(bf16)
    grad_ctx[...] = dot_nt(low, w_out[...]).astype(bf16).astype(f32)
    text_grad[...] = grad_pre
    mix[...] = mixed[...].astype(f32)

    def one(item, carry):
        rows = pl.ds(pl.multiple_of(item * TEXT, 8), TEXT)

        def put(start):
            def store(j, value):
                grad_mix[rows, pair_cols(j, start)] = value
            return store

        attend_backward(
            lambda j: mix[rows, pair_cols(j)],
            lambda j: mix[rows, pair_cols(j, D)].astype(bf16),
            lambda j: mix[rows, pair_cols(j, 2 * D)].astype(bf16),
            probs, item, lambda j: grad_ctx[rows, pair_cols(j)],
            put(0), put(D), put(2 * D),
        )
        return carry

    lax.fori_loop(0, probs.shape[0], one, 0)
    low_mix[...] = grad_mix[...].astype(bf16)

    def weights(cols):
        g_qkv[:, cols] = dot_tn(text[...], low_mix[:, cols]).astype(bf16)
        text_grad[...] += dot_nt(low_mix[:, cols], w_qkv[:, cols])

    tiles(3 * D, 256, weights)


def cross_forward(patches, bias, w_kv, w_q, w_out, norms, normed_one,
                  image, memory, query, probs, ctx, normed, inverse, context, wide):
    chunks, items, local, _ = patches.shape
    slots = bias.shape[1]
    step = slots // chunks
    image[...] = jnp.zeros_like(image)

    def lay(item, carry):
        for c in range(chunks):
            start = pl.multiple_of(item * slots + c * step, 16)
            image[pl.ds(start, local), :] = patches[c, item]
        return carry

    lax.fori_loop(0, items, lay, 0)

    def project(cols):
        memory[:, cols] = dot(image[...], w_kv[:, cols]).astype(bf16)

    tiles(2 * D, 256, project)
    after = normed_one[...] * norms[0:1, :] + norms[1:2, :]
    low = dot(after.astype(bf16), w_q[...]).astype(bf16)
    query[...] = low
    wide[...] = low.astype(f32)

    def one(item, carry):
        rows = pl.ds(pl.multiple_of(item * TEXT, 8), TEXT)
        slot = pl.ds(pl.multiple_of(item * slots, 16), slots)
        attend_forward(
            lambda j: wide[rows, pair_cols(j)],
            lambda j: memory[slot, pair_cols(j)],
            lambda j: memory[slot, pair_cols(j, D)],
            bias[pl.ds(item, 1), :], probs, item, context, rows,
        )
        return carry

    lax.fori_loop(0, items, one, 0)
    ctx[...] = context[...].astype(bf16)
    pre = after + dot(ctx[...], w_out[...])
    n, r = norm_forward(pre)
    normed[...] = n
    inverse[...] = r


def cross_backward(image, memory, query, probs, ctx, normed, inverse, normed_one, grad_after,
                   w_kv, w_q, w_out, norms,
                   g_kv, g_q, g_out, patch_grad, grad_self, g_norm, wide, grad_ctx, grad_q, grad_mem):
    chunks, items, local, _ = patch_grad.shape
    slots = image.shape[0] // items
    step = slots // chunks
    grad_pre, grad_gain, grad_shift = norm_backward(grad_after[...], normed[...], inverse[...], norms[2:3, :])
    g_norm[0:1, :] = grad_gain
    g_norm[1:2, :] = grad_shift
    low = grad_pre.astype(bf16)
    g_out[...] = dot_tn(ctx[...], low).astype(bf16)
    grad_ctx[...] = dot_nt(low, w_out[...]).astype(bf16).astype(f32)
    wide[...] = query[...].astype(f32)

    def one(item, carry):
        rows = pl.ds(pl.multiple_of(item * TEXT, 8), TEXT)
        slot = pl.ds(pl.multiple_of(item * slots, 16), slots)

        def put_q(j, value):
            grad_q[rows, pair_cols(j)] = value

        def put(start):
            def store(j, value):
                grad_mem[slot, pair_cols(j, start)] = value.astype(bf16)
            return store

        attend_backward(
            lambda j: wide[rows, pair_cols(j)],
            lambda j: memory[slot, pair_cols(j)],
            lambda j: memory[slot, pair_cols(j, D)],
            probs, item, lambda j: grad_ctx[rows, pair_cols(j)],
            put_q, put(0), put(D),
        )
        return carry

    lax.fori_loop(0, items, one, 0)
    low_q = grad_q[...].astype(bf16)
    after = (normed_one[...] * norms[0:1, :] + norms[1:2, :]).astype(bf16)
    g_q[...] = dot_tn(after, low_q).astype(bf16)
    grad_self[...] = grad_pre + dot_nt(low_q, w_q[...])

    def weights(cols):
        g_kv[:, cols] = dot_tn(image[...], grad_mem[:, cols]).astype(bf16)

    tiles(2 * D, 256, weights)

    def back(item, carry):
        slot = pl.ds(pl.multiple_of(item * slots, 16), slots)
        got = dot_nt(grad_mem[slot, :], w_kv[...])
        for c in range(chunks):
            patch_grad[c, item] = got[c * step : c * step + local].astype(bf16)
        return carry

    lax.fori_loop(0, items, back, 0)


def feed_forward(normed_two, cotangent, w_inner, w_outer, norms,
                 block_output, g_inner, g_outer, grad_after, g_norm, low_in, hidden, slope, total, grad_low, grad_hid):
    after = normed_two[...] * norms[2:3, :] + norms[3:4, :]
    low_in[...] = after.astype(bf16)
    total[...] = after

    def up(cols):
        pre = dot(low_in[...], w_inner[:, cols])
        bell = 0.5 * (1.0 + lax.erf(pre * (0.5 ** 0.5)))
        low = (pre * bell).astype(bf16)
        hidden[:, cols] = low
        slope[:, cols] = bell + pre * jnp.exp(-0.5 * pre * pre) * 0.3989422804014327
        total[...] += dot(low, w_outer[cols, :])

    ff = w_inner.shape[1]
    tiles(ff, 256, up)
    n, r = norm_forward(total[...])
    gain = norms[4:5, :]
    block_output[...] = (n * gain + norms[5:6, :]).astype(bf16)
    grad_pre, grad_gain, grad_shift = norm_backward(cotangent[...].astype(f32), n, r, gain)
    g_norm[0:1, :] = grad_gain
    g_norm[1:2, :] = grad_shift
    grad_after[...] = grad_pre
    grad_low[...] = grad_pre.astype(bf16)

    def down(cols):
        low = (dot_nt(grad_low[...], w_outer[cols, :]) * slope[:, cols]).astype(bf16)
        g_inner[:, cols] = dot_tn(low_in[...], low).astype(bf16)
        g_outer[cols, :] = dot_tn(hidden[:, cols], grad_low[...]).astype(bf16)
        grad_after[...] += dot_nt(low, w_inner[:, cols])

    tiles(ff, 256, down)


VM = pl.BlockSpec(memory_space=pltpu.VMEM)


def call(body, args, outs, scratch, name, smem=0, limit=60 << 20):
    return pl.pallas_call(
        body,
        out_shape=[jax.ShapeDtypeStruct(s, k) for s, k in outs],
        in_specs=[pl.BlockSpec(memory_space=pltpu.SMEM)] * smem + [VM] * (len(args) - smem),
        out_specs=[VM] * len(outs),
        scratch_shapes=[pltpu.VMEM(s, k) for s, k in scratch],
        compiler_params=pltpu.CompilerParams(vmem_limit_bytes=limit),
        name=name,
    )(*args)


def local_step(text, cotangent, pbuf, pbias, lengths, ws, norms):
    w_qkv, w_out, w_cq, w_kv, w_co, w_in, w_outer = ws
    rows = text.shape[0]
    items = rows // TEXT
    slots = pbias.shape[1]
    pairs = HEADS * TEXT
    row = ((rows, D), f32)
    rowl = ((rows, D), bf16)
    one = ((rows, 1), f32)
    gn = ((2, D), f32)
    mixed, probs, ctx, n1, r1 = call(
        self_forward, (lengths, text, w_qkv, w_out, norms),
        [((rows, 3 * D), bf16), ((items, pairs, TEXT), f32), rowl, row, one],
        [((rows, 3 * D), f32), row], "self_forward", smem=1)
    image, memory, query, cprobs, cctx, n2, r2 = call(
        cross_forward, (pbuf, pbias, w_kv, w_cq, w_co, norms, n1),
        [((items * slots, ENC), bf16), ((items * slots, 2 * D), bf16), rowl, ((items, pairs, slots), f32), rowl, row, one],
        [row, row], "cross_forward")
    ff = w_in.shape[1]
    block_output, g_in, g_outer, grad_after, gn3 = call(
        feed_forward, (n2, cotangent, w_in, w_outer, norms),
        [rowl, ((D, ff), bf16), ((ff, D), bf16), row, gn],
        [rowl, ((rows, ff), bf16), ((rows, ff), f32), row, rowl, rowl], "feed_forward")
    g_kv, g_cq, g_co, patch_grad, grad_self, gn2 = call(
        cross_backward, (image, memory, query, cprobs, cctx, n2, r2, n1, grad_after, w_kv, w_cq, w_co, norms),
        [((ENC, 2 * D), bf16), ((D, D), bf16), ((D, D), bf16), (pbuf.shape, bf16), row, gn],
        [row, row, row, ((items * slots, 2 * D), bf16)], "cross_backward")
    g_qkv, g_out, text_grad, gn1 = call(
        self_backward, (text, mixed, probs, ctx, n1, r1, grad_self, w_qkv, w_out, norms),
        [((D, 3 * D), bf16), ((D, D), bf16), row, gn],
        [((rows, 3 * D), f32), row, ((rows, 3 * D), f32), ((rows, 3 * D), bf16)], "self_backward")
    g_norms = jnp.concatenate([gn1, gn2, gn3], axis=0)
    return block_output, text_grad, patch_grad, (g_qkv, g_out, g_cq, g_kv, g_co, g_in, g_outer), g_norms


MESH = pl.DeviceIdType.MESH
Z, X, Y, C = 4, 2, 2, 2
PLANE_FIRST = (0, 3)


class Place:
    def __init__(self):
        item, self.me = lax.axis_index("items"), lax.axis_index("patch")
        self.z, self.x, self.y, self.c = item // X, item % X, self.me // C, self.me % C
        z, x, y, c = self.z, self.x, self.y, self.c
        self.left = (item - X, self.me)
        self.right = (item + X, self.me)
        self.xdev = (z * X + (1 - x), self.me)
        self.ypeer, self.cpeer, self.dpeer = (1 - y) * C + c, y * C + (1 - c), (1 - y) * C + (1 - c)
        self.ydev, self.cdev, self.ddev = (item, self.ypeer), (item, self.cpeer), (item, self.dpeer)

    def at(self, zz, xx, yy, cc):
        return ((zz * X + xx) * Y + yy) * C + cc

    def greet(self, barrier):
        for dev in (self.xdev, self.ydev, self.cdev, self.ddev):
            pl.semaphore_signal(barrier, inc=1, device_id=dev, device_id_type=MESH)

        @pl.when(self.z > 0)
        def _():
            pl.semaphore_signal(barrier, inc=1, device_id=self.left, device_id_type=MESH)

        @pl.when(self.z < Z - 1)
        def _():
            pl.semaphore_signal(barrier, inc=1, device_id=self.right, device_id_type=MESH)

    def met(self, barrier):
        pl.semaphore_wait(barrier, 4 + (self.z > 0).astype(jnp.int32) + (self.z < Z - 1).astype(jnp.int32))

    def both(self, d, step):
        if d == 0:
            step(self.z, None)
            return

        @pl.when(self.z >= d)
        def _():
            step(self.z - d, True)

        @pl.when(self.z + d < Z)
        def _():
            step(self.z + d, False)


def gather_kernel(nw, plane_first, nx, *refs):
    shards = refs[:nw]
    sources = refs[nw : nw + nx]
    outs = refs[nw + nx : 2 * nw + nx]
    swaps = refs[2 * nw + nx : 2 * nw + 2 * nx]
    low = refs[2 * nw + 2 * nx : 3 * nw + 2 * nx]
    recv, sendx, sendy, sendc, sendl, sendr, local, psend, precv, plocal = refs[3 * nw + 2 * nx :]
    p = Place()
    z, x, y, c, me = p.z, p.x, p.y, p.c, p.me
    barrier = pltpu.get_barrier_semaphore()
    p.greet(barrier)
    for w in range(nw):
        low[w][...] = shards[w][...].astype(low[w].dtype)
    p.met(barrier)

    def send(w, block, dev, sem, own=False):
        pltpu.make_async_remote_copy(
            src_ref=low[w] if own else outs[w].at[block],
            dst_ref=outs[w].at[block],
            send_sem=sem.at[w],
            recv_sem=recv.at[w, block],
            device_id=dev,
            device_id_type=MESH,
        ).start()

    def arrived(w, block):
        pltpu.make_async_remote_copy(
            src_ref=outs[w].at[block],
            dst_ref=outs[w].at[block],
            send_sem=sendx.at[w],
            recv_sem=recv.at[w, block],
            device_id=p.xdev,
            device_id_type=MESH,
        ).wait_recv()

    every = range(nw)
    line = [w for w in every if w not in plane_first]
    plane = [w for w in every if w in plane_first]
    mine = p.at(z, x, y, c)

    def to_left(w, block, own=False):
        @pl.when(z > 0)
        def _():
            send(w, block, p.left, sendl, own)

    def to_right(w, block, own=False):
        @pl.when(z < Z - 1)
        def _():
            send(w, block, p.right, sendr, own)

    def to_x(w, block, own=False):
        send(w, block, p.xdev, sendx, own)

    def to_y(w, block, own=False):
        send(w, block, p.ydev, sendy, own)

    def to_core(w, block, own=False):
        send(w, block, p.cdev, sendc, own)

    for w in plane:
        to_x(w, mine, True)
        to_y(w, mine, True)
    for w in line:
        to_left(w, mine, True)
        to_right(w, mine, True)
        to_y(w, mine, True)
        to_x(w, mine, True)
    for w in plane:
        to_left(w, mine, True)
        to_right(w, mine, True)
    for w in every:
        to_core(w, mine, True)
        pltpu.make_async_copy(low[w], outs[w].at[mine], local.at[w]).start()
    for s in range(nx):
        here = swaps[s].shape[1]
        for k, (dev, peer) in enumerate(((p.ydev, p.ypeer), (p.cdev, p.cpeer), (p.ddev, p.dpeer))):
            pltpu.make_async_remote_copy(
                src_ref=sources[s].at[pl.ds(peer * here, here)],
                dst_ref=swaps[s].at[me],
                send_sem=psend.at[s, k],
                recv_sem=precv.at[s, k],
                device_id=dev,
                device_id_type=MESH,
            ).start()
        pltpu.make_async_copy(sources[s].at[pl.ds(me * here, here)], swaps[s].at[me], plocal.at[s]).start()

    def plane_x():
        for w in plane:
            block = p.at(z, 1 - x, y, c)
            arrived(w, block)
            to_y(w, block)
            to_left(w, block)
            to_right(w, block)
            to_core(w, block)

    def plane_y(xx):
        for w in plane:
            block = p.at(z, xx, 1 - y, c)
            arrived(w, block)
            to_left(w, block)
            to_right(w, block)
            to_core(w, block)

    def plane_z(zz, from_left):
        for xx, yy in ((x, y), (1 - x, y), (x, 1 - y), (1 - x, 1 - y)):
            for w in plane:
                block = p.at(zz, xx, yy, c)
                arrived(w, block)
                (to_right if from_left else to_left)(w, block)
                to_core(w, block)

    def line_z(zz, from_left):
        block = p.at(zz, x, y, c)
        for w in line:
            arrived(w, block)
            (to_right if from_left else to_left)(w, block)
            to_y(w, block)
            to_x(w, block)
            to_core(w, block)

    def line_y(zz, _):
        block = p.at(zz, x, 1 - y, c)
        for w in line:
            arrived(w, block)
            to_x(w, block)
            to_core(w, block)

    def line_x(zz, _):
        for yy in (y, 1 - y):
            block = p.at(zz, 1 - x, yy, c)
            for w in line:
                arrived(w, block)
                to_core(w, block)

    plane_x()
    p.both(1, line_z)
    plane_y(x)
    plane_y(1 - x)
    p.both(0, line_y)
    p.both(1, plane_z)
    p.both(2, line_z)
    p.both(1, line_y)
    p.both(0, line_x)
    p.both(2, plane_z)
    p.both(3, line_z)
    p.both(2, line_y)
    p.both(1, line_x)
    p.both(3, plane_z)
    p.both(3, line_y)
    p.both(2, line_x)
    p.both(3, line_x)
    for zz in range(Z):
        for xx in range(X):
            for yy in range(Y):
                for w in every:
                    arrived(w, p.at(zz, xx, yy, 1 - c))
    for w in every:
        pltpu.make_async_copy(low[w], outs[w].at[mine], local.at[w]).wait()

        def sent(count, sem):
            span = outs[w].at[pl.ds(0, count)]
            pltpu.make_async_copy(span, span, sem.at[w]).wait()

        wide = X * Y if w in plane else 1
        sent(1 if w in plane else Z * Y, sendx)
        sent(X if w in plane else Z, sendy)
        sent(Z * X * Y, sendc)
        for k in range(Z):
            @pl.when(z == k)
            def _():
                if k > 0:
                    sent(wide * (Z - k), sendl)
                if k < Z - 1:
                    sent(wide * (k + 1), sendr)
    for s in range(nx):
        here = swaps[s].shape[1]
        for k, dev in enumerate((p.ydev, p.cdev, p.ddev)):
            pltpu.make_async_remote_copy(
                src_ref=sources[s].at[pl.ds(0, here)],
                dst_ref=swaps[s].at[0],
                send_sem=psend.at[s, k],
                recv_sem=precv.at[s, k],
                device_id=dev,
                device_id_type=MESH,
            ).wait()
        pltpu.make_async_copy(sources[s].at[pl.ds(me * here, here)], swaps[s].at[me], plocal.at[s]).wait()


def gather_all(shards, kinds, swaps, plane_first=PLANE_FIRST, collective=0):
    nw, nx = len(shards), len(swaps)
    n = Z * X * Y * C
    anyspec = pl.BlockSpec(memory_space=pl.ANY)
    vm = pl.BlockSpec(memory_space=pltpu.VMEM)
    dma = pltpu.SemaphoreType.DMA
    out = pl.pallas_call(
        functools.partial(gather_kernel, nw, plane_first, nx),
        out_shape=[jax.ShapeDtypeStruct((n,) + s.shape, k) for s, k in zip(shards, kinds)]
        + [jax.ShapeDtypeStruct((Y * C, s.shape[0] // (Y * C)) + s.shape[1:], s.dtype) for s in swaps],
        in_specs=[vm] * nw + [anyspec] * nx,
        out_specs=[anyspec] * (nw + nx),
        scratch_shapes=[pltpu.VMEM(s.shape, k) for s, k in zip(shards, kinds)]
        + [dma((nw, n))] + [dma((nw,))] * 6 + [dma((nx, 3)), dma((nx, 3)), dma((nx,))],
        compiler_params=pltpu.CompilerParams(collective_id=collective, has_side_effects=True),
        name="gather",
    )(*shards, *swaps)
    return [o.reshape(n * o.shape[1], o.shape[2]) for o in out[:nw]], list(out[nw:])


step_rates = (0.05, 0.15, 0.05, 0.05, 0.3, 0.05, 0.05, 0.5)
step_decays = (0.01, 0.01, 0.01, 0.01, 0.01, 0.01, 0.01, 0.0)
BOTH = ("items", "patch")
STEP = 48


def adamw_step(master, gradient, first_moment, second_moment, rate, decay):
    first_new = 0.9 * first_moment + 0.1 * gradient
    second_new = 0.999 * second_moment + 0.001 * gradient * gradient
    step_size = first_new / (1.0 - 0.9**10) / (jnp.sqrt(second_new / (1.0 - 0.999**10)) + 1e-08)
    return (master - rate * (step_size + decay * master), first_new, second_new)


def pad_to(array, shape, value=0.0):
    return jnp.pad(array, [(0, n - k) for n, k in zip(shape, array.shape)], constant_values=value)


def on_device(direct, text, cotangent, patches, text_lengths, patch_mask, *state):
    masters, firsts, seconds = state[:8], state[8:16], state[16:]
    group, local = patch_mask.shape
    chunks = lax.axis_size("patch")
    items = group // chunks
    index = lax.axis_index("patch") * local + jnp.arange(local, dtype=jnp.int32)
    valid = (patch_mask > 0) & (index[None, :] < VALID)
    bias = pad_to(jnp.where(valid, 0.0, -10000.0).astype(f32), (group, 128), OUTSIDE)
    norms_low = masters[7].astype(bf16).astype(f32)
    if direct:
        wide = pad_to(norms_low, (8, 128))
        weights, (image, bias) = gather_all(
            list(masters[:7]) + [wide], [bf16] * 7 + [f32], [patches, bias]
        )
        norms = weights.pop().reshape(-1, 8, 128)[:, :6, : norms_low.shape[1]]
        norms = norms.transpose(1, 0, 2).reshape(6, D)
    else:
        weights = [lax.all_gather(m.astype(bf16), BOTH, axis=0, tiled=True) for m in masters[:7]]
        norms = lax.all_gather(norms_low, BOTH, axis=1, tiled=True)
        image = lax.all_to_all(patches.reshape(chunks, items, local, ENC), "patch", 0, 0)
        bias = lax.all_to_all(bias.reshape(chunks, items, 128), "patch", 0, 0)
    bias = bias[:, :, :STEP].transpose(1, 0, 2).reshape(items, chunks * STEP)
    block_output, text_grad, image_grad, grads, grad_norms = local_step(
        text, cotangent, image, bias, text_lengths, weights, norms
    )
    image_grad = lax.all_to_all(image_grad, "patch", 0, 0)
    patch_grad = image_grad.astype(f32).reshape(patches.shape)
    joined = lax.psum_scatter(
        jnp.concatenate([grads[k] for k in (0, 1, 2, 4, 5)], axis=1), BOTH, scatter_dimension=0, tiled=True
    )
    reduced = {}
    start = 0
    for k in (0, 1, 2, 4, 5):
        reduced[k] = joined[:, start : start + grads[k].shape[1]].astype(f32)
        start += grads[k].shape[1]
    for k in (3, 6):
        reduced[k] = lax.psum_scatter(grads[k], BOTH, scatter_dimension=0, tiled=True).astype(f32)
    reduced[7] = lax.psum_scatter(grad_norms, BOTH, scatter_dimension=1, tiled=True)
    updated = [
        adamw_step(masters[k], reduced[k], firsts[k], seconds[k], step_rates[k], step_decays[k])
        for k in range(8)
    ]
    return (block_output, text_grad, patch_grad, *[u[part] for part in range(3) for u in updated])


def solution(mesh):
    rows, cols = P(BOTH, None), P(None, BOTH)
    state = (*[rows] * 7, cols)
    direct = dict(mesh.shape) == {"items": Z * X, "patch": Y * C}
    return jax.shard_map(
        functools.partial(on_device, direct),
        mesh=mesh,
        in_specs=(rows, rows, P("items", "patch", None), P(BOTH), P("items", "patch"), *state * 3),
        out_specs=(rows, rows, P("items", "patch", None), *state * 3),
        check_vma=False,
    )
```

```python
import functools

import jax
import jax.numpy as jnp
from jax import lax
from jax.experimental import pallas as pl
from jax.experimental.pallas import tpu as pltpu
from jax.sharding import PartitionSpec as P

D = 768
HEADS = 12
HEAD_DIM = 64
ENC = 1024
TEXT = 40
VALID = 145
PAIR = 2 * HEAD_DIM
PAIRS = HEADS // 2
SCALE = HEAD_DIM ** (-0.5)
OUTSIDE = -1e30
bf16, f32 = jnp.bfloat16, jnp.float32


def dot(a, b):
    return jnp.dot(a, b, preferred_element_type=f32)


def dot_nt(a, b):
    return lax.dot_general(a, b, (((1,), (1,)), ((), ())), preferred_element_type=f32)


def dot_tn(a, b):
    return lax.dot_general(a, b, (((0,), (0,)), ((), ())), preferred_element_type=f32)


def tiles(total, step, body):
    def run(k, carry):
        body(pl.ds(pl.multiple_of(k * step, step), step))
        return carry

    lax.fori_loop(0, total // step, run, 0)


def norm_forward(values):
    center = values - jnp.mean(values, axis=-1, keepdims=True)
    inverse = lax.rsqrt(jnp.mean(center * center, axis=-1, keepdims=True) + 1e-12)
    return center * inverse, inverse


def norm_backward(grad_out, normed, inverse, gain):
    grad_gain = jnp.sum(grad_out * normed, axis=0, keepdims=True)
    grad_shift = jnp.sum(grad_out, axis=0, keepdims=True)
    scaled = grad_out * gain
    grad_values = inverse * (
        scaled
        - jnp.mean(scaled, axis=-1, keepdims=True)
        - normed * jnp.mean(scaled * normed, axis=-1, keepdims=True)
    )
    return grad_values, grad_gain, grad_shift


def low_half():
    return lax.broadcasted_iota(jnp.int32, (TEXT, PAIR), 1) < HEAD_DIM


def expand(rows):
    low = low_half()
    return jnp.concatenate(
        [jnp.where(low, rows, 0.0), jnp.where(low, 0.0, rows)], axis=0
    ).astype(bf16)


def fold(rows):
    return jnp.where(low_half(), rows[:TEXT], rows[TEXT:])


def softmax(scores):
    top = jnp.max(scores, axis=-1, keepdims=True)
    powers = jnp.exp(scores - top)
    return powers / jnp.sum(powers, axis=-1, keepdims=True)


def pair_cols(j, start=0):
    return slice(start + PAIR * j, start + PAIR * (j + 1))


def pair_rows(j):
    return slice(2 * TEXT * j, 2 * TEXT * (j + 1))


def attend_forward(query, keys, values, bias, probs, item, context, rows):
    js = range(PAIRS)
    scores = [dot_nt(expand(query(j)), keys(j)) * SCALE + bias for j in js]
    weights = [softmax(s) for s in scores]
    for j in js:
        probs[item, pair_rows(j), :] = weights[j]
    parts = [dot(weights[j].astype(bf16), values(j)) for j in js]
    for j in js:
        context[rows, pair_cols(j)] = fold(parts[j])


def attend_backward(query, keys, values, probs, item, grad_context, put_q, put_k, put_v):
    js = range(PAIRS)
    outer = [expand(grad_context(j)) for j in js]
    grads = [dot_nt(outer[j], values(j)) for j in js]
    inner = []
    for j in js:
        weights = probs[item, pair_rows(j), :]
        delta = jnp.sum(weights * grads[j], axis=-1, keepdims=True)
        inner.append((weights * (grads[j] - delta)).astype(bf16))
    for j in js:
        put_v(j, dot_tn(probs[item, pair_rows(j), :].astype(bf16), outer[j]))
    for j in js:
        put_q(j, fold(dot(inner[j], keys(j))) * SCALE)
    for j in js:
        put_k(j, dot_tn(inner[j], expand(query(j))) * SCALE)


def self_forward(lengths, text, w_qkv, w_out, blocks, mixed, probs, ctx, normed, inverse, norms, mix, context):
    spread(blocks, norms)

    def project(cols):
        got = dot(text[...], w_qkv[:, cols]).astype(bf16)
        mixed[:, cols] = got
        mix[:, cols] = got.astype(f32)

    tiles(3 * D, 256, project)
    position = lax.broadcasted_iota(jnp.int32, (1, TEXT), 1)

    def one(item, carry):
        rows = pl.ds(pl.multiple_of(item * TEXT, 8), TEXT)
        bias = jnp.where(position < lengths[item], 0.0, -10000.0).astype(f32)
        attend_forward(
            lambda j: mix[rows, pair_cols(j)],
            lambda j: mix[rows, pair_cols(j, D)].astype(bf16),
            lambda j: mix[rows, pair_cols(j, 2 * D)].astype(bf16),
            bias, probs, item, context, rows,
        )
        return carry

    lax.fori_loop(0, probs.shape[0], one, 0)
    ctx[...] = context[...].astype(bf16)
    pre = text[...].astype(f32) + dot(ctx[...], w_out[...])
    n, r = norm_forward(pre)
    normed[...] = n
    inverse[...] = r


def self_backward(text, mixed, probs, ctx, normed, inverse, grad_after, w_qkv, w_out, norms, g_second, g_third,
                  g_qkv, g_out, text_grad, g_blocks, mix, grad_ctx, grad_mix, low_mix):
    grad_pre, grad_gain, grad_shift = norm_backward(grad_after[...], normed[...], inverse[...], norms[0:1, :])
    rows = jnp.concatenate([grad_gain, grad_shift, g_second[...], g_third[...], jnp.zeros((2, D), f32)], axis=0)
    width = D // g_blocks.shape[0]
    for b in range(g_blocks.shape[0]):
        g_blocks[b, :, :width] = rows[:, width * b : width * (b + 1)]
        g_blocks[b, :, width:] = jnp.zeros((8, g_blocks.shape[2] - width), f32)
    low = grad_pre.astype(bf16)
    g_out[...] = dot_tn(ctx[...], low).astype(bf16)
    grad_ctx[...] = dot_nt(low, w_out[...]).astype(bf16).astype(f32)
    text_grad[...] = grad_pre
    mix[...] = mixed[...].astype(f32)

    def one(item, carry):
        rows = pl.ds(pl.multiple_of(item * TEXT, 8), TEXT)

        def put(start):
            def store(j, value):
                grad_mix[rows, pair_cols(j, start)] = value
            return store

        attend_backward(
            lambda j: mix[rows, pair_cols(j)],
            lambda j: mix[rows, pair_cols(j, D)].astype(bf16),
            lambda j: mix[rows, pair_cols(j, 2 * D)].astype(bf16),
            probs, item, lambda j: grad_ctx[rows, pair_cols(j)],
            put(0), put(D), put(2 * D),
        )
        return carry

    lax.fori_loop(0, probs.shape[0], one, 0)
    low_mix[...] = grad_mix[...].astype(bf16)

    def weights(cols):
        g_qkv[:, cols] = dot_tn(text[...], low_mix[:, cols]).astype(bf16)
        text_grad[...] += dot_nt(low_mix[:, cols], w_qkv[:, cols])

    tiles(3 * D, 256, weights)


def spread(blocks, norms):
    width = D // blocks.shape[0]
    for b in range(blocks.shape[0]):
        norms[:, width * b : width * (b + 1)] = blocks[b, :, :width]


def cross_forward(image, masks, w_kv, w_q, w_out, norms, normed_one,
                  memory, query, probs, ctx, normed, inverse, bias, context, wide, flat):
    items = masks.shape[1]
    slots = bias.shape[1]
    local = slots // masks.shape[0]
    for c in range(masks.shape[0]):
        bias[:, local * c : local * (c + 1)] = masks[c, :, :local]

    def project(k, carry):
        got = dot(image[...], w_kv[:, pl.ds(pl.multiple_of(2 * PAIR * k, 2 * PAIR), 2 * PAIR)]).astype(bf16).astype(f32)
        flat[2 * k] = got[:, :PAIR]
        flat[2 * k + 1] = got[:, PAIR:]
        return carry

    lax.fori_loop(0, PAIRS, project, 0)
    after = normed_one[...] * norms[0:1, :] + norms[1:2, :]
    low = dot(after.astype(bf16), w_q[...]).astype(bf16)
    query[...] = low
    wide[...] = low.astype(f32)

    def one(item, carry):
        rows = pl.ds(pl.multiple_of(item * TEXT, 8), TEXT)
        every = pl.ds(item, slots, stride=items)
        for j in range(2 * PAIRS):
            memory[item, :, pair_cols(j)] = flat[j, every, :].astype(bf16)
        attend_forward(
            lambda j: wide[rows, pair_cols(j)],
            lambda j: memory[item, :, pair_cols(j)],
            lambda j: memory[item, :, pair_cols(j, D)],
            bias[pl.ds(item, 1), :], probs, item, context, rows,
        )
        return carry

    lax.fori_loop(0, items, one, 0)
    ctx[...] = context[...].astype(bf16)
    pre = after + dot(ctx[...], w_out[...])
    n, r = norm_forward(pre)
    normed[...] = n
    inverse[...] = r


def cross_backward(image, memory, query, probs, ctx, normed, inverse, normed_one, grad_after,
                   w_kv, w_q, w_out, norms,
                   g_kv, g_q, g_out, image_grad, grad_self, g_norm, wide, grad_ctx, grad_q, flat, grad_mem):
    items, slots = memory.shape[:2]
    grad_pre, grad_gain, grad_shift = norm_backward(grad_after[...], normed[...], inverse[...], norms[2:3, :])
    g_norm[0:1, :] = grad_gain
    g_norm[1:2, :] = grad_shift
    low = grad_pre.astype(bf16)
    g_out[...] = dot_tn(ctx[...], low).astype(bf16)
    grad_ctx[...] = dot_nt(low, w_out[...]).astype(bf16).astype(f32)
    wide[...] = query[...].astype(f32)

    def one(item, carry):
        rows = pl.ds(pl.multiple_of(item * TEXT, 8), TEXT)
        every = pl.ds(item, slots, stride=items)

        def put_q(j, value):
            grad_q[rows, pair_cols(j)] = value

        def put(start):
            def store(j, value):
                flat[start + j, every, :] = value
            return store

        attend_backward(
            lambda j: wide[rows, pair_cols(j)],
            lambda j: memory[item, :, pair_cols(j)],
            lambda j: memory[item, :, pair_cols(j, D)],
            probs, item, lambda j: grad_ctx[rows, pair_cols(j)],
            put_q, put(0), put(PAIRS),
        )
        return carry

    lax.fori_loop(0, items, one, 0)
    low_q = grad_q[...].astype(bf16)
    after = (normed_one[...] * norms[0:1, :] + norms[1:2, :]).astype(bf16)
    g_q[...] = dot_tn(after, low_q).astype(bf16)
    grad_self[...] = grad_pre + dot_nt(low_q, w_q[...])
    for j in range(2 * PAIRS):
        grad_mem[:, pair_cols(j)] = flat[j].astype(bf16)

    def weights(cols):
        g_kv[:, cols] = dot_tn(image[...], grad_mem[:, cols]).astype(bf16)

    tiles(2 * D, 256, weights)

    def back(cols):
        image_grad[:, cols] = dot_nt(grad_mem[...], w_kv[cols, :]).astype(bf16)

    tiles(ENC, 256, back)


def feed_forward(normed_two, cotangent, w_inner, w_outer, norms,
                 block_output, g_inner, g_outer, grad_after, g_norm, low_in, hidden, slope, total, grad_low, grad_hid):
    after = normed_two[...] * norms[2:3, :] + norms[3:4, :]
    low_in[...] = after.astype(bf16)
    total[...] = after

    def up(cols):
        pre = dot(low_in[...], w_inner[:, cols])
        bell = 0.5 * (1.0 + lax.erf(pre * (0.5 ** 0.5)))
        low = (pre * bell).astype(bf16)
        hidden[:, cols] = low
        slope[:, cols] = bell + pre * jnp.exp(-0.5 * pre * pre) * 0.3989422804014327
        total[...] += dot(low, w_outer[cols, :])

    ff = w_inner.shape[1]
    tiles(ff, 256, up)
    n, r = norm_forward(total[...])
    gain = norms[4:5, :]
    block_output[...] = (n * gain + norms[5:6, :]).astype(bf16)
    grad_pre, grad_gain, grad_shift = norm_backward(cotangent[...].astype(f32), n, r, gain)
    g_norm[0:1, :] = grad_gain
    g_norm[1:2, :] = grad_shift
    grad_after[...] = grad_pre
    grad_low[...] = grad_pre.astype(bf16)

    def down(cols):
        low = (dot_nt(grad_low[...], w_outer[cols, :]) * slope[:, cols]).astype(bf16)
        g_inner[:, cols] = dot_tn(low_in[...], low).astype(bf16)
        g_outer[cols, :] = dot_tn(hidden[:, cols], grad_low[...]).astype(bf16)
        grad_after[...] += dot_nt(low, w_inner[:, cols])

    tiles(ff, 256, down)


VM = pl.BlockSpec(memory_space=pltpu.VMEM)


def call(body, args, outs, scratch, name, smem=0, limit=60 << 20):
    return pl.pallas_call(
        body,
        out_shape=[jax.ShapeDtypeStruct(s, k) for s, k in outs],
        in_specs=[pl.BlockSpec(memory_space=pltpu.SMEM)] * smem + [VM] * (len(args) - smem),
        out_specs=[VM] * len(outs),
        scratch_shapes=[pltpu.VMEM(s, k) for s, k in scratch],
        compiler_params=pltpu.CompilerParams(vmem_limit_bytes=limit),
        name=name,
    )(*args)


def adamw(count, decays, rates, *refs):
    masters, firsts, seconds, grads = (refs[count * i : count * (i + 1)] for i in range(4))
    image_low = refs[4 * count]
    new_m, new_f, new_s = (refs[4 * count + 1 + count * i : 4 * count + 1 + count * (i + 1)] for i in range(3))
    image_grad = refs[7 * count + 1]
    for k in range(count):
        rows, cols = masters[k].shape
        gradient = grads[k][:rows, :cols]
        first = 0.9 * firsts[k][...] + 0.1 * gradient
        second = 0.999 * seconds[k][...] + 0.001 * gradient * gradient
        step = first / (1.0 - 0.9**10) / (jnp.sqrt(second / (1.0 - 0.999**10)) + 1e-08)
        master = masters[k][...]
        new_m[k][...] = master - rates[k] * (step + decays[k] * master)
        new_f[k][...] = first
        new_s[k][...] = second
    image_grad[...] = image_low[...].astype(f32)


def local_step(text, cotangent, image, masks, lengths, ws, blocks):
    w_qkv, w_out, w_cq, w_kv, w_co, w_in, w_outer = ws
    rows = text.shape[0]
    slots, items, _ = image.shape
    image = image.reshape(slots * items, ENC)
    pairs = HEADS * TEXT
    row = ((rows, D), f32)
    rowl = ((rows, D), bf16)
    one = ((rows, 1), f32)
    gn = ((2, D), f32)
    mixed, probs, ctx, n1, r1, norms = call(
        self_forward, (lengths, text, w_qkv, w_out, blocks),
        [((rows, 3 * D), bf16), ((items, pairs, TEXT), f32), rowl, row, one, ((8, D), f32)],
        [((rows, 3 * D), f32), row], "self_forward", smem=1)
    memory, query, cprobs, cctx, n2, r2 = call(
        cross_forward, (image, masks, w_kv, w_cq, w_co, norms, n1),
        [((items, slots, 2 * D), bf16), rowl, ((items, pairs, slots), f32), rowl, row, one],
        [((items, slots), f32), row, row, ((2 * PAIRS, items * slots, PAIR), f32)], "cross_forward")
    ff = w_in.shape[1]
    block_output, g_in, g_outer, grad_after, gn3 = call(
        feed_forward, (n2, cotangent, w_in, w_outer, norms),
        [rowl, ((D, ff), bf16), ((ff, D), bf16), row, gn],
        [rowl, ((rows, ff), bf16), ((rows, ff), f32), row, rowl, rowl], "feed_forward")
    g_kv, g_cq, g_co, image_grad, grad_self, gn2 = call(
        cross_backward, (image, memory, query, cprobs, cctx, n2, r2, n1, grad_after, w_kv, w_cq, w_co, norms),
        [((ENC, 2 * D), bf16), ((D, D), bf16), ((D, D), bf16), (image.shape, bf16), row, gn],
        [row, row, row, ((2 * PAIRS, items * slots, PAIR), f32), ((items * slots, 2 * D), bf16)], "cross_backward")
    g_qkv, g_out, text_grad, g_blocks = call(
        self_backward, (text, mixed, probs, ctx, n1, r1, grad_self, w_qkv, w_out, norms, gn2, gn3),
        [((D, 3 * D), bf16), ((D, D), bf16), row, (blocks.shape, f32)],
        [((rows, 3 * D), f32), row, ((rows, 3 * D), f32), ((rows, 3 * D), bf16)], "self_backward")
    return block_output, text_grad, image_grad, (g_qkv, g_out, g_cq, g_kv, g_co, g_in, g_outer), g_blocks


MESH = pl.DeviceIdType.MESH
Z, X, Y, C = 4, 2, 2, 2
PLANE_FIRST = (0, 3)


class Place:
    def __init__(self):
        item, self.me = lax.axis_index("items"), lax.axis_index("patch")
        self.z, self.x, self.y, self.c = item // X, item % X, self.me // C, self.me % C
        z, x, y, c = self.z, self.x, self.y, self.c
        self.left = (item - X, self.me)
        self.right = (item + X, self.me)
        self.xdev = (z * X + (1 - x), self.me)
        self.ypeer, self.cpeer, self.dpeer = (1 - y) * C + c, y * C + (1 - c), (1 - y) * C + (1 - c)
        self.ydev, self.cdev, self.ddev = (item, self.ypeer), (item, self.cpeer), (item, self.dpeer)

    def at(self, zz, xx, yy, cc):
        return ((zz * X + xx) * Y + yy) * C + cc

    def greet(self, barrier):
        for dev in (self.xdev, self.ydev, self.cdev, self.ddev):
            pl.semaphore_signal(barrier, inc=1, device_id=dev, device_id_type=MESH)

        @pl.when(self.z > 0)
        def _():
            pl.semaphore_signal(barrier, inc=1, device_id=self.left, device_id_type=MESH)

        @pl.when(self.z < Z - 1)
        def _():
            pl.semaphore_signal(barrier, inc=1, device_id=self.right, device_id_type=MESH)

    def met(self, barrier):
        pl.semaphore_wait(barrier, 4 + (self.z > 0).astype(jnp.int32) + (self.z < Z - 1).astype(jnp.int32))

    def both(self, d, step):
        if d == 0:
            step(self.z, None)
            return

        @pl.when(self.z >= d)
        def _():
            step(self.z - d, True)

        @pl.when(self.z + d < Z)
        def _():
            step(self.z + d, False)


def patch_bias(mask, first, valid):
    index = first + lax.broadcasted_iota(jnp.int32, mask.shape, 1)
    return jnp.where((mask > 0) & (index < valid), 0.0, -10000.0).astype(f32)


def gather_kernel(nw, plane_first, valid, *refs):
    shards = refs[:nw]
    image, mask = refs[nw : nw + 2]
    outs = refs[nw + 2 : 2 * nw + 2]
    swaps = refs[2 * nw + 2 : 2 * nw + 4]
    low = refs[2 * nw + 4 : 3 * nw + 4]
    bias = refs[3 * nw + 4]
    recv, sendx, sendy, sendc, sendl, sendr, local, psend, precv, plocal = refs[3 * nw + 5 :]
    p = Place()
    z, x, y, c, me = p.z, p.x, p.y, p.c, p.me
    barrier = pltpu.get_barrier_semaphore()
    p.greet(barrier)
    for w in range(nw - 1):
        low[w][...] = shards[w][...].astype(low[w].dtype)
    low[nw - 1][...] = jnp.zeros(low[nw - 1].shape, f32)
    rows, cols = shards[nw - 1].shape
    low[nw - 1][:rows, :cols] = shards[nw - 1][...].astype(bf16).astype(f32)
    slots = mask.shape[1]
    bias[...] = jnp.zeros(bias.shape, f32)
    bias[:, :slots] = patch_bias(mask[...], me * slots, valid)
    here = mask.shape[0] // (Y * C)
    peers = ((p.ydev, p.ypeer), (p.cdev, p.cpeer), (p.ddev, p.dpeer))

    def part(s, peer):
        rows = pl.ds(pl.multiple_of(peer * here, here), here)
        return bias.at[rows] if s else image.at[:, rows]

    p.met(barrier)

    def send(w, block, dev, sem, own=False):
        pltpu.make_async_remote_copy(
            src_ref=low[w] if own else outs[w].at[block],
            dst_ref=outs[w].at[block],
            send_sem=sem.at[w],
            recv_sem=recv.at[w, block],
            device_id=dev,
            device_id_type=MESH,
        ).start()

    def arrived(w, block):
        pltpu.make_async_remote_copy(
            src_ref=outs[w].at[block],
            dst_ref=outs[w].at[block],
            send_sem=sendx.at[w],
            recv_sem=recv.at[w, block],
            device_id=p.xdev,
            device_id_type=MESH,
        ).wait_recv()

    every = range(nw)
    line = [w for w in every if w not in plane_first]
    plane = [w for w in every if w in plane_first]
    mine = p.at(z, x, y, c)

    def to_left(w, block, own=False):
        @pl.when(z > 0)
        def _():
            send(w, block, p.left, sendl, own)

    def to_right(w, block, own=False):
        @pl.when(z < Z - 1)
        def _():
            send(w, block, p.right, sendr, own)

    def to_x(w, block, own=False):
        send(w, block, p.xdev, sendx, own)

    def to_y(w, block, own=False):
        send(w, block, p.ydev, sendy, own)

    def to_core(w, block, own=False):
        send(w, block, p.cdev, sendc, own)

    for w in plane:
        to_x(w, mine, True)
        to_y(w, mine, True)
    for w in line:
        to_left(w, mine, True)
        to_right(w, mine, True)
        to_y(w, mine, True)
        to_x(w, mine, True)
    for w in plane:
        to_left(w, mine, True)
        to_right(w, mine, True)
    for w in every:
        to_core(w, mine, True)
        pltpu.make_async_copy(low[w], outs[w].at[mine], local.at[w]).start()
    for s in range(2):
        for k, (dev, peer) in enumerate(peers):
            pltpu.make_async_remote_copy(
                src_ref=part(s, peer),
                dst_ref=swaps[s].at[me],
                send_sem=psend.at[s, k],
                recv_sem=precv.at[s, k],
                device_id=dev,
                device_id_type=MESH,
            ).start()
        pltpu.make_async_copy(part(s, me), swaps[s].at[me], plocal.at[s]).start()

    def plane_x():
        for w in plane:
            block = p.at(z, 1 - x, y, c)
            arrived(w, block)
            to_y(w, block)
            to_left(w, block)
            to_right(w, block)
            to_core(w, block)

    def plane_y(xx):
        for w in plane:
            block = p.at(z, xx, 1 - y, c)
            arrived(w, block)
            to_left(w, block)
            to_right(w, block)
            to_core(w, block)

    def plane_z(zz, from_left):
        for xx, yy in ((x, y), (1 - x, y), (x, 1 - y), (1 - x, 1 - y)):
            for w in plane:
                block = p.at(zz, xx, yy, c)
                arrived(w, block)
                (to_right if from_left else to_left)(w, block)
                to_core(w, block)

    def line_z(zz, from_left):
        block = p.at(zz, x, y, c)
        for w in line:
            arrived(w, block)
            (to_right if from_left else to_left)(w, block)
            to_y(w, block)
            to_x(w, block)
            to_core(w, block)

    def line_y(zz, _):
        block = p.at(zz, x, 1 - y, c)
        for w in line:
            arrived(w, block)
            to_x(w, block)
            to_core(w, block)

    def line_x(zz, _):
        for yy in (y, 1 - y):
            block = p.at(zz, 1 - x, yy, c)
            for w in line:
                arrived(w, block)
                to_core(w, block)

    plane_x()
    p.both(1, line_z)
    plane_y(x)
    plane_y(1 - x)
    p.both(0, line_y)
    p.both(1, plane_z)
    p.both(2, line_z)
    p.both(1, line_y)
    p.both(0, line_x)
    p.both(2, plane_z)
    p.both(3, line_z)
    p.both(2, line_y)
    p.both(1, line_x)
    p.both(3, plane_z)
    p.both(3, line_y)
    p.both(2, line_x)
    p.both(3, line_x)
    for zz in range(Z):
        for xx in range(X):
            for yy in range(Y):
                for w in every:
                    arrived(w, p.at(zz, xx, yy, 1 - c))
    for w in every:
        pltpu.make_async_copy(low[w], outs[w].at[mine], local.at[w]).wait()

        def sent(count, sem):
            span = outs[w].at[pl.ds(0, count)]
            pltpu.make_async_copy(span, span, sem.at[w]).wait()

        wide = X * Y if w in plane else 1
        sent(1 if w in plane else Z * Y, sendx)
        sent(X if w in plane else Z, sendy)
        sent(Z * X * Y, sendc)
        for k in range(Z):
            @pl.when(z == k)
            def _():
                if k > 0:
                    sent(wide * (Z - k), sendl)
                if k < Z - 1:
                    sent(wide * (k + 1), sendr)
    for s in range(2):
        for k, (dev, peer) in enumerate(peers):
            pltpu.make_async_remote_copy(
                src_ref=part(s, peer),
                dst_ref=swaps[s].at[me],
                send_sem=psend.at[s, k],
                recv_sem=precv.at[s, k],
                device_id=dev,
                device_id_type=MESH,
            ).wait()
        pltpu.make_async_copy(part(s, me), swaps[s].at[me], plocal.at[s]).wait()


def gather_all(shards, image, mask, valid, plane_first=PLANE_FIRST, collective=0):
    nw = len(shards)
    n = Z * X * Y * C
    shapes = [s.shape for s in shards[:-1]] + [(8, 128)]
    kinds = [bf16] * (nw - 1) + [f32]
    slots, group, width = image.shape
    here = group // (Y * C)
    anyspec = pl.BlockSpec(memory_space=pl.ANY)
    vm = pl.BlockSpec(memory_space=pltpu.VMEM)
    dma = pltpu.SemaphoreType.DMA
    out = pl.pallas_call(
        functools.partial(gather_kernel, nw, plane_first, valid),
        out_shape=[jax.ShapeDtypeStruct((n,) + s, k) for s, k in zip(shapes, kinds)]
        + [
            jax.ShapeDtypeStruct((Y * C, slots, here, width), image.dtype),
            jax.ShapeDtypeStruct((Y * C, here, 128), f32),
        ],
        in_specs=[vm] * nw + [anyspec, vm],
        out_specs=[anyspec] * (nw + 2),
        scratch_shapes=[pltpu.VMEM(s, k) for s, k in zip(shapes, kinds)]
        + [pltpu.VMEM((group, 128), f32)]
        + [dma((nw, n))] + [dma((nw,))] * 6 + [dma((2, 3)), dma((2, 3)), dma((2,))],
        compiler_params=pltpu.CompilerParams(collective_id=collective, has_side_effects=True),
        name="gather",
    )(*shards, image, mask)
    whole = [o.reshape(n * o.shape[1], o.shape[2]) for o in out[: nw - 1]]
    return whole, out[nw - 1], out[nw].reshape(Y * C * slots, here, width), out[nw + 1]


def scatter_kernel(nw, plane_first, *refs):
    grads = refs[:nw]
    source = refs[nw]
    outs = refs[nw + 1 : 2 * nw + 1]
    swapped = refs[2 * nw + 1]
    rest = refs[2 * nw + 2 :]
    own, from_core, from_x, from_y, from_l, from_r = (rest[nw * i : nw * (i + 1)] for i in range(6))
    (load, rcore, rx, ry, rl, rr, score, sx, sy, sl, sr, psend, precv, plocal) = rest[6 * nw :]
    p = Place()
    z, x, y, c, me = p.z, p.x, p.y, p.c, p.me
    every = range(nw)
    line = [w for w in every if w not in plane_first]
    plane = [w for w in every if w in plane_first]
    half = z // 2
    near = z * (1 - half) + (Z - 1 - z) * half

    def target(k):
        place = (Z - 1, 2 - 2 * near, 1 + near, near)[k]
        return half * (Z - 1) + (1 - 2 * half) * place

    def copy(src, dst, send_sem, recv_sem, dev):
        return pltpu.make_async_remote_copy(
            src_ref=src, dst_ref=dst, send_sem=send_sem, recv_sem=recv_sem, device_id=dev, device_id_type=MESH
        )

    def arrived(dst, sem):
        copy(dst, dst, score.at[0], sem, p.cdev).wait_recv()

    def loads(w, t):
        return pltpu.make_async_copy(grads[w].at[pl.ds(t * X * Y, X * Y), c], own[w].at[pl.ds(t * X * Y, X * Y)], load.at[w, t])

    def add(w, at, count, ref, start):
        def one(i, carry):
            mine = own[w]
            mine[at + i] = (mine[at + i].astype(f32) + ref[start + i].astype(f32)).astype(mine.dtype)
            return carry

        if count == 1:
            one(0, 0)
        else:
            lax.fori_loop(0, count, one, 0)

    def begin(k):
        t = target(k)
        for w in every:
            loads(w, t).start()
            span = pl.ds(t * X * Y, X * Y)
            copy(grads[w].at[span, 1 - c], from_core[w].at[span], score.at[w], rcore.at[w, t], p.cdev).start()

    def core(k):
        t = target(k)
        for w in line + plane:
            loads(w, t).wait()
            span = pl.ds(t * X * Y, X * Y)
            arrived(from_core[w].at[span], rcore.at[w, t])
            add(w, t * X * Y, X * Y, from_core[w], t * X * Y)
            if w in line:
                copy(own[w].at[pl.ds((t * X + 1 - x) * Y, Y)], from_x[w].at[pl.ds(t * Y, Y)], sx.at[w], rx.at[w, t], p.xdev).start()

    def across(k):
        t = target(k)
        for w in line:
            arrived(from_x[w].at[pl.ds(t * Y, Y)], rx.at[w, t])
            add(w, (t * X + x) * Y, Y, from_x[w], t * Y)
            copy(own[w].at[(t * X + x) * Y + 1 - y], from_y[w].at[t], sy.at[w], ry.at[w, t], p.ydev).start()

    def along(k, ws, first, count):
        t = target(k)

        def span(ref):
            return ref.at[pl.ds(first(t), count)]

        def slot(ref):
            return ref.at[pl.ds(t * count, count)]

        def take(w, ref, sem):
            arrived(slot(ref), sem.at[w, t])
            add(w, first(t), count, ref, t * count)

        if k < Z - 1:
            @pl.when(t > z)
            def _():
                for w in ws:
                    @pl.when(z > 0)
                    def _():
                        take(w, from_l[w], rl)

                    copy(span(own[w]), slot(from_l[w]), sr.at[w], rl.at[w, t], p.right).start()

            @pl.when(t < z)
            def _():
                for w in ws:
                    @pl.when(z < Z - 1)
                    def _():
                        take(w, from_r[w], rr)

                    copy(span(own[w]), slot(from_r[w]), sl.at[w], rr.at[w, t], p.left).start()
        else:
            for w in ws:
                @pl.when(z > 0)
                def _():
                    take(w, from_l[w], rl)

                @pl.when(z < Z - 1)
                def _():
                    take(w, from_r[w], rr)

    def down(k):
        t = target(k)
        for w in line:
            arrived(from_y[w].at[t], ry.at[w, t])
            add(w, (t * X + x) * Y + y, 1, from_y[w], t)
        along(k, line, lambda t: (t * X + x) * Y + y, 1)

    barrier = pltpu.get_barrier_semaphore()
    p.greet(barrier)
    p.met(barrier)
    begin(0)
    here = swapped.shape[1] // (Y * C)
    place = swapped.at[:, pl.ds(pl.multiple_of(me * here, here), here)]
    peers = ((p.ydev, p.ypeer), (p.cdev, p.cpeer), (p.ddev, p.dpeer))
    for k, (dev, peer) in enumerate(peers):
        copy(source.at[peer], place, psend.at[k], precv.at[k], dev).start()
    pltpu.make_async_copy(source.at[me], place, plocal).start()
    for k in range(Z + 2):
        if k + 1 < Z:
            begin(k + 1)
        if k < Z:
            core(k)
            along(k, plane, lambda t: t * X * Y, X * Y)
        if 1 <= k <= Z:
            across(k - 1)
        if k == Z - 1:
            for w in plane:
                for xx in range(X):
                    copy(own[w].at[(z * X + xx) * Y + 1 - y], from_y[w].at[xx], sy.at[w], ry.at[w, xx], p.ydev).start()
        if k >= 2:
            down(k - 2)
        if k == Z:
            for w in plane:
                for xx in range(X):
                    arrived(from_y[w].at[xx], ry.at[w, xx])
                    add(w, (z * X + xx) * Y + y, 1, from_y[w], xx)
                copy(own[w].at[(z * X + 1 - x) * Y + y], from_x[w].at[0], sx.at[w], rx.at[w, 0], p.xdev).start()
    for w in plane:
        arrived(from_x[w].at[0], rx.at[w, 0])
        outs[w][...] = own[w][(z * X + x) * Y + y].astype(f32) + from_x[w][0].astype(f32)
    for w in line:
        outs[w][...] = own[w][(z * X + x) * Y + y].astype(f32)
    for w in every:
        wide = w in plane

        def sent(count, sem):
            span = own[w].at[pl.ds(0, count)]
            pltpu.make_async_copy(span, span, sem.at[w]).wait()

        sent(Z * X * Y, score)
        sent(1 if wide else Z * Y, sx)
        sent(X if wide else Z, sy)
        per = X * Y if wide else 1
        for k in range(Z):
            @pl.when(z == k)
            def _():
                if k > 0:
                    sent(per * k, sl)
                if k < Z - 1:
                    sent(per * (Z - 1 - k), sr)
    for k, (dev, peer) in enumerate(peers):
        copy(source.at[peer], place, psend.at[k], precv.at[k], dev).wait()
    pltpu.make_async_copy(source.at[me], place, plocal).wait()


def scatter_all(grads, image_grad, plane_first=PLANE_FIRST, collective=1):
    nw = len(grads)
    blocks = [g.shape[1:] for g in grads]
    slots, items, width = image_grad.shape
    anyspec = pl.BlockSpec(memory_space=pl.ANY)
    vm = pl.BlockSpec(memory_space=pltpu.VMEM)
    dma = pltpu.SemaphoreType.DMA

    def room(line, plane):
        return [
            pltpu.VMEM((plane if w in plane_first else line,) + b, g.dtype)
            for w, (b, g) in enumerate(zip(blocks, grads))
        ]

    every = Z * X * Y
    out = pl.pallas_call(
        functools.partial(scatter_kernel, nw, plane_first),
        out_shape=[jax.ShapeDtypeStruct(b, f32) for b in blocks]
        + [jax.ShapeDtypeStruct((slots // (Y * C), items * Y * C, width), image_grad.dtype)],
        in_specs=[anyspec] * (nw + 1),
        out_specs=[vm] * nw + [anyspec],
        scratch_shapes=room(every, every) + room(every, every) + room(Z * Y, 1) + room(Z, X) + room(Z, every) + room(Z, every)
        + [dma((nw, Z))] * 6 + [dma((nw,))] * 5 + [dma((3,)), dma((3,)), dma],
        compiler_params=pltpu.CompilerParams(collective_id=collective, has_side_effects=True, vmem_limit_bytes=60 << 20),
        name="scatter",
    )(*[g.reshape(every, C, *b) for g, b in zip(grads, blocks)],
      image_grad.reshape(Y * C, slots // (Y * C), items, width))
    return list(out[:nw]), out[nw]


step_rates = (0.05, 0.15, 0.05, 0.05, 0.3, 0.05, 0.05, 0.5)
step_decays = (0.01, 0.01, 0.01, 0.01, 0.01, 0.01, 0.01, 0.0)
BOTH = ("items", "patch")


def in_blocks(norms, count):
    width = D // count
    return jnp.pad(norms.reshape(6, count, width).transpose(1, 0, 2), ((0, 0), (0, 2), (0, 128 - width)))


def on_device(direct, text, cotangent, patches, text_lengths, patch_mask, *state):
    masters, firsts, seconds = state[:8], state[8:16], state[16:]
    group, local = patch_mask.shape
    chunks = lax.axis_size("patch")
    items = group // chunks
    devices = chunks * lax.axis_size("items")
    by_slot = patches.transpose(1, 0, 2)
    if direct:
        weights, blocks, image, masks = gather_all(masters, by_slot, patch_mask, VALID)
    else:
        weights = [lax.all_gather(m.astype(bf16), BOTH, axis=0, tiled=True) for m in masters[:7]]
        blocks = in_blocks(lax.all_gather(masters[7].astype(bf16), BOTH, axis=1, tiled=True).astype(f32), devices)
        image = lax.all_to_all(by_slot.reshape(local, chunks, items, ENC), "patch", 1, 0)
        image = image.reshape(chunks * local, items, ENC)
        masks = patch_bias(patch_mask, lax.axis_index("patch") * local, VALID)
        masks = jnp.pad(masks, ((0, 0), (0, 128 - local))).reshape(chunks, items, 128)
        masks = lax.all_to_all(masks, "patch", 0, 0)
    block_output, text_grad, image_grad, grads, grad_blocks = local_step(
        text, cotangent, image, masks, text_lengths, weights, blocks
    )
    image_grad = image_grad.reshape(image.shape)
    if direct:
        grads = [g.reshape(devices, -1, g.shape[1]) for g in grads]
        reduced, image_grad = scatter_all([*grads, grad_blocks], image_grad)
    else:
        reduced = [lax.psum_scatter(g, BOTH, scatter_dimension=0, tiled=True).astype(f32) for g in grads]
        reduced.append(lax.psum_scatter(grad_blocks, BOTH, scatter_dimension=0, tiled=True)[0])
        image_grad = lax.all_to_all(image_grad.reshape(chunks, local, items, ENC), "patch", 0, 1)
        image_grad = image_grad.reshape(local, group, ENC)
    state_shapes = [(m.shape, f32) for m in masters]
    *updated, patch_grad = call(
        functools.partial(adamw, 8, step_decays, step_rates),
        (*masters, *firsts, *seconds, *reduced, image_grad),
        [*state_shapes * 3, (image_grad.shape, f32)], [], "adamw",
    )
    return (block_output, text_grad, patch_grad.transpose(1, 0, 2), *updated)


def solution(mesh):
    rows, cols = P(BOTH, None), P(None, BOTH)
    state = (*[rows] * 7, cols)
    direct = dict(mesh.shape) == {"items": Z * X, "patch": Y * C}
    return jax.shard_map(
        functools.partial(on_device, direct),
        mesh=mesh,
        in_specs=(rows, rows, P("items", "patch", None), P(BOTH), P("items", "patch"), *state * 3),
        out_specs=(rows, rows, P("items", "patch", None), *state * 3),
        check_vma=False,
    )
```

```python
import functools

import jax
import jax.numpy as jnp
from jax import lax
from jax.experimental import pallas as pl
from jax.experimental.pallas import tpu as pltpu
from jax.sharding import PartitionSpec as P

D = 768
HEADS = 12
HEAD_DIM = 64
ENC = 1024
TEXT = 40
VALID = 145
PAIR = 2 * HEAD_DIM
PAIRS = HEADS // 2
SCALE = HEAD_DIM ** (-0.5)
OUTSIDE = -1e30
bf16, f32 = jnp.bfloat16, jnp.float32


def dot(a, b):
    return jnp.dot(a, b, preferred_element_type=f32)


def dot_nt(a, b):
    return lax.dot_general(a, b, (((1,), (1,)), ((), ())), preferred_element_type=f32)


def dot_tn(a, b):
    return lax.dot_general(a, b, (((0,), (0,)), ((), ())), preferred_element_type=f32)


def quiet():
    pass


def chunks_of(count, parts, body, pause):
    def run(k, carry):
        body(k)
        return carry

    for part in range(parts):
        lax.fori_loop(count * part // parts, count * (part + 1) // parts, run, 0)
        if part < parts - 1:
            pause()


def tiles(total, step, body):
    def run(k, carry):
        body(pl.ds(pl.multiple_of(k * step, step), step))
        return carry

    lax.fori_loop(0, total // step, run, 0)


def norm_forward(values):
    center = values - jnp.mean(values, axis=-1, keepdims=True)
    inverse = lax.rsqrt(jnp.mean(center * center, axis=-1, keepdims=True) + 1e-12)
    return center * inverse, inverse


def norm_backward(grad_out, normed, inverse, gain):
    grad_gain = jnp.sum(grad_out * normed, axis=0, keepdims=True)
    grad_shift = jnp.sum(grad_out, axis=0, keepdims=True)
    scaled = grad_out * gain
    grad_values = inverse * (
        scaled
        - jnp.mean(scaled, axis=-1, keepdims=True)
        - normed * jnp.mean(scaled * normed, axis=-1, keepdims=True)
    )
    return grad_values, grad_gain, grad_shift


def low_half():
    return lax.broadcasted_iota(jnp.int32, (TEXT, PAIR), 1) < HEAD_DIM


def expand(rows):
    low = low_half()
    return jnp.concatenate(
        [jnp.where(low, rows, 0.0), jnp.where(low, 0.0, rows)], axis=0
    ).astype(bf16)


def fold(rows):
    return jnp.where(low_half(), rows[:TEXT], rows[TEXT:])


def softmax(scores):
    top = jnp.max(scores, axis=-1, keepdims=True)
    powers = jnp.exp(scores - top)
    return powers / jnp.sum(powers, axis=-1, keepdims=True)


def pair_cols(j, start=0):
    return slice(start + PAIR * j, start + PAIR * (j + 1))


def pair_rows(j):
    return slice(2 * TEXT * j, 2 * TEXT * (j + 1))


def attend_forward(query, keys, values, bias, probs, item, context, rows):
    js = range(PAIRS)
    scores = [dot_nt(expand(query(j)), keys(j)) * SCALE + bias for j in js]
    weights = [softmax(s) for s in scores]
    for j in js:
        probs[item, pair_rows(j), :] = weights[j]
    parts = [dot(weights[j].astype(bf16), values(j)) for j in js]
    for j in js:
        context[rows, pair_cols(j)] = fold(parts[j])


def attend_backward(query, keys, values, probs, item, grad_context, put_q, put_k, put_v):
    js = range(PAIRS)
    outer = [expand(grad_context(j)) for j in js]
    grads = [dot_nt(outer[j], values(j)) for j in js]
    inner = []
    for j in js:
        weights = probs[item, pair_rows(j), :]
        delta = jnp.sum(weights * grads[j], axis=-1, keepdims=True)
        inner.append((weights * (grads[j] - delta)).astype(bf16))
    for j in js:
        put_v(j, dot_tn(probs[item, pair_rows(j), :].astype(bf16), outer[j]))
    for j in js:
        put_q(j, fold(dot(inner[j], keys(j))) * SCALE)
    for j in js:
        put_k(j, dot_tn(inner[j], expand(query(j))) * SCALE)


def self_forward(lengths, text, w_qkv, w_out, blocks, mixed, probs, ctx, normed, inverse, norms, mix, context,
                 pause=quiet, parts=1):
    spread(blocks, norms)

    def project(cols):
        got = dot(text[...], w_qkv[:, cols]).astype(bf16)
        mixed[:, cols] = got
        mix[:, cols] = got.astype(f32)

    tiles(3 * D, 768, project)
    pause()
    position = lax.broadcasted_iota(jnp.int32, (1, TEXT), 1)

    def one(item):
        rows = pl.ds(pl.multiple_of(item * TEXT, 8), TEXT)
        bias = jnp.where(position < lengths[item], 0.0, -10000.0).astype(f32)
        attend_forward(
            lambda j: mix[rows, pair_cols(j)],
            lambda j: mix[rows, pair_cols(j, D)].astype(bf16),
            lambda j: mix[rows, pair_cols(j, 2 * D)].astype(bf16),
            bias, probs, item, context, rows,
        )

    chunks_of(probs.shape[0], parts, one, pause)
    pause()
    ctx[...] = context[...].astype(bf16)
    pre = text[...].astype(f32) + dot(ctx[...], w_out[...])
    n, r = norm_forward(pre)
    normed[...] = n
    inverse[...] = r


def self_backward(text, mixed, probs, ctx, normed, inverse, grad_after, w_qkv, w_out, norms, g_second, g_third,
                  g_qkv, g_out, text_grad, g_blocks, mix, grad_ctx, grad_mix, low_mix,
                  pause=quiet, parts=1, wide=1):
    grad_pre, grad_gain, grad_shift = norm_backward(grad_after[...], normed[...], inverse[...], norms[0:1, :])
    rows = jnp.concatenate([grad_gain, grad_shift, g_second[...], g_third[...], jnp.zeros((2, D), f32)], axis=0)
    count = g_blocks.shape[0] // 8
    width = D // count
    g_blocks[...] = jnp.zeros(g_blocks.shape, f32)
    for b in range(count):
        g_blocks[8 * b : 8 * b + 8, :width] = rows[:, width * b : width * (b + 1)]
    low = grad_pre.astype(bf16)
    g_out[...] = dot_tn(ctx[...], low).astype(bf16)
    grad_ctx[...] = dot_nt(low, w_out[...]).astype(bf16).astype(f32)
    text_grad[...] = grad_pre
    mix[...] = mixed[...].astype(f32)
    pause()

    def one(item):
        rows = pl.ds(pl.multiple_of(item * TEXT, 8), TEXT)

        def put(start):
            def store(j, value):
                grad_mix[rows, pair_cols(j, start)] = value
            return store

        attend_backward(
            lambda j: mix[rows, pair_cols(j)],
            lambda j: mix[rows, pair_cols(j, D)].astype(bf16),
            lambda j: mix[rows, pair_cols(j, 2 * D)].astype(bf16),
            probs, item, lambda j: grad_ctx[rows, pair_cols(j)],
            put(0), put(D), put(2 * D),
        )

    chunks_of(probs.shape[0], parts, one, pause)
    pause()
    low_mix[...] = grad_mix[...].astype(bf16)

    def weights(k):
        cols = pl.ds(pl.multiple_of(k * D, D), D)
        g_qkv[:, cols] = dot_tn(text[...], low_mix[:, cols]).astype(bf16)
        text_grad[...] += dot_nt(low_mix[:, cols], w_qkv[:, cols])

    chunks_of(3, wide, weights, pause)


def spread(blocks, norms):
    count = blocks.shape[0] // 8
    width = D // count
    for b in range(count):
        norms[:, width * b : width * (b + 1)] = blocks[8 * b : 8 * b + 8, :width]


def cross_forward(image, masks, w_kv, w_q, w_out, norms, normed_one,
                  memory, query, probs, ctx, normed, inverse, bias, context, wide, flat,
                  pause=quiet, tall=1, parts=1):
    items = masks.shape[1]
    slots = bias.shape[1]
    local = slots // masks.shape[0]
    for c in range(masks.shape[0]):
        bias[:, local * c : local * (c + 1)] = masks[c, :, :local]

    def project(k):
        got = dot(image[...], w_kv[:, pl.ds(pl.multiple_of(4 * PAIR * k, 4 * PAIR), 4 * PAIR)]).astype(bf16).astype(f32)
        for j in range(4):
            flat[4 * k + j] = got[:, pair_cols(j)]

    chunks_of(PAIRS // 2, tall, project, pause)
    pause()
    after = normed_one[...] * norms[0:1, :] + norms[1:2, :]
    low = dot(after.astype(bf16), w_q[...]).astype(bf16)
    query[...] = low
    wide[...] = low.astype(f32)

    def one(item):
        rows = pl.ds(pl.multiple_of(item * TEXT, 8), TEXT)
        every = pl.ds(item, slots, stride=items)
        for j in range(2 * PAIRS):
            memory[item, :, pair_cols(j)] = flat[j, every, :].astype(bf16)
        attend_forward(
            lambda j: wide[rows, pair_cols(j)],
            lambda j: memory[item, :, pair_cols(j)],
            lambda j: memory[item, :, pair_cols(j, D)],
            bias[pl.ds(item, 1), :], probs, item, context, rows,
        )

    chunks_of(items, parts, one, pause)
    pause()
    ctx[...] = context[...].astype(bf16)
    pre = after + dot(ctx[...], w_out[...])
    n, r = norm_forward(pre)
    normed[...] = n
    inverse[...] = r


def cross_backward(memory, query, probs, ctx, normed, inverse, normed_one, grad_after, w_q, w_out, norms,
                   g_q, g_out, grad_self, g_norm, flat, wide, grad_ctx, grad_q, pause=quiet, parts=1):
    items, slots = memory.shape[:2]
    grad_pre, grad_gain, grad_shift = norm_backward(grad_after[...], normed[...], inverse[...], norms[2:3, :])
    g_norm[0:1, :] = grad_gain
    g_norm[1:2, :] = grad_shift
    grad_self[...] = grad_pre
    low = grad_pre.astype(bf16)
    g_out[...] = dot_tn(ctx[...], low).astype(bf16)
    grad_ctx[...] = dot_nt(low, w_out[...]).astype(bf16).astype(f32)
    wide[...] = query[...].astype(f32)
    pause()

    def one(item):
        rows = pl.ds(pl.multiple_of(item * TEXT, 8), TEXT)
        every = pl.ds(item, slots, stride=items)

        def put_q(j, value):
            grad_q[rows, pair_cols(j)] = value

        def put(start):
            def store(j, value):
                flat[start + j, every, :] = value
            return store

        attend_backward(
            lambda j: wide[rows, pair_cols(j)],
            lambda j: memory[item, :, pair_cols(j)],
            lambda j: memory[item, :, pair_cols(j, D)],
            probs, item, lambda j: grad_ctx[rows, pair_cols(j)],
            put_q, put(0), put(PAIRS),
        )

    chunks_of(items, parts, one, pause)
    low_q = grad_q[...].astype(bf16)
    after = (normed_one[...] * norms[0:1, :] + norms[1:2, :]).astype(bf16)
    g_q[...] = dot_tn(after, low_q).astype(bf16)
    grad_self[...] += dot_nt(low_q, w_q[...])


def memory_backward(image, w_kv, flat, g_kv, image_grad, grad_mem, pause=quiet, wide=1):
    for j in range(2 * PAIRS):
        grad_mem[:, pair_cols(j)] = flat[j].astype(bf16)
    step = 4 * PAIR

    def weights(k):
        cols = pl.ds(pl.multiple_of(k * step, step), step)
        g_kv[:, cols] = dot_tn(image[...], grad_mem[:, cols]).astype(bf16)

    chunks_of(2 * D // step, wide, weights, pause)
    pause()

    def back(k):
        cols = pl.ds(pl.multiple_of(k * step, step), step)
        image_grad[:, cols] = dot_nt(grad_mem[...], w_kv[cols, :]).astype(bf16)

    chunks_of(ENC // step, 1, back, pause)


def feed_forward(normed_two, cotangent, w_inner, w_outer, norms,
                 block_output, g_inner, g_outer, grad_after, g_norm, low_in, hidden, slope, total, grad_low, grad_hid):
    after = normed_two[...] * norms[2:3, :] + norms[3:4, :]
    low_in[...] = after.astype(bf16)
    total[...] = after

    def up(cols):
        pre = dot(low_in[...], w_inner[:, cols])
        bell = 0.5 * (1.0 + lax.erf(pre * (0.5 ** 0.5)))
        low = (pre * bell).astype(bf16)
        hidden[:, cols] = low
        slope[:, cols] = bell + pre * jnp.exp(-0.5 * pre * pre) * 0.3989422804014327
        total[...] += dot(low, w_outer[cols, :])

    ff = w_inner.shape[1]
    tiles(ff, 768, up)
    n, r = norm_forward(total[...])
    gain = norms[4:5, :]
    block_output[...] = (n * gain + norms[5:6, :]).astype(bf16)
    grad_pre, grad_gain, grad_shift = norm_backward(cotangent[...].astype(f32), n, r, gain)
    g_norm[0:1, :] = grad_gain
    g_norm[1:2, :] = grad_shift
    grad_after[...] = grad_pre
    grad_low[...] = grad_pre.astype(bf16)

    def down(cols):
        low = (dot_nt(grad_low[...], w_outer[cols, :]) * slope[:, cols]).astype(bf16)
        g_inner[:, cols] = dot_tn(low_in[...], low).astype(bf16)
        g_outer[cols, :] = dot_tn(hidden[:, cols], grad_low[...]).astype(bf16)
        grad_after[...] += dot_nt(low, w_inner[:, cols])

    tiles(ff, 768, down)


VM = pl.BlockSpec(memory_space=pltpu.VMEM)


def call(body, args, outs, scratch, name, smem=0, limit=60 << 20):
    return pl.pallas_call(
        body,
        out_shape=[jax.ShapeDtypeStruct(s, k) for s, k in outs],
        in_specs=[pl.BlockSpec(memory_space=pltpu.SMEM)] * smem + [VM] * (len(args) - smem),
        out_specs=[VM] * len(outs),
        scratch_shapes=[pltpu.VMEM(s, k) for s, k in scratch],
        compiler_params=pltpu.CompilerParams(vmem_limit_bytes=limit),
        name=name,
    )(*args)


def adamw(count, decays, rates, *refs):
    masters, firsts, seconds, grads = (refs[count * i : count * (i + 1)] for i in range(4))
    image_low = refs[4 * count]
    new_m, new_f, new_s = (refs[4 * count + 1 + count * i : 4 * count + 1 + count * (i + 1)] for i in range(3))
    image_grad = refs[7 * count + 1]
    for k in range(count):
        rows, cols = masters[k].shape
        gradient = grads[k][:rows, :cols]
        first = 0.9 * firsts[k][...] + 0.1 * gradient
        second = 0.999 * seconds[k][...] + 0.001 * gradient * gradient
        step = first / (1.0 - 0.9**10) / (jnp.sqrt(second / (1.0 - 0.999**10)) + 1e-08)
        master = masters[k][...]
        new_m[k][...] = master - rates[k] * (step + decays[k] * master)
        new_f[k][...] = first
        new_s[k][...] = second
    image_grad[...] = image_low[...].astype(f32)


def forward_local(text, lengths, image, masks, ws, blocks):
    w_qkv, w_out, w_cq, w_kv, w_co = ws[:5]
    rows = text.shape[0]
    items = rows // TEXT
    slots = image.shape[0] // items
    pairs = HEADS * TEXT
    row = ((rows, D), f32)
    rowl = ((rows, D), bf16)
    one = ((rows, 1), f32)
    *first, norms = call(
        self_forward, (lengths, text, w_qkv, w_out, blocks),
        [((rows, 3 * D), bf16), ((items, pairs, TEXT), f32), rowl, row, one, ((8, D), f32)],
        [((rows, 3 * D), f32), row], "self_forward", smem=1)
    second = call(
        cross_forward, (image, masks, w_kv, w_cq, w_co, norms, first[3]),
        [((items, slots, 2 * D), bf16), rowl, ((items, pairs, slots), f32), rowl, row, one],
        [((items, slots), f32), row, row, ((2 * PAIRS, items * slots, PAIR), f32)], "cross_forward")
    return norms, [*first, *second]


def feed_forward_call(cotangent, ws, norms, n2):
    w_in, w_outer = ws
    rows, ff = n2.shape[0], w_in.shape[1]
    row = ((rows, D), f32)
    rowl = ((rows, D), bf16)
    return call(
        feed_forward, (n2, cotangent, w_in, w_outer, norms),
        [rowl, ((D, ff), bf16), ((ff, D), bf16), row, ((2, D), f32)],
        [rowl, ((rows, ff), bf16), ((rows, ff), f32), row, rowl, rowl], "feed_forward")


def backward_local(text, image, ws, norms, saved, grad_after, gn3, count):
    w_qkv, w_out, w_cq, w_kv, w_co = ws
    mixed, probs, ctx, n1, r1, memory, query, cprobs, cctx, n2, r2 = saved
    rows = text.shape[0]
    row = ((rows, D), f32)
    flat = (2 * PAIRS, image.shape[0], PAIR)
    g_cq, g_co, grad_self, gn2, flat_grad = call(
        cross_backward, (memory, query, cprobs, cctx, n2, r2, n1, grad_after, w_cq, w_co, norms),
        [((D, D), bf16), ((D, D), bf16), row, ((2, D), f32), (flat, f32)], [row, row, row], "cross_backward")
    g_kv, image_grad = call(
        memory_backward, (image, w_kv, flat_grad), [((ENC, 2 * D), bf16), (image.shape, bf16)],
        [((image.shape[0], 2 * D), bf16)], "memory_backward")
    g_qkv, g_out, text_grad, g_blocks = call(
        self_backward, (text, mixed, probs, ctx, n1, r1, grad_self, w_qkv, w_out, norms, gn2, gn3),
        [((D, 3 * D), bf16), ((D, D), bf16), row, ((count * 8, 128), f32)],
        [((rows, 3 * D), f32), row, ((rows, 3 * D), f32), ((rows, 3 * D), bf16)], "self_backward")
    return text_grad, image_grad, (g_qkv, g_out, g_cq, g_kv, g_co), g_blocks


MESH = pl.DeviceIdType.MESH
Z, X, Y, C = 4, 2, 2, 2
PLANE_FIRST = (0, 6)
SETS = ((0, 1, 7, 3, 2, 4), (5, 6))
PLANE_LAST = (6, 3)
PLAN = (
    ("0", "00", "01", "1", "02", "10", "swap", "03", "11", "04", "12", "05", "06", "swapped"),
    ((), ("13",)),
    (),
    (("14",), (), (), ("15",)),
    ("16",),
)
ROUNDS = tuple((k, (6, 5)) for k in range(4)) + tuple((k, (0, 1, 2, 3, 4, 7)) for k in range(4))
BACK_PLAN = (
    (100, 101), (0, 102), (), (1, 103), (), (2,), (), (3,), (), (), (), (),
    (104, 105, 200, 4, 106), (5, 107), (6,), (7,), (8,), (9,),
)
bf16, f32 = jnp.bfloat16, jnp.float32


class Place:
    def __init__(self):
        item, self.me = lax.axis_index("items"), lax.axis_index("patch")
        self.z, self.x, self.y, self.c = item // X, item % X, self.me // C, self.me % C
        z, x, y, c = self.z, self.x, self.y, self.c
        self.left = (item - X, self.me)
        self.right = (item + X, self.me)
        self.xdev = (z * X + (1 - x), self.me)
        self.ypeer, self.cpeer, self.dpeer = (1 - y) * C + c, y * C + (1 - c), (1 - y) * C + (1 - c)
        self.ydev, self.cdev, self.ddev = (item, self.ypeer), (item, self.cpeer), (item, self.dpeer)

    def at(self, zz, xx, yy, cc):
        return ((zz * X + xx) * Y + yy) * C + cc

    def greet(self, barrier):
        for dev in (self.xdev, self.ydev, self.cdev, self.ddev):
            pl.semaphore_signal(barrier, inc=1, device_id=dev, device_id_type=MESH)

        @pl.when(self.z > 0)
        def _():
            pl.semaphore_signal(barrier, inc=1, device_id=self.left, device_id_type=MESH)

        @pl.when(self.z < Z - 1)
        def _():
            pl.semaphore_signal(barrier, inc=1, device_id=self.right, device_id_type=MESH)

    def met(self, barrier):
        pl.semaphore_wait(barrier, 4 + (self.z > 0).astype(jnp.int32) + (self.z < Z - 1).astype(jnp.int32))

    def both(self, d, step):
        if d == 0:
            step(self.z, None)
            return

        @pl.when(self.z >= d)
        def _():
            step(self.z - d, True)

        @pl.when(self.z + d < Z)
        def _():
            step(self.z + d, False)


def patch_bias(mask, first, valid):
    index = first + lax.broadcasted_iota(jnp.int32, mask.shape, 1)
    return jnp.where((mask > 0) & (index < valid), 0.0, -10000.0).astype(f32)


class Gather:
    def __init__(self, place, plane_first, low, outs, recv, to_x, to_y, to_c, to_l, to_r, local):
        self.place, self.plane_first, self.low, self.outs, self.recv, self.local = place, plane_first, low, outs, recv, local
        self.sems = {"x": to_x, "y": to_y, "c": to_c, "l": to_l, "r": to_r}
        self.devs = {"x": place.xdev, "y": place.ydev, "c": place.cdev, "l": place.left, "r": place.right}
        self.mine = place.at(place.z, place.x, place.y, place.c)

    def blocks(self, w, first, count=1):
        rows = self.low[w].shape[0]
        return self.outs[w].at[pl.ds(pl.multiple_of(first * rows, rows), count * rows)]

    def copy(self, w, block, way, own=False):
        return pltpu.make_async_remote_copy(
            src_ref=self.low[w] if own else self.blocks(w, block),
            dst_ref=self.blocks(w, block),
            send_sem=self.sems[way].at[w],
            recv_sem=self.recv.at[w, block],
            device_id=self.devs[way],
            device_id_type=MESH,
        )

    def send(self, w, block, ways, own=False):
        z = self.place.z
        for way in ways:
            if way == "l":
                @pl.when(z > 0)
                def _():
                    self.copy(w, block, "l", own).start()
            elif way == "r":
                @pl.when(z < Z - 1)
                def _():
                    self.copy(w, block, "r", own).start()
            else:
                self.copy(w, block, way, own).start()

    def arrived(self, w, block):
        self.copy(w, block, "x").wait_recv()

    def pass_on(self, w, block, ways):
        self.arrived(w, block)
        self.send(w, block, ways)

    def keep(self, w):
        return pltpu.make_async_copy(self.low[w], self.blocks(w, self.mine), self.local.at[w])

    def start(self, ws):
        for w in ws:
            self.send(w, self.mine, "xylr" if w in self.plane_first else "lryx", True)
        for w in ws:
            self.send(w, self.mine, "c", True)
            self.keep(w).start()

    def stages(self, ws):
        p = self.place
        x, y, c = p.x, p.y, p.c
        line = [w for w in ws if w not in self.plane_first]
        plane = [w for w in ws if w in self.plane_first]

        def plane_x():
            for w in plane:
                self.pass_on(w, p.at(p.z, 1 - x, y, c), "ylrc")

        def plane_y():
            for xx in (x, 1 - x):
                for w in plane:
                    self.pass_on(w, p.at(p.z, xx, 1 - y, c), "lrc")

        def plane_z(zz, from_left):
            for xx, yy in ((x, y), (1 - x, y), (x, 1 - y), (1 - x, 1 - y)):
                for w in plane:
                    self.pass_on(w, p.at(zz, xx, yy, c), "rc" if from_left else "lc")

        def line_z(zz, from_left):
            for w in line:
                self.pass_on(w, p.at(zz, x, y, c), "ryxc" if from_left else "lyxc")

        def line_y(zz, _):
            for w in line:
                self.pass_on(w, p.at(zz, x, 1 - y, c), "xc")

        def line_x(zz, _):
            for yy in (y, 1 - y):
                for w in line:
                    self.pass_on(w, p.at(zz, 1 - x, yy, c), "c")

        def from_core():
            for zz in range(Z):
                for xx in range(X):
                    for yy in range(Y):
                        for w in ws:
                            self.arrived(w, p.at(zz, xx, yy, 1 - c))
            for w in ws:
                self.keep(w).wait()

        def steps(*pairs):
            def run():
                for d, step in pairs:
                    if d is None:
                        step()
                    else:
                        p.both(d, step)
            return run

        first = [(None, plane_x)] if plane else []
        second = [(None, plane_y)] if plane else []

        def deep(d):
            return [(d, plane_z)] if plane else []

        if not line:
            return [steps(*first), steps(*second), steps(*deep(1)), steps(*deep(2)), steps(*deep(3)), quiet, from_core]
        return [
            steps(*first, (1, line_z)),
            steps(*second, (0, line_y)),
            steps(*deep(1), (2, line_z), (1, line_y), (0, line_x)),
            steps(*deep(2), (3, line_z), (2, line_y), (1, line_x)),
            steps(*deep(3), (3, line_y), (2, line_x)),
            steps((3, line_x)),
            from_core,
        ]

    def finish(self):
        z = self.place.z
        for w in range(len(self.low)):
            def sent(count, way):
                span = self.blocks(w, 0, count)
                pltpu.make_async_copy(span, span, self.sems[way].at[w]).wait()

            plane = w in self.plane_first
            wide = X * Y if plane else 1
            sent(1 if plane else Z * Y, "x")
            sent(X if plane else Z, "y")
            sent(Z * X * Y, "c")
            for k in range(Z):
                @pl.when(z == k)
                def _():
                    if k > 0:
                        sent(wide * (Z - k), "l")
                    if k < Z - 1:
                        sent(wide * (k + 1), "r")


def forward_kernel(plane_first, sets, plan, valid, *refs):
    nw = 8
    refs = list(refs)

    def take(count):
        got = refs[:count]
        del refs[:count]
        return got

    (lengths,), shards, (image, mask, text) = take(1), take(nw), take(3)
    whole, (image_out, norms) = take(nw - 1), take(2)
    saved = take(11)
    low, (blocks, masks, bias_here) = take(nw), take(3)
    w_qkv, w_out, w_cq, w_kv, w_co = take(5)
    image_in, mix, context, bias, wide, flat = take(6)
    kept = take(11)
    recv, to_x, to_y, to_c, to_l, to_r, local, psend, precv, plocal, load, save = take(12)
    p = Place()
    me = p.me
    barrier = pltpu.get_barrier_semaphore()
    p.greet(barrier)
    for w in range(nw - 1):
        low[w][...] = shards[w][...].astype(low[w].dtype)
    low[nw - 1][...] = jnp.zeros(low[nw - 1].shape, f32)
    rows, cols = shards[nw - 1].shape
    low[nw - 1][:rows, :cols] = shards[nw - 1][...].astype(bf16).astype(f32)
    slots = mask.shape[1]
    bias_here[...] = jnp.zeros(bias_here.shape, f32)
    bias_here[:, :slots] = patch_bias(mask[...], me * slots, valid)
    here = mask.shape[0] // (Y * C)
    peers = ((p.ydev, p.ypeer), (p.cdev, p.cpeer), (p.ddev, p.dpeer))
    swaps = (image_out, masks)

    def part(s, peer):
        rows = pl.ds(pl.multiple_of(peer * here, here), here)
        return bias_here.at[rows] if s else image.at[:, rows]

    def swap(s, k):
        dev, peer = peers[k]
        return pltpu.make_async_remote_copy(
            src_ref=part(s, peer),
            dst_ref=swaps[s].at[me],
            send_sem=psend.at[s, k],
            recv_sem=precv.at[s, k],
            device_id=dev,
            device_id_type=MESH,
        )

    def stay(s):
        return pltpu.make_async_copy(part(s, me), swaps[s].at[me], plocal.at[s])

    gather = Gather(p, plane_first, low, [*whole, blocks], recv, to_x, to_y, to_c, to_l, to_r, local)
    staged = [gather.stages(ws) for ws in sets]
    p.met(barrier)

    def start_swaps():
        for s in range(2):
            for k in range(3):
                swap(s, k).start()
            stay(s).start()

    def end_swaps():
        for s in range(2):
            for k in range(3):
                swap(s, k).wait()
            stay(s).wait()

    def loads(pairs):
        return [pltpu.make_async_copy(src, dst, load.at[k]) for k, src, dst in pairs]

    early = loads([(0, whole[0], w_qkv), (1, whole[1], w_out)])
    late = loads([(2, whole[2], w_cq), (3, whole[3], w_kv), (4, whole[4], w_co)])

    def flatten(k, carry):
        rows = pl.ds(pl.multiple_of(k * here, here), here)
        pltpu.make_async_copy(image_out.at[k // slots, k % slots], image_in.at[rows], load.at[5]).start()
        return carry
    saves = [pltpu.make_async_copy(src, dst, save.at[k]) for k, (src, dst) in enumerate(zip(kept, saved))]

    def run(tokens):
        for token in tokens:
            if token == "swap":
                start_swaps()
            elif token == "swapped":
                end_swaps()
            elif len(token) == 1:
                gather.start(sets[int(token)])
            else:
                staged[int(token[0])][int(token[1])]()

    def queue(events):
        left = list(events)

        def pause():
            if left:
                run(left.pop(0))

        return pause

    before, during_self, between, during_cross, after = plan
    run(before)
    for copy in early:
        copy.start()
    for copy in early:
        copy.wait()
    mixed, probs, ctx, normed, inverse, memory, query, cross_probs, cross_ctx, normed_two, inverse_two = kept
    self_forward(
        lengths, text, w_qkv, w_out, blocks, mixed, probs, ctx, normed, inverse, norms, mix, context,
        queue(during_self), 2,
    )
    for copy in saves[:5]:
        copy.start()
    run(between)
    for copy in late:
        copy.start()
    lax.fori_loop(0, Y * C * slots, flatten, 0)
    for copy in late:
        copy.wait()
    pltpu.make_async_copy(image_in, image_in, load.at[5]).wait()
    cross_forward(
        image_in, masks, w_kv, w_cq, w_co, norms, normed,
        memory, query, cross_probs, cross_ctx, normed_two, inverse_two, bias, context, wide, flat,
        queue(during_cross), 2, 4,
    )
    for copy in saves[5:]:
        copy.start()
    run(after)
    gather.finish()
    for copy in saves:
        copy.wait()


def forward_all(text, lengths, shards, image, mask, valid, plane_first=PLANE_FIRST, sets=SETS, plan=PLAN, collective=0):
    nw = len(shards)
    n = Z * X * Y * C
    shapes = [s.shape for s in shards[:-1]] + [(8, 128)]
    kinds = [bf16] * (nw - 1) + [f32]
    slots, group, width = image.shape
    items = group // (Y * C)
    rows = text.shape[0]
    every = slots * Y * C
    pairs = HEADS * TEXT
    row, low_row, one = ((rows, D), f32), ((rows, D), bf16), ((rows, 1), f32)
    keep = [
        ((rows, 3 * D), bf16), ((items, pairs, TEXT), f32), low_row, row, one,
        ((items, every, 2 * D), bf16), low_row, ((items, pairs, every), f32), low_row, row, one,
    ]
    anyspec = pl.BlockSpec(memory_space=pl.ANY)
    dma = pltpu.SemaphoreType.DMA
    shape = jax.ShapeDtypeStruct
    out = pl.pallas_call(
        functools.partial(forward_kernel, plane_first, sets, plan, valid),
        out_shape=[shape((n * s[0], s[1]), bf16) for s in shapes[:-1]]
        + [shape((Y * C, slots, items, width), image.dtype), shape((8, D), f32)]
        + [shape(*k) for k in keep],
        in_specs=[pl.BlockSpec(memory_space=pltpu.SMEM)] + [VM] * nw + [anyspec, VM, VM],
        out_specs=[anyspec] * nw + [VM] + [anyspec] * len(keep),
        scratch_shapes=[pltpu.VMEM(s, k) for s, k in zip(shapes, kinds)]
        + [pltpu.VMEM((n * 8, 128), f32), pltpu.VMEM((Y * C, items, 128), f32), pltpu.VMEM((group, 128), f32)]
        + [pltpu.VMEM((n * shapes[w][0], shapes[w][1]), bf16) for w in range(5)]
        + [pltpu.VMEM(s, k) for s, k in (
            ((every * items, width), bf16), ((rows, 3 * D), f32), row, ((items, every), f32), row,
            ((2 * PAIRS, items * every, PAIR), f32), *keep)]
        + [dma((nw, n))] + [dma((nw,))] * 6 + [dma((2, 3)), dma((2, 3)), dma((2,)), dma((6,)), dma((len(keep),))],
        compiler_params=pltpu.CompilerParams(collective_id=collective, has_side_effects=True, vmem_limit_bytes=60 << 20),
        name="forward",
    )(lengths, *shards, image, mask, text)
    return out[: nw - 1], out[nw - 1].reshape(every * items, width), out[nw], out[nw + 1 :]


class Scatter:
    def __init__(self, place, plane_first, grads, own, from_core, from_x, from_y, from_z, sems):
        self.place, self.plane_first, self.grads, self.own = place, plane_first, grads, own
        self.from_core, self.from_x, self.from_y, self.from_z = from_core, from_x, from_y, from_z
        self.load, self.rcore, self.rx, self.ry, self.rl, self.rr, self.score, self.sx, self.sy, self.sl, self.sr = sems

    def target(self, k):
        half = self.place.z // 2
        near = self.place.z * (1 - half) + (Z - 1 - self.place.z) * half
        return half * (Z - 1) + (1 - 2 * half) * (Z - 1, 2 - 2 * near, 1 + near, near)[k]

    def copy(self, src, dst, send_sem, recv_sem, dev):
        return pltpu.make_async_remote_copy(
            src_ref=src, dst_ref=dst, send_sem=send_sem, recv_sem=recv_sem, device_id=dev, device_id_type=MESH
        )

    def arrived(self, dst, sem):
        self.copy(dst, dst, self.score.at[0], sem, self.place.cdev).wait_recv()

    def block(self, w, b):
        rows = self.own[w].shape[1]
        return self.grads[w].at[pl.ds(pl.multiple_of(b * rows, rows), rows)]

    def add(self, w, at, count, ref, start):
        mine = self.own[w]

        def one(i, carry):
            mine[at + i] = (mine[at + i].astype(f32) + ref[start + i].astype(f32)).astype(mine.dtype)
            return carry

        if count == 1:
            one(0, 0)
        else:
            lax.fori_loop(0, count, one, 0)

    def begin(self, k, ws):
        t, c = self.target(k), self.place.c
        for w in ws:
            for s in range(X * Y):
                q = t * X * Y + s
                pltpu.make_async_copy(self.block(w, q * C + c), self.own[w].at[q], self.load.at[w, t]).start()
                self.copy(
                    self.block(w, q * C + 1 - c), self.from_core[w].at[q], self.score.at[w], self.rcore.at[w, t], self.place.cdev
                ).start()

    def core(self, k, ws):
        t, p = self.target(k), self.place
        span = pl.ds(t * X * Y, X * Y)
        for w in ws:
            mine = self.own[w].at[span]
            pltpu.make_async_copy(mine, mine, self.load.at[w, t]).wait()
            self.arrived(self.from_core[w].at[span], self.rcore.at[w, t])
            self.add(w, t * X * Y, X * Y, self.from_core[w], t * X * Y)
            if w not in self.plane_first:
                self.copy(
                    self.own[w].at[pl.ds((t * X + 1 - p.x) * Y, Y)], self.from_x[w].at[pl.ds(t * Y, Y)],
                    self.sx.at[w], self.rx.at[w, t], p.xdev,
                ).start()

    def across(self, k, ws):
        t, p = self.target(k), self.place
        for w in ws:
            self.arrived(self.from_x[w].at[pl.ds(t * Y, Y)], self.rx.at[w, t])
            self.add(w, (t * X + p.x) * Y, Y, self.from_x[w], t * Y)
            self.copy(
                self.own[w].at[(t * X + p.x) * Y + 1 - p.y], self.from_y[w].at[t], self.sy.at[w], self.ry.at[w, t], p.ydev
            ).start()

    def along(self, k, ws, first, count):
        t, z = self.target(k), self.place.z

        def span(w):
            return self.own[w].at[pl.ds(first(t), count)]

        def slot(w, s):
            return self.from_z[w].at[pl.ds(s * count, count)]

        def take(w, s, sem):
            self.arrived(slot(w, s), sem.at[w, t])
            self.add(w, first(t), count, self.from_z[w], s * count)

        if k < Z - 1:
            @pl.when(t > z)
            def _():
                for w in ws:
                    @pl.when(z > 0)
                    def _():
                        take(w, t, self.rl)

                    self.copy(span(w), slot(w, t), self.sr.at[w], self.rl.at[w, t], self.place.right).start()

            @pl.when(t < z)
            def _():
                there = t + (Z - t) * (t == z - 1).astype(jnp.int32)
                for w in ws:
                    @pl.when(z < Z - 1)
                    def _():
                        take(w, t, self.rr)

                    self.copy(span(w), slot(w, there), self.sl.at[w], self.rr.at[w, t], self.place.left).start()
        else:
            for w in ws:
                @pl.when(z > 0)
                def _():
                    take(w, t, self.rl)

                @pl.when(z < Z - 1)
                def _():
                    take(w, Z, self.rr)

    def down(self, k, ws):
        t, p = self.target(k), self.place
        for w in ws:
            self.arrived(self.from_y[w].at[t], self.ry.at[w, t])
            self.add(w, (t * X + p.x) * Y + p.y, 1, self.from_y[w], t)
        self.along(k, ws, lambda t: (t * X + p.x) * Y + p.y, 1)

    def plane(self, k, ws):
        p = self.place
        self.along(k, ws, lambda t: t * X * Y, X * Y)
        if k == Z - 1:
            for w in ws:
                for xx in range(X):
                    self.copy(
                        self.own[w].at[(p.z * X + xx) * Y + 1 - p.y], self.from_y[w].at[xx], self.sy.at[w], self.ry.at[w, xx], p.ydev
                    ).start()

    def plane_across(self, ws):
        p = self.place
        for w in ws:
            for xx in range(X):
                self.arrived(self.from_y[w].at[xx], self.ry.at[w, xx])
                self.add(w, (p.z * X + xx) * Y + p.y, 1, self.from_y[w], xx)
            self.copy(
                self.own[w].at[(p.z * X + 1 - p.x) * Y + p.y], self.from_x[w].at[0], self.sx.at[w], self.rx.at[w, 0], p.xdev
            ).start()

    def steps(self, rounds):
        def some(i, plane):
            k, ws = rounds[i]
            return k, [w for w in ws if (w in self.plane_first) == plane]

        def step(i):
            if i < len(rounds):
                self.core(*rounds[i])
                k, ws = some(i, True)
                self.plane(k, ws)
            if 0 <= i - 1 < len(rounds):
                k, ws = some(i - 1, True)
                if k == Z - 1:
                    self.plane_across(ws)
                self.across(*some(i - 1, False))
            if 0 <= i - 2 < len(rounds):
                self.down(*some(i - 2, False))

        return step

    def finish(self, outs):
        p = self.place
        at = (p.z * X + p.x) * Y + p.y
        for w, out in enumerate(outs):
            plane = w in self.plane_first
            total = self.own[w][at].astype(f32)
            if plane:
                self.arrived(self.from_x[w].at[0], self.rx.at[w, 0])
                total = total + self.from_x[w][0].astype(f32)
            out[...] = total

            def sent(count, sem):
                span = self.own[w].at[pl.ds(0, count)]
                pltpu.make_async_copy(span, span, sem.at[w]).wait()

            sent(Z * X * Y, self.score)
            sent(1 if plane else Z * Y, self.sx)
            sent(X if plane else Z, self.sy)
            per = X * Y if plane else 1
            for k in range(Z):
                @pl.when(p.z == k)
                def _():
                    if k > 0:
                        sent(per * k, self.sl)
                    if k < Z - 1:
                        sent(per * (Z - 1 - k), self.sr)


def backward_kernel(plane_first, rounds, plan, *refs):
    nw = 8
    refs = list(refs)

    def take(count):
        got = refs[:count]
        del refs[:count]
        return got

    norms, g_third = take(2)
    text, image, w_qkv, w_out, w_cq, w_kv, w_co = take(7)
    mixed, probs, ctx, n1, r1, memory, query, cprobs, cctx, n2, r2 = take(11)
    grad_after, g_in, g_outer = take(3)
    outs, (swapped, text_grad) = take(nw), take(2)
    g_qkv, g_out, g_cq, g_kv, g_co, image_grad = take(6)
    own, from_core, from_x, from_y, from_z = (take(nw) for _ in range(5))
    g_blocks, grad_self, g_second = take(3)
    sems = take(11)
    psend, precv, plocal, fetch, store = take(5)
    p = Place()
    me = p.me
    barrier = pltpu.get_barrier_semaphore()
    p.greet(barrier)
    scatter = Scatter(
        p, plane_first, [g_qkv, g_out, g_cq, g_kv, g_co, g_in, g_outer, g_blocks], own, from_core, from_x, from_y, from_z, sems
    )
    step = scatter.steps(rounds)
    here = swapped.shape[1] // (Y * C)
    place = swapped.at[:, pl.ds(pl.multiple_of(me * here, here), here)]
    peers = ((p.ydev, p.ypeer), (p.cdev, p.cpeer), (p.ddev, p.dpeer))

    def swap(k):
        return scatter.copy(image_grad.at[peers[k][1]], place, psend.at[k], precv.at[k], peers[k][0])

    def stay():
        return pltpu.make_async_copy(image_grad.at[me], place, plocal)

    def run(tokens):
        for token in tokens:
            if token == 200:
                for k in range(3):
                    swap(k).start()
                stay().start()
            elif token >= 100:
                scatter.begin(*rounds[token - 100])
            else:
                step(token)

    left = list(plan)

    def pause():
        run(left.pop(0))

    def copies(pairs, sem):
        made = [pltpu.make_async_copy(src, dst, sem.at[k]) for k, (src, dst) in enumerate(pairs)]
        for copy in made:
            copy.start()
        return made

    def done(made):
        for copy in made:
            copy.wait()

    p.met(barrier)

    def cross(flat):
        def attention(*scope):
            made = copies(list(zip((memory, query, cprobs, cctx, n2, r2, n1, grad_after, w_cq, w_co), scope)), fetch)
            pause()
            done(made)
            cross_backward(*scope[:10], norms, *scope[10:12], grad_self, g_second, flat, *scope[12:], scope[7], pause, 2)
            made = copies([(scope[10], g_cq), (scope[11], g_co)], store)
            pause()
            done(made)

        row = pltpu.VMEM(n1.shape, f32)
        pl.run_scoped(
            attention,
            *[pltpu.VMEM(r.shape, r.dtype) for r in (memory, query, cprobs, cctx, n2, r2, n1, grad_after, w_cq, w_co, g_cq, g_co)],
            row, row,
        )

        def weights(image_in, w_in, g_low, back, grad_mem):
            made = copies([(image, image_in), (w_kv, w_in)], fetch)
            pause()
            done(made)
            memory_backward(image_in, w_in, flat, g_low, back, grad_mem, pause, 1)
            made = copies([(g_low, g_kv)], store)
            count = image_grad.shape[1]

            def out(k, carry):
                rows = pl.ds(pl.multiple_of(k * here, here), here)
                pltpu.make_async_copy(back.at[rows], image_grad.at[k // count, k % count], store.at[1]).start()
                return carry

            lax.fori_loop(0, Y * C * count, out, 0)
            pause()
            done(made)
            pltpu.make_async_copy(back, back, store.at[1]).wait()

        pl.run_scoped(
            weights, pltpu.VMEM(image.shape, bf16), pltpu.VMEM(w_kv.shape, bf16), pltpu.VMEM(g_kv.shape, bf16),
            pltpu.VMEM(image.shape, bf16), pltpu.VMEM((image.shape[0], 2 * D), bf16),
        )

    pl.run_scoped(cross, pltpu.VMEM((2 * PAIRS, image.shape[0], PAIR), f32))

    def alone(*scope):
        made = copies(list(zip((text, mixed, probs, ctx, n1, r1, w_qkv, w_out), scope)), fetch)
        pause()
        done(made)
        text_in, mixed_in, probs_in, ctx_in, normed, inverse, w_mix, w_ctx, g_mix, g_ctx, back, *work = scope
        self_backward(
            text_in, mixed_in, probs_in, ctx_in, normed, inverse, grad_self, w_mix, w_ctx, norms, g_second, g_third,
            g_mix, g_ctx, back, g_blocks, *work, pause, 2, 1,
        )
        made = copies([(g_mix, g_qkv), (g_ctx, g_out), (back, text_grad)], store)
        pause()
        done(made)

    rows = text.shape[0]
    pl.run_scoped(
        alone, *[pltpu.VMEM(r.shape, r.dtype) for r in (text, mixed, probs, ctx, n1, r1, w_qkv, w_out, g_qkv, g_out, text_grad)],
        pltpu.VMEM((rows, 3 * D), f32), pltpu.VMEM((rows, D), f32), pltpu.VMEM((rows, 3 * D), f32), pltpu.VMEM((rows, 3 * D), bf16),
    )
    while left:
        pause()
    scatter.finish(outs)
    for k in range(3):
        swap(k).wait()
    stay().wait()


def backward_all(text, image, ws, norms, saved, grad_after, g_third, g_in, g_outer, slots,
                 plane_first=PLANE_LAST, rounds=ROUNDS, plan=BACK_PLAN, collective=1):
    nw = 8
    n = Z * X * Y * C
    every = Z * X * Y
    items = image.shape[0] // slots
    shapes = [w.shape for w in ws] + [g_in.shape, g_outer.shape, (n * 8, 128)]
    blocks = [(s[0] // n, s[1]) for s in shapes]
    kinds = [bf16] * (nw - 1) + [f32]
    anyspec = pl.BlockSpec(memory_space=pl.ANY)
    dma = pltpu.SemaphoreType.DMA
    shape = jax.ShapeDtypeStruct

    def room(line, plane):
        return [
            pltpu.VMEM((plane if w in plane_first else line,) + b, k) for w, (b, k) in enumerate(zip(blocks, kinds))
        ]

    out = pl.pallas_call(
        functools.partial(backward_kernel, plane_first, rounds, plan),
        out_shape=[shape(b, f32) for b in blocks]
        + [shape((slots // (Y * C), items * Y * C, ENC), bf16), shape(text.shape, f32)]
        + [shape(s, bf16) for s in shapes[:5]] + [shape((Y * C, slots // (Y * C), items, ENC), bf16)],
        in_specs=[VM] * 2 + [anyspec] * 21,
        out_specs=[VM] * nw + [anyspec] * 8,
        scratch_shapes=room(every, every) + room(every, every) + room(Z * Y, 1) + room(Z, X) + room(Z + 1, (Z + 1) * X * Y)
        + [pltpu.VMEM((n * 8, 128), f32), pltpu.VMEM(text.shape, f32), pltpu.VMEM((2, D), f32)]
        + [dma((nw, Z))] * 6 + [dma((nw,))] * 5 + [dma((3,)), dma((3,)), dma, dma((12,)), dma((4,))],
        compiler_params=pltpu.CompilerParams(collective_id=collective, has_side_effects=True, vmem_limit_bytes=60 << 20),
        name="backward",
    )(norms, g_third, text, image, *ws, *saved, grad_after, g_in, g_outer)
    return list(out[:nw]), out[nw], out[nw + 1]


step_rates = (0.05, 0.15, 0.05, 0.05, 0.3, 0.05, 0.05, 0.5)
step_decays = (0.01, 0.01, 0.01, 0.01, 0.01, 0.01, 0.01, 0.0)
BOTH = ("items", "patch")


def in_blocks(norms, count):
    width = D // count
    return jnp.pad(norms.reshape(6, count, width).transpose(1, 0, 2), ((0, 0), (0, 2), (0, 128 - width))).reshape(8 * count, 128)


def on_device(direct, text, cotangent, patches, text_lengths, patch_mask, *state):
    masters, firsts, seconds = state[:8], state[8:16], state[16:]
    group, local = patch_mask.shape
    chunks = lax.axis_size("patch")
    items = group // chunks
    devices = chunks * lax.axis_size("items")
    by_slot = patches.transpose(1, 0, 2)
    if direct:
        weights, image, norms, saved = forward_all(text, text_lengths, masters, by_slot, patch_mask, VALID)
    else:
        weights = [lax.all_gather(m.astype(bf16), BOTH, axis=0, tiled=True) for m in masters[:7]]
        blocks = in_blocks(lax.all_gather(masters[7].astype(bf16), BOTH, axis=1, tiled=True).astype(f32), devices)
        image = lax.all_to_all(by_slot.reshape(local, chunks, items, ENC), "patch", 1, 0)
        image = image.reshape(chunks * local * items, ENC)
        masks = patch_bias(patch_mask, lax.axis_index("patch") * local, VALID)
        masks = jnp.pad(masks, ((0, 0), (0, 128 - local))).reshape(chunks, items, 128)
        masks = lax.all_to_all(masks, "patch", 0, 0)
        norms, saved = forward_local(text, text_lengths, image, masks, weights, blocks)
    block_output, g_in, g_outer, grad_after, g_third = feed_forward_call(cotangent, weights[5:7], norms, saved[9])
    if direct:
        reduced, image_grad, text_grad = backward_all(
            text, image, weights[:5], norms, saved, grad_after, g_third, g_in, g_outer, chunks * local
        )
    else:
        text_grad, image_grad, grads, grad_blocks = backward_local(
            text, image, weights[:5], norms, saved, grad_after, g_third, devices
        )
        grads = (*grads, g_in, g_outer)
        reduced = [lax.psum_scatter(g, BOTH, scatter_dimension=0, tiled=True).astype(f32) for g in grads]
        reduced.append(lax.psum_scatter(grad_blocks, BOTH, scatter_dimension=0, tiled=True))
        image_grad = lax.all_to_all(image_grad.reshape(chunks, local, items, ENC), "patch", 0, 1)
        image_grad = image_grad.reshape(local, group, ENC)
    state_shapes = [(m.shape, f32) for m in masters]
    *updated, patch_grad = call(
        functools.partial(adamw, 8, step_decays, step_rates),
        (*masters, *firsts, *seconds, *reduced, image_grad),
        [*state_shapes * 3, (image_grad.shape, f32)], [], "adamw",
    )
    return (block_output, text_grad, patch_grad.transpose(1, 0, 2), *updated)


def solution(mesh):
    rows, cols = P(BOTH, None), P(None, BOTH)
    state = (*[rows] * 7, cols)
    direct = dict(mesh.shape) == {"items": Z * X, "patch": Y * C}
    return jax.shard_map(
        functools.partial(on_device, direct),
        mesh=mesh,
        in_specs=(rows, rows, P("items", "patch", None), P(BOTH), P("items", "patch"), *state * 3),
        out_specs=(rows, rows, P("items", "patch", None), *state * 3),
        check_vma=False,
    )
```

```python
import functools

import jax
import jax.numpy as jnp
from jax import lax
from jax.experimental import pallas as pl
from jax.experimental.pallas import tpu as pltpu
from jax.sharding import PartitionSpec as P

D = 768
HEADS = 12
HEAD_DIM = 64
ENC = 1024
TEXT = 40
VALID = 145
PAIR = 2 * HEAD_DIM
PAIRS = HEADS // 2
SCALE = HEAD_DIM ** (-0.5)
OUTSIDE = -1e30
bf16, f32 = jnp.bfloat16, jnp.float32


def dot(a, b):
    return jnp.dot(a, b, preferred_element_type=f32)


def dot_nt(a, b):
    return lax.dot_general(a, b, (((1,), (1,)), ((), ())), preferred_element_type=f32)


def dot_tn(a, b):
    return lax.dot_general(a, b, (((0,), (0,)), ((), ())), preferred_element_type=f32)


def quiet():
    pass


def chunks_of(count, parts, body, pause):
    def run(k, carry):
        body(k)
        return carry

    for part in range(parts):
        lax.fori_loop(count * part // parts, count * (part + 1) // parts, run, 0)
        if part < parts - 1:
            pause()


def tiles(total, step, body):
    def run(k, carry):
        body(pl.ds(pl.multiple_of(k * step, step), step))
        return carry

    lax.fori_loop(0, total // step, run, 0)


def norm_forward(values):
    center = values - jnp.mean(values, axis=-1, keepdims=True)
    inverse = lax.rsqrt(jnp.mean(center * center, axis=-1, keepdims=True) + 1e-12)
    return center * inverse, inverse


def norm_backward(grad_out, normed, inverse, gain):
    grad_gain = jnp.sum(grad_out * normed, axis=0, keepdims=True)
    grad_shift = jnp.sum(grad_out, axis=0, keepdims=True)
    scaled = grad_out * gain
    grad_values = inverse * (
        scaled
        - jnp.mean(scaled, axis=-1, keepdims=True)
        - normed * jnp.mean(scaled * normed, axis=-1, keepdims=True)
    )
    return grad_values, grad_gain, grad_shift


def low_half():
    return lax.broadcasted_iota(jnp.int32, (TEXT, PAIR), 1) < HEAD_DIM


def expand(rows):
    low = low_half()
    return jnp.concatenate(
        [jnp.where(low, rows, 0.0), jnp.where(low, 0.0, rows)], axis=0
    ).astype(bf16)


def fold(rows):
    return jnp.where(low_half(), rows[:TEXT], rows[TEXT:])


def softmax(scores):
    top = jnp.max(scores, axis=-1, keepdims=True)
    powers = jnp.exp(scores - top)
    return powers / jnp.sum(powers, axis=-1, keepdims=True)


def pair_cols(j, start=0):
    return slice(start + PAIR * j, start + PAIR * (j + 1))


def pair_rows(j):
    return slice(2 * TEXT * j, 2 * TEXT * (j + 1))


def attend_forward(query, keys, values, bias, probs, item, context, rows):
    js = range(PAIRS)
    scores = [dot_nt(expand(query(j)), keys(j)) * SCALE + bias for j in js]
    weights = [softmax(s) for s in scores]
    for j in js:
        probs[item, pair_rows(j), :] = weights[j]
    parts = [dot(weights[j].astype(bf16), values(j)) for j in js]
    for j in js:
        context[rows, pair_cols(j)] = fold(parts[j])


def attend_backward(query, keys, values, probs, item, grad_context, put_q, put_k, put_v):
    js = range(PAIRS)
    outer = [expand(grad_context(j)) for j in js]
    grads = [dot_nt(outer[j], values(j)) for j in js]
    inner = []
    for j in js:
        weights = probs[item, pair_rows(j), :]
        delta = jnp.sum(weights * grads[j], axis=-1, keepdims=True)
        inner.append((weights * (grads[j] - delta)).astype(bf16))
    for j in js:
        put_v(j, dot_tn(probs[item, pair_rows(j), :].astype(bf16), outer[j]))
    for j in js:
        put_q(j, fold(dot(inner[j], keys(j))) * SCALE)
    for j in js:
        put_k(j, dot_tn(inner[j], expand(query(j))) * SCALE)


def self_forward(lengths, text, w_qkv, w_out, blocks, mixed, probs, ctx, normed, inverse, norms, mix, context,
                 pause=quiet, parts=1):
    spread(blocks, norms)

    def project(cols):
        got = dot(text[...], w_qkv[:, cols]).astype(bf16)
        mixed[:, cols] = got
        mix[:, cols] = got.astype(f32)

    tiles(3 * D, 768, project)
    pause()
    position = lax.broadcasted_iota(jnp.int32, (1, TEXT), 1)

    def one(item):
        rows = pl.ds(pl.multiple_of(item * TEXT, 8), TEXT)
        bias = jnp.where(position < lengths[item], 0.0, -10000.0).astype(f32)
        attend_forward(
            lambda j: mix[rows, pair_cols(j)],
            lambda j: mix[rows, pair_cols(j, D)].astype(bf16),
            lambda j: mix[rows, pair_cols(j, 2 * D)].astype(bf16),
            bias, probs, item, context, rows,
        )

    chunks_of(probs.shape[0], parts, one, pause)
    pause()
    ctx[...] = context[...].astype(bf16)
    pre = text[...].astype(f32) + dot(ctx[...], w_out[...])
    n, r = norm_forward(pre)
    normed[...] = n
    inverse[...] = r


def self_backward(text, mixed, probs, ctx, normed, inverse, grad_after, w_qkv, w_out, norms, g_second, g_third,
                  g_qkv, g_out, text_grad, g_blocks, mix, grad_ctx, grad_mix, low_mix,
                  pause=quiet, parts=1, wide=1):
    grad_pre, grad_gain, grad_shift = norm_backward(grad_after[...], normed[...], inverse[...], norms[0:1, :])
    rows = jnp.concatenate([grad_gain, grad_shift, g_second[...], g_third[...], jnp.zeros((2, D), f32)], axis=0)
    count = g_blocks.shape[0] // 8
    width = D // count
    g_blocks[...] = jnp.zeros(g_blocks.shape, f32)
    for b in range(count):
        g_blocks[8 * b : 8 * b + 8, :width] = rows[:, width * b : width * (b + 1)]
    low = grad_pre.astype(bf16)
    g_out[...] = dot_tn(ctx[...], low).astype(bf16)
    grad_ctx[...] = dot_nt(low, w_out[...]).astype(bf16).astype(f32)
    text_grad[...] = grad_pre
    mix[...] = mixed[...].astype(f32)
    pause()

    def one(item):
        rows = pl.ds(pl.multiple_of(item * TEXT, 8), TEXT)

        def put(start):
            def store(j, value):
                grad_mix[rows, pair_cols(j, start)] = value
            return store

        attend_backward(
            lambda j: mix[rows, pair_cols(j)],
            lambda j: mix[rows, pair_cols(j, D)].astype(bf16),
            lambda j: mix[rows, pair_cols(j, 2 * D)].astype(bf16),
            probs, item, lambda j: grad_ctx[rows, pair_cols(j)],
            put(0), put(D), put(2 * D),
        )

    chunks_of(probs.shape[0], parts, one, pause)
    pause()
    low_mix[...] = grad_mix[...].astype(bf16)

    def weights(k):
        cols = pl.ds(pl.multiple_of(k * D, D), D)
        g_qkv[:, cols] = dot_tn(text[...], low_mix[:, cols]).astype(bf16)
        text_grad[...] += dot_nt(low_mix[:, cols], w_qkv[:, cols])

    chunks_of(3, wide, weights, pause)


def spread(blocks, norms):
    count = blocks.shape[0] // 8
    width = D // count
    for b in range(count):
        norms[:, width * b : width * (b + 1)] = blocks[8 * b : 8 * b + 8, :width]


def cross_forward(image, masks, w_kv, w_q, w_out, norms, normed_one,
                  memory, query, probs, ctx, normed, inverse, bias, context, wide, flat,
                  pause=quiet, tall=1, parts=1):
    items = masks.shape[1]
    slots = bias.shape[1]
    local = slots // masks.shape[0]
    for c in range(masks.shape[0]):
        bias[:, local * c : local * (c + 1)] = masks[c, :, :local]

    def project(k):
        got = dot(image[...], w_kv[:, pl.ds(pl.multiple_of(4 * PAIR * k, 4 * PAIR), 4 * PAIR)]).astype(bf16).astype(f32)
        for j in range(4):
            flat[4 * k + j] = got[:, pair_cols(j)]

    chunks_of(PAIRS // 2, tall, project, pause)
    pause()
    after = normed_one[...] * norms[0:1, :] + norms[1:2, :]
    low = dot(after.astype(bf16), w_q[...]).astype(bf16)
    query[...] = low
    wide[...] = low.astype(f32)

    def one(item):
        rows = pl.ds(pl.multiple_of(item * TEXT, 8), TEXT)
        every = pl.ds(item, slots, stride=items)
        for j in range(2 * PAIRS):
            memory[item, :, pair_cols(j)] = flat[j, every, :].astype(bf16)
        attend_forward(
            lambda j: wide[rows, pair_cols(j)],
            lambda j: memory[item, :, pair_cols(j)],
            lambda j: memory[item, :, pair_cols(j, D)],
            bias[pl.ds(item, 1), :], probs, item, context, rows,
        )

    chunks_of(items, parts, one, pause)
    pause()
    ctx[...] = context[...].astype(bf16)
    pre = after + dot(ctx[...], w_out[...])
    n, r = norm_forward(pre)
    normed[...] = n
    inverse[...] = r


def cross_backward(memory, query, probs, ctx, normed, inverse, normed_one, grad_after, w_q, w_out, norms,
                   g_q, g_out, grad_self, g_norm, flat, wide, grad_ctx, grad_q, pause=quiet, parts=1):
    items, slots = memory.shape[:2]
    grad_pre, grad_gain, grad_shift = norm_backward(grad_after[...], normed[...], inverse[...], norms[2:3, :])
    g_norm[0:1, :] = grad_gain
    g_norm[1:2, :] = grad_shift
    grad_self[...] = grad_pre
    low = grad_pre.astype(bf16)
    g_out[...] = dot_tn(ctx[...], low).astype(bf16)
    grad_ctx[...] = dot_nt(low, w_out[...]).astype(bf16).astype(f32)
    wide[...] = query[...].astype(f32)
    pause()

    def one(item):
        rows = pl.ds(pl.multiple_of(item * TEXT, 8), TEXT)
        every = pl.ds(item, slots, stride=items)

        def put_q(j, value):
            grad_q[rows, pair_cols(j)] = value

        def put(start):
            def store(j, value):
                flat[start + j, every, :] = value
            return store

        attend_backward(
            lambda j: wide[rows, pair_cols(j)],
            lambda j: memory[item, :, pair_cols(j)],
            lambda j: memory[item, :, pair_cols(j, D)],
            probs, item, lambda j: grad_ctx[rows, pair_cols(j)],
            put_q, put(0), put(PAIRS),
        )

    chunks_of(items, parts, one, pause)
    low_q = grad_q[...].astype(bf16)
    after = (normed_one[...] * norms[0:1, :] + norms[1:2, :]).astype(bf16)
    g_q[...] = dot_tn(after, low_q).astype(bf16)
    grad_self[...] += dot_nt(low_q, w_q[...])


def memory_backward(image, w_kv, flat, g_kv, image_grad, grad_mem, pause=quiet, wide=1):
    for j in range(2 * PAIRS):
        grad_mem[:, pair_cols(j)] = flat[j].astype(bf16)
    step = 4 * PAIR

    def weights(k):
        cols = pl.ds(pl.multiple_of(k * step, step), step)
        g_kv[:, cols] = dot_tn(image[...], grad_mem[:, cols]).astype(bf16)

    chunks_of(2 * D // step, wide, weights, pause)
    pause()

    def back(k):
        cols = pl.ds(pl.multiple_of(k * step, step), step)
        image_grad[:, cols] = dot_nt(grad_mem[...], w_kv[cols, :]).astype(bf16)

    chunks_of(ENC // step, 1, back, pause)


def feed_forward(normed_two, cotangent, w_inner, w_outer, norms,
                 block_output, g_inner, g_outer, grad_after, g_norm, low_in, hidden, slope, total, grad_low, grad_hid):
    after = normed_two[...] * norms[2:3, :] + norms[3:4, :]
    low_in[...] = after.astype(bf16)
    total[...] = after

    def up(cols):
        pre = dot(low_in[...], w_inner[:, cols])
        bell = 0.5 * (1.0 + lax.erf(pre * (0.5 ** 0.5)))
        low = (pre * bell).astype(bf16)
        hidden[:, cols] = low
        slope[:, cols] = bell + pre * jnp.exp(-0.5 * pre * pre) * 0.3989422804014327
        total[...] += dot(low, w_outer[cols, :])

    ff = w_inner.shape[1]
    tiles(ff, 768, up)
    n, r = norm_forward(total[...])
    gain = norms[4:5, :]
    block_output[...] = (n * gain + norms[5:6, :]).astype(bf16)
    grad_pre, grad_gain, grad_shift = norm_backward(cotangent[...].astype(f32), n, r, gain)
    g_norm[0:1, :] = grad_gain
    g_norm[1:2, :] = grad_shift
    grad_after[...] = grad_pre
    grad_low[...] = grad_pre.astype(bf16)

    def down(cols):
        low = (dot_nt(grad_low[...], w_outer[cols, :]) * slope[:, cols]).astype(bf16)
        g_inner[:, cols] = dot_tn(low_in[...], low).astype(bf16)
        g_outer[cols, :] = dot_tn(hidden[:, cols], grad_low[...]).astype(bf16)
        grad_after[...] += dot_nt(low, w_inner[:, cols])

    tiles(ff, 768, down)


VM = pl.BlockSpec(memory_space=pltpu.VMEM)


def call(body, args, outs, scratch, name, smem=0, limit=60 << 20):
    return pl.pallas_call(
        body,
        out_shape=[jax.ShapeDtypeStruct(s, k) for s, k in outs],
        in_specs=[pl.BlockSpec(memory_space=pltpu.SMEM)] * smem + [VM] * (len(args) - smem),
        out_specs=[VM] * len(outs),
        scratch_shapes=[pltpu.VMEM(s, k) for s, k in scratch],
        compiler_params=pltpu.CompilerParams(vmem_limit_bytes=limit),
        name=name,
    )(*args)


def adamw(count, decays, rates, *refs):
    masters, firsts, seconds, grads = (refs[count * i : count * (i + 1)] for i in range(4))
    image_low = refs[4 * count]
    new_m, new_f, new_s = (refs[4 * count + 1 + count * i : 4 * count + 1 + count * (i + 1)] for i in range(3))
    image_grad = refs[7 * count + 1]
    for k in range(count):
        rows, cols = masters[k].shape
        gradient = grads[k][:rows, :cols]
        first = 0.9 * firsts[k][...] + 0.1 * gradient
        second = 0.999 * seconds[k][...] + 0.001 * gradient * gradient
        step = first / (1.0 - 0.9**10) / (jnp.sqrt(second / (1.0 - 0.999**10)) + 1e-08)
        master = masters[k][...]
        new_m[k][...] = master - rates[k] * (step + decays[k] * master)
        new_f[k][...] = first
        new_s[k][...] = second
    image_grad[...] = image_low[...].astype(f32)


def forward_local(text, lengths, image, masks, ws, blocks):
    w_qkv, w_out, w_cq, w_kv, w_co = ws[:5]
    rows = text.shape[0]
    items = rows // TEXT
    slots = image.shape[0] // items
    pairs = HEADS * TEXT
    row = ((rows, D), f32)
    rowl = ((rows, D), bf16)
    one = ((rows, 1), f32)
    *first, norms = call(
        self_forward, (lengths, text, w_qkv, w_out, blocks),
        [((rows, 3 * D), bf16), ((items, pairs, TEXT), f32), rowl, row, one, ((8, D), f32)],
        [((rows, 3 * D), f32), row], "self_forward", smem=1)
    second = call(
        cross_forward, (image, masks, w_kv, w_cq, w_co, norms, first[3]),
        [((items, slots, 2 * D), bf16), rowl, ((items, pairs, slots), f32), rowl, row, one],
        [((items, slots), f32), row, row, ((2 * PAIRS, items * slots, PAIR), f32)], "cross_forward")
    return norms, [*first, *second]


def feed_forward_call(cotangent, ws, norms, n2):
    w_in, w_outer = ws
    rows, ff = n2.shape[0], w_in.shape[1]
    row = ((rows, D), f32)
    rowl = ((rows, D), bf16)
    return call(
        feed_forward, (n2, cotangent, w_in, w_outer, norms),
        [rowl, ((D, ff), bf16), ((ff, D), bf16), row, ((2, D), f32)],
        [rowl, ((rows, ff), bf16), ((rows, ff), f32), row, rowl, rowl], "feed_forward")


def backward_local(text, image, ws, norms, saved, grad_after, gn3, count):
    w_qkv, w_out, w_cq, w_kv, w_co = ws
    mixed, probs, ctx, n1, r1, memory, query, cprobs, cctx, n2, r2 = saved
    rows = text.shape[0]
    row = ((rows, D), f32)
    flat = (2 * PAIRS, image.shape[0], PAIR)
    g_cq, g_co, grad_self, gn2, flat_grad = call(
        cross_backward, (memory, query, cprobs, cctx, n2, r2, n1, grad_after, w_cq, w_co, norms),
        [((D, D), bf16), ((D, D), bf16), row, ((2, D), f32), (flat, f32)], [row, row, row], "cross_backward")
    g_kv, image_grad = call(
        memory_backward, (image, w_kv, flat_grad), [((ENC, 2 * D), bf16), (image.shape, bf16)],
        [((image.shape[0], 2 * D), bf16)], "memory_backward")
    g_qkv, g_out, text_grad, g_blocks = call(
        self_backward, (text, mixed, probs, ctx, n1, r1, grad_self, w_qkv, w_out, norms, gn2, gn3),
        [((D, 3 * D), bf16), ((D, D), bf16), row, ((count * 8, 128), f32)],
        [((rows, 3 * D), f32), row, ((rows, 3 * D), f32), ((rows, 3 * D), bf16)], "self_backward")
    return text_grad, image_grad, (g_qkv, g_out, g_cq, g_kv, g_co), g_blocks


MESH = pl.DeviceIdType.MESH
Z, X, Y, C = 4, 2, 2, 2
PLANE_FIRST, TURNED = (0,), (6,)
SETS = ((0, 1, 7, 3, 2, 4), (5, 6))
PLAN = (
    ("0", "00", "01", "1", "02", "swap", "03", "10", "04", "11", "05", "06", "swapped"),
    (("12",),),
    (),
    (("13",), (), ("14",), ("15",)),
    ("16",),
)
PLANE_LAST, TURNED_BACK = (3,), (6,)
ROUNDS = tuple((k, ws) for ws in ((6, 5), (3, 2, 4), (0, 1, 7)) for k in range(4))
BACK_PLAN = (
    ("b0", "b1", "c0", "b2"),
    ("c1", "b3"),
    ("c2", "a0"),
    ("c3", "a1"),
    ("a2",),
    ("d0", "a3"),
    ("d1",),
    ("b4", "b5", "s", "d2"),
    ("c4", "e4", "b6"),
    ("c5", "e5", "a4", "b7"),
    ("c6", "e6", "a5", "d3"),
    ("c7", "a6", "m4"),
    ("b8", "b9", "c8", "b10", "c9", "b11", "a7", "a8", "c10", "d4", "m5", "d5", "a9", "c11", "m6", "d6", "d8", "a10", "p7", "d7", "d9", "a11", "q7", "d10", "d11"),
)
bf16, f32 = jnp.bfloat16, jnp.float32


class Place:
    def __init__(self):
        item, self.me = lax.axis_index("items"), lax.axis_index("patch")
        self.z, self.x, self.y, self.c = item // X, item % X, self.me // C, self.me % C
        z, x, y, c = self.z, self.x, self.y, self.c
        self.left = (item - X, self.me)
        self.right = (item + X, self.me)
        self.xdev = (z * X + (1 - x), self.me)
        self.ypeer, self.cpeer, self.dpeer = (1 - y) * C + c, y * C + (1 - c), (1 - y) * C + (1 - c)
        self.ydev, self.cdev, self.ddev = (item, self.ypeer), (item, self.cpeer), (item, self.dpeer)

    def at(self, zz, xx, yy, cc):
        return ((zz * X + xx) * Y + yy) * C + cc

    def greet(self, barrier):
        for dev in (self.xdev, self.ydev, self.cdev, self.ddev):
            pl.semaphore_signal(barrier, inc=1, device_id=dev, device_id_type=MESH)

        @pl.when(self.z > 0)
        def _():
            pl.semaphore_signal(barrier, inc=1, device_id=self.left, device_id_type=MESH)

        @pl.when(self.z < Z - 1)
        def _():
            pl.semaphore_signal(barrier, inc=1, device_id=self.right, device_id_type=MESH)

    def met(self, barrier):
        pl.semaphore_wait(barrier, 4 + (self.z > 0).astype(jnp.int32) + (self.z < Z - 1).astype(jnp.int32))

    def both(self, d, step):
        if d == 0:
            step(self.z, None)
            return

        @pl.when(self.z >= d)
        def _():
            step(self.z - d, True)

        @pl.when(self.z + d < Z)
        def _():
            step(self.z + d, False)


def patch_bias(mask, first, valid):
    index = first + lax.broadcasted_iota(jnp.int32, mask.shape, 1)
    return jnp.where((mask > 0) & (index < valid), 0.0, -10000.0).astype(f32)


class Gather:
    def __init__(self, place, plane_first, turned, low, outs, recv, to_x, to_y, to_c, to_l, to_r, local):
        self.place, self.plane_first, self.turned = place, plane_first, turned
        self.low, self.outs, self.recv, self.local = low, outs, recv, local
        self.sems = {"x": to_x, "y": to_y, "c": to_c, "l": to_l, "r": to_r}
        self.devs = {"x": place.xdev, "y": place.ydev, "c": place.cdev, "l": place.left, "r": place.right}
        self.mine = place.at(place.z, place.x, place.y, place.c)

    def blocks(self, w, first, count=1):
        rows = self.low[w].shape[0]
        return self.outs[w].at[pl.ds(pl.multiple_of(first * rows, rows), count * rows)]

    def copy(self, w, block, way, own=False):
        return pltpu.make_async_remote_copy(
            src_ref=self.low[w] if own else self.blocks(w, block),
            dst_ref=self.blocks(w, block),
            send_sem=self.sems[way].at[w],
            recv_sem=self.recv.at[w, block],
            device_id=self.devs[way],
            device_id_type=MESH,
        )

    def send(self, w, block, ways, own=False):
        z = self.place.z
        for way in ways:
            if way == "l":
                @pl.when(z > 0)
                def _():
                    self.copy(w, block, "l", own).start()
            elif way == "r":
                @pl.when(z < Z - 1)
                def _():
                    self.copy(w, block, "r", own).start()
            else:
                self.copy(w, block, way, own).start()

    def arrived(self, w, block):
        self.copy(w, block, "x").wait_recv()

    def pass_on(self, w, block, ways):
        self.arrived(w, block)
        self.send(w, block, ways)

    def keep(self, w):
        return pltpu.make_async_copy(self.low[w], self.blocks(w, self.mine), self.local.at[w])

    def start(self, ws):
        for w in ws:
            self.send(w, self.mine, "xylr" if w in self.plane_first else "lryx", True)
        for w in ws:
            self.send(w, self.mine, "c", True)
            self.keep(w).start()

    def stages(self, ws):
        p = self.place
        x, y, c = p.x, p.y, p.c
        line = [w for w in ws if w not in self.plane_first]
        plane = [w for w in ws if w in self.plane_first]

        def plane_x():
            for w in plane:
                self.pass_on(w, p.at(p.z, 1 - x, y, c), "ylrc")

        def plane_y():
            for xx in (x, 1 - x):
                for w in plane:
                    self.pass_on(w, p.at(p.z, xx, 1 - y, c), "lrc")

        def plane_z(zz, from_left):
            for xx, yy in ((x, y), (1 - x, y), (x, 1 - y), (1 - x, 1 - y)):
                for w in plane:
                    self.pass_on(w, p.at(zz, xx, yy, c), "rc" if from_left else "lc")

        def line_z(zz, from_left):
            for w in line:
                self.pass_on(w, p.at(zz, x, y, c), "ryxc" if from_left else "lyxc")

        def line_y(zz, _):
            for w in line:
                if w in self.turned:
                    self.pass_on(w, p.at(zz, 1 - x, y, c), "yc")
                else:
                    self.pass_on(w, p.at(zz, x, 1 - y, c), "xc")

        def line_x(zz, _):
            for near in (True, False):
                for w in line:
                    if w in self.turned:
                        self.pass_on(w, p.at(zz, x if near else 1 - x, 1 - y, c), "c")
                    else:
                        self.pass_on(w, p.at(zz, 1 - x, y if near else 1 - y, c), "c")

        def from_core():
            for zz in range(Z):
                for xx in range(X):
                    for yy in range(Y):
                        for w in ws:
                            self.arrived(w, p.at(zz, xx, yy, 1 - c))
            for w in ws:
                self.keep(w).wait()

        def steps(*pairs):
            def run():
                for d, step in pairs:
                    if d is None:
                        step()
                    else:
                        p.both(d, step)
            return run

        first = [(None, plane_x)] if plane else []
        second = [(None, plane_y)] if plane else []

        def deep(d):
            return [(d, plane_z)] if plane else []

        if not line:
            return [steps(*first), steps(*second), steps(*deep(1)), steps(*deep(2)), steps(*deep(3)), quiet, from_core]
        return [
            steps(*first, (1, line_z)),
            steps(*second, (0, line_y)),
            steps(*deep(1), (2, line_z), (1, line_y), (0, line_x)),
            steps(*deep(2), (3, line_z), (2, line_y), (1, line_x)),
            steps(*deep(3), (3, line_y), (2, line_x)),
            steps((3, line_x)),
            from_core,
        ]

    def finish(self):
        z = self.place.z
        for w in range(len(self.low)):
            def sent(count, way):
                span = self.blocks(w, 0, count)
                pltpu.make_async_copy(span, span, self.sems[way].at[w]).wait()

            plane = w in self.plane_first
            wide = X * Y if plane else 1
            turned = w in self.turned
            sent(1 if plane else Z if turned else Z * Y, "x")
            sent(X if plane else Z * X if turned else Z, "y")
            sent(Z * X * Y, "c")
            for k in range(Z):
                @pl.when(z == k)
                def _():
                    if k > 0:
                        sent(wide * (Z - k), "l")
                    if k < Z - 1:
                        sent(wide * (k + 1), "r")


def forward_kernel(plane_first, turned, sets, plan, valid, *refs):
    nw = 8
    refs = list(refs)

    def take(count):
        got = refs[:count]
        del refs[:count]
        return got

    (lengths,), shards, (image, mask, text) = take(1), take(nw), take(3)
    whole, (image_out, norms) = take(nw - 1), take(2)
    saved = take(11)
    low, (blocks, masks, bias_here) = take(nw), take(3)
    w_qkv, w_out, w_cq, w_kv, w_co = take(5)
    image_in, mix, context, bias, wide, flat = take(6)
    kept = take(11)
    recv, to_x, to_y, to_c, to_l, to_r, local, psend, precv, plocal, load, save = take(12)
    p = Place()
    me = p.me
    barrier = pltpu.get_barrier_semaphore()
    p.greet(barrier)
    for w in range(nw - 1):
        low[w][...] = shards[w][...].astype(low[w].dtype)
    low[nw - 1][...] = jnp.zeros(low[nw - 1].shape, f32)
    rows, cols = shards[nw - 1].shape
    low[nw - 1][:rows, :cols] = shards[nw - 1][...].astype(bf16).astype(f32)
    slots = mask.shape[1]
    bias_here[...] = jnp.zeros(bias_here.shape, f32)
    bias_here[:, :slots] = patch_bias(mask[...], me * slots, valid)
    here = mask.shape[0] // (Y * C)
    peers = ((p.ydev, p.ypeer), (p.cdev, p.cpeer), (p.ddev, p.dpeer))
    swaps = (image_out, masks)

    def part(s, peer):
        rows = pl.ds(pl.multiple_of(peer * here, here), here)
        return bias_here.at[rows] if s else image.at[:, rows]

    def swap(s, k):
        dev, peer = peers[k]
        return pltpu.make_async_remote_copy(
            src_ref=part(s, peer),
            dst_ref=swaps[s].at[me],
            send_sem=psend.at[s, k],
            recv_sem=precv.at[s, k],
            device_id=dev,
            device_id_type=MESH,
        )

    def stay(s):
        return pltpu.make_async_copy(part(s, me), swaps[s].at[me], plocal.at[s])

    gather = Gather(p, plane_first, turned, low, [*whole, blocks], recv, to_x, to_y, to_c, to_l, to_r, local)
    staged = [gather.stages(ws) for ws in sets]
    p.met(barrier)

    def start_swaps():
        for s in range(2):
            for k in range(3):
                swap(s, k).start()
            stay(s).start()

    def end_swaps():
        for s in range(2):
            for k in range(3):
                swap(s, k).wait()
            stay(s).wait()

    def loads(pairs):
        return [pltpu.make_async_copy(src, dst, load.at[k]) for k, src, dst in pairs]

    early = loads([(0, whole[0], w_qkv), (1, whole[1], w_out)])
    late = loads([(2, whole[2], w_cq), (3, whole[3], w_kv), (4, whole[4], w_co)])

    def flatten(k, carry):
        rows = pl.ds(pl.multiple_of(k * here, here), here)
        pltpu.make_async_copy(image_out.at[k // slots, k % slots], image_in.at[rows], load.at[5]).start()
        return carry
    saves = [pltpu.make_async_copy(src, dst, save.at[k]) for k, (src, dst) in enumerate(zip(kept, saved))]

    def run(tokens):
        for token in tokens:
            if token == "swap":
                start_swaps()
            elif token == "swapped":
                end_swaps()
            elif len(token) == 1:
                gather.start(sets[int(token)])
            else:
                staged[int(token[0])][int(token[1])]()

    def queue(events):
        left = list(events)

        def pause():
            if left:
                run(left.pop(0))

        return pause

    before, during_self, between, during_cross, after = plan
    run(before)
    for copy in early:
        copy.start()
    for copy in early:
        copy.wait()
    mixed, probs, ctx, normed, inverse, memory, query, cross_probs, cross_ctx, normed_two, inverse_two = kept
    self_forward(
        lengths, text, w_qkv, w_out, blocks, mixed, probs, ctx, normed, inverse, norms, mix, context,
        queue(during_self), 2,
    )
    for copy in saves[:5]:
        copy.start()
    run(between)
    for copy in late:
        copy.start()
    lax.fori_loop(0, Y * C * slots, flatten, 0)
    for copy in late:
        copy.wait()
    pltpu.make_async_copy(image_in, image_in, load.at[5]).wait()
    cross_forward(
        image_in, masks, w_kv, w_cq, w_co, norms, normed,
        memory, query, cross_probs, cross_ctx, normed_two, inverse_two, bias, context, wide, flat,
        queue(during_cross), 2, 4,
    )
    for copy in saves[5:]:
        copy.start()
    run(after)
    gather.finish()
    for copy in saves:
        copy.wait()


def forward_all(text, lengths, shards, image, mask, valid, plane_first=PLANE_FIRST, turned=TURNED, sets=SETS, plan=PLAN, collective=0):
    nw = len(shards)
    n = Z * X * Y * C
    shapes = [s.shape for s in shards[:-1]] + [(8, 128)]
    kinds = [bf16] * (nw - 1) + [f32]
    slots, group, width = image.shape
    items = group // (Y * C)
    rows = text.shape[0]
    every = slots * Y * C
    pairs = HEADS * TEXT
    row, low_row, one = ((rows, D), f32), ((rows, D), bf16), ((rows, 1), f32)
    keep = [
        ((rows, 3 * D), bf16), ((items, pairs, TEXT), f32), low_row, row, one,
        ((items, every, 2 * D), bf16), low_row, ((items, pairs, every), f32), low_row, row, one,
    ]
    anyspec = pl.BlockSpec(memory_space=pl.ANY)
    dma = pltpu.SemaphoreType.DMA
    shape = jax.ShapeDtypeStruct
    out = pl.pallas_call(
        functools.partial(forward_kernel, plane_first, turned, sets, plan, valid),
        out_shape=[shape((n * s[0], s[1]), bf16) for s in shapes[:-1]]
        + [shape((Y * C, slots, items, width), image.dtype), shape((8, D), f32)]
        + [shape(*k) for k in keep],
        in_specs=[pl.BlockSpec(memory_space=pltpu.SMEM)] + [VM] * nw + [anyspec, VM, VM],
        out_specs=[anyspec] * nw + [VM] + [anyspec] * len(keep),
        scratch_shapes=[pltpu.VMEM(s, k) for s, k in zip(shapes, kinds)]
        + [pltpu.VMEM((n * 8, 128), f32), pltpu.VMEM((Y * C, items, 128), f32), pltpu.VMEM((group, 128), f32)]
        + [pltpu.VMEM((n * shapes[w][0], shapes[w][1]), bf16) for w in range(5)]
        + [pltpu.VMEM(s, k) for s, k in (
            ((every * items, width), bf16), ((rows, 3 * D), f32), row, ((items, every), f32), row,
            ((2 * PAIRS, items * every, PAIR), f32), *keep)]
        + [dma((nw, n))] + [dma((nw,))] * 6 + [dma((2, 3)), dma((2, 3)), dma((2,)), dma((6,)), dma((len(keep),))],
        compiler_params=pltpu.CompilerParams(collective_id=collective, has_side_effects=True, vmem_limit_bytes=60 << 20),
        name="forward",
    )(lengths, *shards, image, mask, text)
    return out[: nw - 1], out[nw - 1].reshape(every * items, width), out[nw], out[nw + 1 :]


class Scatter:
    def __init__(self, place, plane_first, turned, grads, own, from_core, from_x, from_y, from_z, sems):
        self.place, self.plane_first, self.turned, self.grads, self.own = place, plane_first, turned, grads, own
        self.from_core, self.from_x, self.from_y, self.from_z = from_core, from_x, from_y, from_z
        self.load, self.rcore, self.rx, self.ry, self.rl, self.rr, self.score, self.sx, self.sy, self.sl, self.sr = sems

    def target(self, k):
        half = self.place.z // 2
        near = self.place.z * (1 - half) + (Z - 1 - self.place.z) * half
        return half * (Z - 1) + (1 - 2 * half) * (Z - 1, 2 - 2 * near, 1 + near, near)[k]

    def copy(self, src, dst, send_sem, recv_sem, dev):
        return pltpu.make_async_remote_copy(
            src_ref=src, dst_ref=dst, send_sem=send_sem, recv_sem=recv_sem, device_id=dev, device_id_type=MESH
        )

    def arrived(self, dst, sem):
        self.copy(dst, dst, self.score.at[0], sem, self.place.cdev).wait_recv()

    def block(self, w, b):
        rows = self.own[w].shape[1]
        return self.grads[w].at[pl.ds(pl.multiple_of(b * rows, rows), rows)]

    def add(self, w, at, count, ref, start):
        mine = self.own[w]

        def one(i, carry):
            mine[at + i] = (mine[at + i].astype(f32) + ref[start + i].astype(f32)).astype(mine.dtype)
            return carry

        if count == 1:
            one(0, 0)
        else:
            lax.fori_loop(0, count, one, 0)

    def begin(self, k, ws):
        t, c = self.target(k), self.place.c
        for w in ws:
            for s in range(X * Y):
                q = t * X * Y + s
                pltpu.make_async_copy(self.block(w, q * C + c), self.own[w].at[q], self.load.at[w, t]).start()
                self.copy(
                    self.block(w, q * C + 1 - c), self.from_core[w].at[q], self.score.at[w], self.rcore.at[w, t], self.place.cdev
                ).start()

    def core(self, k, ws):
        t, p = self.target(k), self.place
        span = pl.ds(t * X * Y, X * Y)
        for w in ws:
            mine = self.own[w].at[span]
            pltpu.make_async_copy(mine, mine, self.load.at[w, t]).wait()
            self.arrived(self.from_core[w].at[span], self.rcore.at[w, t])
            self.add(w, t * X * Y, X * Y, self.from_core[w], t * X * Y)
            if w in self.turned:
                for xx in range(X):
                    self.copy(
                        self.own[w].at[(t * X + xx) * Y + 1 - p.y], self.from_y[w].at[t * X + xx],
                        self.sy.at[w], self.ry.at[w, t], p.ydev,
                    ).start()
            elif w not in self.plane_first:
                self.copy(
                    self.own[w].at[pl.ds((t * X + 1 - p.x) * Y, Y)], self.from_x[w].at[pl.ds(t * Y, Y)],
                    self.sx.at[w], self.rx.at[w, t], p.xdev,
                ).start()

    def across(self, k, ws):
        t, p = self.target(k), self.place
        for w in ws:
            if w in self.turned:
                self.arrived(self.from_y[w].at[pl.ds(t * X, X)], self.ry.at[w, t])
                for xx in range(X):
                    self.add(w, (t * X + xx) * Y + p.y, 1, self.from_y[w], t * X + xx)
                self.copy(
                    self.own[w].at[(t * X + 1 - p.x) * Y + p.y], self.from_x[w].at[t], self.sx.at[w], self.rx.at[w, t], p.xdev
                ).start()
                continue
            self.arrived(self.from_x[w].at[pl.ds(t * Y, Y)], self.rx.at[w, t])
            self.add(w, (t * X + p.x) * Y, Y, self.from_x[w], t * Y)
            self.copy(
                self.own[w].at[(t * X + p.x) * Y + 1 - p.y], self.from_y[w].at[t], self.sy.at[w], self.ry.at[w, t], p.ydev
            ).start()

    def along(self, k, ws, first, count):
        t, z = self.target(k), self.place.z

        def span(w):
            return self.own[w].at[pl.ds(first(t), count)]

        def slot(w, s):
            return self.from_z[w].at[pl.ds(s * count, count)]

        def take(w, s, sem):
            self.arrived(slot(w, s), sem.at[w, t])
            self.add(w, first(t), count, self.from_z[w], s * count)

        if k < Z - 1:
            @pl.when(t > z)
            def _():
                for w in ws:
                    @pl.when(z > 0)
                    def _():
                        take(w, t, self.rl)

                    self.copy(span(w), slot(w, t), self.sr.at[w], self.rl.at[w, t], self.place.right).start()

            @pl.when(t < z)
            def _():
                there = t + (Z - t) * (t == z - 1).astype(jnp.int32)
                for w in ws:
                    @pl.when(z < Z - 1)
                    def _():
                        take(w, t, self.rr)

                    self.copy(span(w), slot(w, there), self.sl.at[w], self.rr.at[w, t], self.place.left).start()
        else:
            for w in ws:
                @pl.when(z > 0)
                def _():
                    take(w, t, self.rl)

                @pl.when(z < Z - 1)
                def _():
                    take(w, Z, self.rr)

    def down(self, k, ws):
        t, p = self.target(k), self.place
        for w in ws:
            ref, sem = (self.from_x, self.rx) if w in self.turned else (self.from_y, self.ry)
            self.arrived(ref[w].at[t], sem.at[w, t])
            self.add(w, (t * X + p.x) * Y + p.y, 1, ref[w], t)
        self.along(k, ws, lambda t: (t * X + p.x) * Y + p.y, 1)

    def plane(self, k, ws):
        p = self.place
        self.along(k, ws, lambda t: t * X * Y, X * Y)
        if k == Z - 1:
            for w in ws:
                for xx in range(X):
                    self.copy(
                        self.own[w].at[(p.z * X + xx) * Y + 1 - p.y], self.from_y[w].at[xx], self.sy.at[w], self.ry.at[w, xx], p.ydev
                    ).start()

    def plane_across(self, ws):
        p = self.place
        for w in ws:
            for xx in range(X):
                self.arrived(self.from_y[w].at[xx], self.ry.at[w, xx])
                self.add(w, (p.z * X + xx) * Y + p.y, 1, self.from_y[w], xx)
            self.copy(
                self.own[w].at[(p.z * X + 1 - p.x) * Y + p.y], self.from_x[w].at[0], self.sx.at[w], self.rx.at[w, 0], p.xdev
            ).start()

    def act(self, name, k, ws):
        line = [w for w in ws if w not in self.plane_first]
        plane = [w for w in ws if w in self.plane_first]
        z = self.place.z
        if name == "b":
            self.begin(k, ws)
        elif name == "c":
            self.core(k, ws)
        elif name == "a":
            self.across(k, line)
        elif name == "d":
            self.down(k, line)
        elif name == "e":
            @pl.when((z == 0) | (z == Z - 1))
            def _():
                self.plane(k, plane)
        elif name == "m":
            @pl.when((z > 0) & (z < Z - 1))
            def _():
                self.plane(k, plane)
        elif name == "p":
            self.plane(k, plane)
        elif name == "q":
            self.plane_across(plane)

    def finish(self, outs):
        p = self.place
        at = (p.z * X + p.x) * Y + p.y
        for w, out in enumerate(outs):
            plane = w in self.plane_first
            total = self.own[w][at].astype(f32)
            if plane:
                self.arrived(self.from_x[w].at[0], self.rx.at[w, 0])
                total = total + self.from_x[w][0].astype(f32)
            out[...] = total

            def sent(count, sem):
                span = self.own[w].at[pl.ds(0, count)]
                pltpu.make_async_copy(span, span, sem.at[w]).wait()

            sent(Z * X * Y, self.score)
            turned = w in self.turned
            sent(1 if plane else Z if turned else Z * Y, self.sx)
            sent(X if plane else Z * X if turned else Z, self.sy)
            per = X * Y if plane else 1
            for k in range(Z):
                @pl.when(p.z == k)
                def _():
                    if k > 0:
                        sent(per * k, self.sl)
                    if k < Z - 1:
                        sent(per * (Z - 1 - k), self.sr)


def backward_kernel(plane_first, turned, rounds, plan, *refs):
    nw = 8
    refs = list(refs)

    def take(count):
        got = refs[:count]
        del refs[:count]
        return got

    norms, g_third = take(2)
    text, image, w_qkv, w_out, w_cq, w_kv, w_co = take(7)
    mixed, probs, ctx, n1, r1, memory, query, cprobs, cctx, n2, r2 = take(11)
    grad_after, g_in, g_outer = take(3)
    outs, (swapped, text_grad) = take(nw), take(2)
    g_qkv, g_out, g_cq, g_kv, g_co, image_grad = take(6)
    own, from_core, from_x, from_y, from_z = (take(nw) for _ in range(5))
    g_blocks, grad_self, g_second = take(3)
    sems = take(11)
    psend, precv, plocal, fetch, store = take(5)
    p = Place()
    me = p.me
    barrier = pltpu.get_barrier_semaphore()
    p.greet(barrier)
    scatter = Scatter(
        p, plane_first, turned, [g_qkv, g_out, g_cq, g_kv, g_co, g_in, g_outer, g_blocks], own, from_core, from_x, from_y, from_z, sems
    )
    here = swapped.shape[1] // (Y * C)
    place = swapped.at[:, pl.ds(pl.multiple_of(me * here, here), here)]
    peers = ((p.ydev, p.ypeer), (p.cdev, p.cpeer), (p.ddev, p.dpeer))

    def swap(k):
        return scatter.copy(image_grad.at[peers[k][1]], place, psend.at[k], precv.at[k], peers[k][0])

    def stay():
        return pltpu.make_async_copy(image_grad.at[me], place, plocal)

    def run(tokens):
        for token in tokens:
            if token == "s":
                for k in range(3):
                    swap(k).start()
                stay().start()
            else:
                scatter.act(token[0], *rounds[int(token[1:])])

    left = list(plan)

    def pause():
        run(left.pop(0))

    def copies(pairs, sem):
        made = [pltpu.make_async_copy(src, dst, sem.at[k]) for k, (src, dst) in enumerate(pairs)]
        for copy in made:
            copy.start()
        return made

    def done(made):
        for copy in made:
            copy.wait()

    p.met(barrier)

    def cross(flat):
        def attention(*scope):
            made = copies(list(zip((memory, query, cprobs, cctx, n2, r2, n1, grad_after, w_cq, w_co), scope)), fetch)
            pause()
            done(made)
            cross_backward(*scope[:10], norms, *scope[10:12], grad_self, g_second, flat, *scope[12:], scope[7], pause, 2)
            made = copies([(scope[10], g_cq), (scope[11], g_co)], store)
            pause()
            done(made)

        row = pltpu.VMEM(n1.shape, f32)
        pl.run_scoped(
            attention,
            *[pltpu.VMEM(r.shape, r.dtype) for r in (memory, query, cprobs, cctx, n2, r2, n1, grad_after, w_cq, w_co, g_cq, g_co)],
            row, row,
        )

        def weights(image_in, w_in, g_low, back, grad_mem):
            made = copies([(image, image_in), (w_kv, w_in)], fetch)
            pause()
            done(made)
            memory_backward(image_in, w_in, flat, g_low, back, grad_mem, pause, 1)
            made = copies([(g_low, g_kv)], store)
            count = image_grad.shape[1]

            def out(k, carry):
                rows = pl.ds(pl.multiple_of(k * here, here), here)
                pltpu.make_async_copy(back.at[rows], image_grad.at[k // count, k % count], store.at[1]).start()
                return carry

            lax.fori_loop(0, Y * C * count, out, 0)
            pause()
            done(made)
            pltpu.make_async_copy(back, back, store.at[1]).wait()

        pl.run_scoped(
            weights, pltpu.VMEM(image.shape, bf16), pltpu.VMEM(w_kv.shape, bf16), pltpu.VMEM(g_kv.shape, bf16),
            pltpu.VMEM(image.shape, bf16), pltpu.VMEM((image.shape[0], 2 * D), bf16),
        )

    pl.run_scoped(cross, pltpu.VMEM((2 * PAIRS, image.shape[0], PAIR), f32))

    def alone(*scope):
        made = copies(list(zip((text, mixed, probs, ctx, n1, r1, w_qkv, w_out), scope)), fetch)
        pause()
        done(made)
        text_in, mixed_in, probs_in, ctx_in, normed, inverse, w_mix, w_ctx, g_mix, g_ctx, back, *work = scope
        self_backward(
            text_in, mixed_in, probs_in, ctx_in, normed, inverse, grad_self, w_mix, w_ctx, norms, g_second, g_third,
            g_mix, g_ctx, back, g_blocks, *work, pause, 2, 1,
        )
        made = copies([(g_mix, g_qkv), (g_ctx, g_out), (back, text_grad)], store)
        pause()
        done(made)

    rows = text.shape[0]
    pl.run_scoped(
        alone, *[pltpu.VMEM(r.shape, r.dtype) for r in (text, mixed, probs, ctx, n1, r1, w_qkv, w_out, g_qkv, g_out, text_grad)],
        pltpu.VMEM((rows, 3 * D), f32), pltpu.VMEM((rows, D), f32), pltpu.VMEM((rows, 3 * D), f32), pltpu.VMEM((rows, 3 * D), bf16),
    )
    while left:
        pause()
    scatter.finish(outs)
    for k in range(3):
        swap(k).wait()
    stay().wait()


def backward_all(text, image, ws, norms, saved, grad_after, g_third, g_in, g_outer, slots,
                 plane_first=PLANE_LAST, turned=TURNED_BACK, rounds=ROUNDS, plan=BACK_PLAN, collective=1):
    nw = 8
    n = Z * X * Y * C
    every = Z * X * Y
    items = image.shape[0] // slots
    shapes = [w.shape for w in ws] + [g_in.shape, g_outer.shape, (n * 8, 128)]
    blocks = [(s[0] // n, s[1]) for s in shapes]
    kinds = [bf16] * (nw - 1) + [f32]
    anyspec = pl.BlockSpec(memory_space=pl.ANY)
    dma = pltpu.SemaphoreType.DMA
    shape = jax.ShapeDtypeStruct

    def room(line, plane, other=None):
        return [
            pltpu.VMEM((plane if w in plane_first else other or line if w in turned else line,) + b, k)
            for w, (b, k) in enumerate(zip(blocks, kinds))
        ]

    out = pl.pallas_call(
        functools.partial(backward_kernel, plane_first, turned, rounds, plan),
        out_shape=[shape(b, f32) for b in blocks]
        + [shape((slots // (Y * C), items * Y * C, ENC), bf16), shape(text.shape, f32)]
        + [shape(s, bf16) for s in shapes[:5]] + [shape((Y * C, slots // (Y * C), items, ENC), bf16)],
        in_specs=[VM] * 2 + [anyspec] * 21,
        out_specs=[VM] * nw + [anyspec] * 8,
        scratch_shapes=room(every, every) + room(every, every) + room(Z * Y, 1, Z) + room(Z, X, Z * X) + room(Z + 1, (Z + 1) * X * Y)
        + [pltpu.VMEM((n * 8, 128), f32), pltpu.VMEM(text.shape, f32), pltpu.VMEM((2, D), f32)]
        + [dma((nw, Z))] * 6 + [dma((nw,))] * 5 + [dma((3,)), dma((3,)), dma, dma((12,)), dma((4,))],
        compiler_params=pltpu.CompilerParams(collective_id=collective, has_side_effects=True, vmem_limit_bytes=60 << 20),
        name="backward",
    )(norms, g_third, text, image, *ws, *saved, grad_after, g_in, g_outer)
    return list(out[:nw]), out[nw], out[nw + 1]


step_rates = (0.05, 0.15, 0.05, 0.05, 0.3, 0.05, 0.05, 0.5)
step_decays = (0.01, 0.01, 0.01, 0.01, 0.01, 0.01, 0.01, 0.0)
BOTH = ("items", "patch")


def in_blocks(norms, count):
    width = D // count
    return jnp.pad(norms.reshape(6, count, width).transpose(1, 0, 2), ((0, 0), (0, 2), (0, 128 - width))).reshape(8 * count, 128)


def on_device(direct, text, cotangent, patches, text_lengths, patch_mask, *state):
    masters, firsts, seconds = state[:8], state[8:16], state[16:]
    group, local = patch_mask.shape
    chunks = lax.axis_size("patch")
    items = group // chunks
    devices = chunks * lax.axis_size("items")
    by_slot = patches.transpose(1, 0, 2)
    if direct:
        weights, image, norms, saved = forward_all(text, text_lengths, masters, by_slot, patch_mask, VALID)
    else:
        weights = [lax.all_gather(m.astype(bf16), BOTH, axis=0, tiled=True) for m in masters[:7]]
        blocks = in_blocks(lax.all_gather(masters[7].astype(bf16), BOTH, axis=1, tiled=True).astype(f32), devices)
        image = lax.all_to_all(by_slot.reshape(local, chunks, items, ENC), "patch", 1, 0)
        image = image.reshape(chunks * local * items, ENC)
        masks = patch_bias(patch_mask, lax.axis_index("patch") * local, VALID)
        masks = jnp.pad(masks, ((0, 0), (0, 128 - local))).reshape(chunks, items, 128)
        masks = lax.all_to_all(masks, "patch", 0, 0)
        norms, saved = forward_local(text, text_lengths, image, masks, weights, blocks)
    block_output, g_in, g_outer, grad_after, g_third = feed_forward_call(cotangent, weights[5:7], norms, saved[9])
    if direct:
        reduced, image_grad, text_grad = backward_all(
            text, image, weights[:5], norms, saved, grad_after, g_third, g_in, g_outer, chunks * local
        )
    else:
        text_grad, image_grad, grads, grad_blocks = backward_local(
            text, image, weights[:5], norms, saved, grad_after, g_third, devices
        )
        grads = (*grads, g_in, g_outer)
        reduced = [lax.psum_scatter(g, BOTH, scatter_dimension=0, tiled=True).astype(f32) for g in grads]
        reduced.append(lax.psum_scatter(grad_blocks, BOTH, scatter_dimension=0, tiled=True))
        image_grad = lax.all_to_all(image_grad.reshape(chunks, local, items, ENC), "patch", 0, 1)
        image_grad = image_grad.reshape(local, group, ENC)
    state_shapes = [(m.shape, f32) for m in masters]
    *updated, patch_grad = call(
        functools.partial(adamw, 8, step_decays, step_rates),
        (*masters, *firsts, *seconds, *reduced, image_grad),
        [*state_shapes * 3, (image_grad.shape, f32)], [], "adamw",
    )
    return (block_output, text_grad, patch_grad.transpose(1, 0, 2), *updated)


def solution(mesh):
    rows, cols = P(BOTH, None), P(None, BOTH)
    state = (*[rows] * 7, cols)
    direct = dict(mesh.shape) == {"items": Z * X, "patch": Y * C}
    return jax.shard_map(
        functools.partial(on_device, direct),
        mesh=mesh,
        in_specs=(rows, rows, P("items", "patch", None), P(BOTH), P("items", "patch"), *state * 3),
        out_specs=(rows, rows, P("items", "patch", None), *state * 3),
        check_vma=False,
    )
```

```python
import functools

import jax
import jax.numpy as jnp
from jax import lax
from jax.experimental import pallas as pl
from jax.experimental.pallas import tpu as pltpu
from jax.sharding import PartitionSpec as P

D = 768
HEADS = 12
HEAD_DIM = 64
ENC = 1024
TEXT = 40
VALID = 145
PAIR = 2 * HEAD_DIM
PAIRS = HEADS // 2
SCALE = HEAD_DIM ** (-0.5)
OUTSIDE = -1e30
bf16, f32 = jnp.bfloat16, jnp.float32


def dot(a, b):
    return jnp.dot(a, b, preferred_element_type=f32)


def dot_nt(a, b):
    return lax.dot_general(a, b, (((1,), (1,)), ((), ())), preferred_element_type=f32)


def dot_tn(a, b):
    return lax.dot_general(a, b, (((0,), (0,)), ((), ())), preferred_element_type=f32)


def quiet():
    pass


def chunks_of(count, parts, body, pause):
    def run(k, carry):
        body(k)
        return carry

    for part in range(parts):
        lax.fori_loop(count * part // parts, count * (part + 1) // parts, run, 0)
        if part < parts - 1:
            pause()


def tiles(total, step, body):
    def run(k, carry):
        body(pl.ds(pl.multiple_of(k * step, step), step))
        return carry

    lax.fori_loop(0, total // step, run, 0)


def norm_forward(values):
    center = values - jnp.mean(values, axis=-1, keepdims=True)
    inverse = lax.rsqrt(jnp.mean(center * center, axis=-1, keepdims=True) + 1e-12)
    return center * inverse, inverse


def norm_backward(grad_out, normed, inverse, gain):
    grad_gain = jnp.sum(grad_out * normed, axis=0, keepdims=True)
    grad_shift = jnp.sum(grad_out, axis=0, keepdims=True)
    scaled = grad_out * gain
    grad_values = inverse * (
        scaled
        - jnp.mean(scaled, axis=-1, keepdims=True)
        - normed * jnp.mean(scaled * normed, axis=-1, keepdims=True)
    )
    return grad_values, grad_gain, grad_shift


def low_half():
    return lax.broadcasted_iota(jnp.int32, (TEXT, PAIR), 1) < HEAD_DIM


def expand(rows):
    low = low_half()
    return jnp.concatenate(
        [jnp.where(low, rows, 0.0), jnp.where(low, 0.0, rows)], axis=0
    ).astype(bf16)


def fold(rows):
    return jnp.where(low_half(), rows[:TEXT], rows[TEXT:])


def softmax(scores):
    top = jnp.max(scores, axis=-1, keepdims=True)
    powers = jnp.exp(scores - top)
    return powers / jnp.sum(powers, axis=-1, keepdims=True)


def pair_cols(j, start=0):
    return slice(start + PAIR * j, start + PAIR * (j + 1))


def pair_rows(j):
    return slice(2 * TEXT * j, 2 * TEXT * (j + 1))


def attend_forward(query, keys, values, bias, probs, item, context, rows):
    js = range(PAIRS)
    scores = [dot_nt(expand(query(j)), keys(j)) * SCALE + bias for j in js]
    weights = [softmax(s) for s in scores]
    for j in js:
        probs[item, pair_rows(j), :] = weights[j]
    parts = [dot(weights[j].astype(bf16), values(j)) for j in js]
    for j in js:
        context[rows, pair_cols(j)] = fold(parts[j])


def attend_backward(query, keys, values, probs, item, grad_context, put_q, put_k, put_v):
    js = range(PAIRS)
    outer = [expand(grad_context(j)) for j in js]
    grads = [dot_nt(outer[j], values(j)) for j in js]
    inner = []
    for j in js:
        weights = probs[item, pair_rows(j), :]
        delta = jnp.sum(weights * grads[j], axis=-1, keepdims=True)
        inner.append((weights * (grads[j] - delta)).astype(bf16))
    for j in js:
        put_v(j, dot_tn(probs[item, pair_rows(j), :].astype(bf16), outer[j]))
    for j in js:
        put_q(j, fold(dot(inner[j], keys(j))) * SCALE)
    for j in js:
        put_k(j, dot_tn(inner[j], expand(query(j))) * SCALE)


def self_forward(lengths, text, w_qkv, w_out, blocks, mixed, probs, ctx, normed, inverse, norms, mix, context,
                 pause=quiet, parts=1):
    spread(blocks, norms)

    def project(cols):
        got = dot(text[...], w_qkv[:, cols]).astype(bf16)
        mixed[:, cols] = got
        mix[:, cols] = got.astype(f32)

    tiles(3 * D, 768, project)
    pause()
    position = lax.broadcasted_iota(jnp.int32, (1, TEXT), 1)

    def one(item):
        rows = pl.ds(pl.multiple_of(item * TEXT, 8), TEXT)
        bias = jnp.where(position < lengths[item], 0.0, -10000.0).astype(f32)
        attend_forward(
            lambda j: mix[rows, pair_cols(j)],
            lambda j: mix[rows, pair_cols(j, D)].astype(bf16),
            lambda j: mix[rows, pair_cols(j, 2 * D)].astype(bf16),
            bias, probs, item, context, rows,
        )

    chunks_of(probs.shape[0], parts, one, pause)
    pause()
    ctx[...] = context[...].astype(bf16)
    pre = text[...].astype(f32) + dot(ctx[...], w_out[...])
    n, r = norm_forward(pre)
    normed[...] = n
    inverse[...] = r


def self_backward(text, mixed, probs, ctx, normed, inverse, grad_after, w_qkv, w_out, norms, g_second, g_third,
                  g_qkv, g_out, text_grad, g_blocks, mix, grad_ctx, grad_mix, low_mix,
                  pause=quiet, parts=1, wide=1):
    grad_pre, grad_gain, grad_shift = norm_backward(grad_after[...], normed[...], inverse[...], norms[0:1, :])
    rows = jnp.concatenate([grad_gain, grad_shift, g_second[...], g_third[...], jnp.zeros((2, D), f32)], axis=0)
    count = g_blocks.shape[0] // 8
    width = D // count
    g_blocks[...] = jnp.zeros(g_blocks.shape, f32)
    for b in range(count):
        g_blocks[8 * b : 8 * b + 8, :width] = rows[:, width * b : width * (b + 1)]
    low = grad_pre.astype(bf16)
    g_out[...] = dot_tn(ctx[...], low).astype(bf16)
    grad_ctx[...] = dot_nt(low, w_out[...]).astype(bf16).astype(f32)
    text_grad[...] = grad_pre
    mix[...] = mixed[...].astype(f32)
    pause()

    def one(item):
        rows = pl.ds(pl.multiple_of(item * TEXT, 8), TEXT)

        def put(start):
            def store(j, value):
                grad_mix[rows, pair_cols(j, start)] = value
            return store

        attend_backward(
            lambda j: mix[rows, pair_cols(j)],
            lambda j: mix[rows, pair_cols(j, D)].astype(bf16),
            lambda j: mix[rows, pair_cols(j, 2 * D)].astype(bf16),
            probs, item, lambda j: grad_ctx[rows, pair_cols(j)],
            put(0), put(D), put(2 * D),
        )

    chunks_of(probs.shape[0], parts, one, pause)
    pause()
    low_mix[...] = grad_mix[...].astype(bf16)

    def weights(k):
        cols = pl.ds(pl.multiple_of(k * D, D), D)
        g_qkv[:, cols] = dot_tn(text[...], low_mix[:, cols]).astype(bf16)
        text_grad[...] += dot_nt(low_mix[:, cols], w_qkv[:, cols])

    chunks_of(3, wide, weights, pause)


def spread(blocks, norms):
    count = blocks.shape[0] // 8
    width = D // count
    for b in range(count):
        norms[:, width * b : width * (b + 1)] = blocks[8 * b : 8 * b + 8, :width]


def cross_forward(image, masks, w_kv, w_q, w_out, norms, normed_one,
                  memory, query, probs, ctx, normed, inverse, bias, context, wide, flat,
                  pause=quiet, tall=1, parts=1):
    items = masks.shape[1]
    slots = bias.shape[1]
    local = slots // masks.shape[0]
    for c in range(masks.shape[0]):
        bias[:, local * c : local * (c + 1)] = masks[c, :, :local]

    def project(k):
        got = dot(image[...], w_kv[:, pl.ds(pl.multiple_of(4 * PAIR * k, 4 * PAIR), 4 * PAIR)]).astype(bf16).astype(f32)
        for j in range(4):
            flat[4 * k + j] = got[:, pair_cols(j)]

    chunks_of(PAIRS // 2, tall, project, pause)
    pause()
    after = normed_one[...] * norms[0:1, :] + norms[1:2, :]
    low = dot(after.astype(bf16), w_q[...]).astype(bf16)
    query[...] = low
    wide[...] = low.astype(f32)

    def one(item):
        rows = pl.ds(pl.multiple_of(item * TEXT, 8), TEXT)
        every = pl.ds(item, slots, stride=items)
        for j in range(2 * PAIRS):
            memory[item, :, pair_cols(j)] = flat[j, every, :].astype(bf16)
        attend_forward(
            lambda j: wide[rows, pair_cols(j)],
            lambda j: memory[item, :, pair_cols(j)],
            lambda j: memory[item, :, pair_cols(j, D)],
            bias[pl.ds(item, 1), :], probs, item, context, rows,
        )

    chunks_of(items, parts, one, pause)
    pause()
    ctx[...] = context[...].astype(bf16)
    pre = after + dot(ctx[...], w_out[...])
    n, r = norm_forward(pre)
    normed[...] = n
    inverse[...] = r


def cross_backward(memory, query, probs, ctx, normed, inverse, normed_one, grad_after, w_q, w_out, norms,
                   g_q, g_out, grad_self, g_norm, flat, wide, grad_ctx, grad_q, pause=quiet, parts=1):
    items, slots = memory.shape[:2]
    grad_pre, grad_gain, grad_shift = norm_backward(grad_after[...], normed[...], inverse[...], norms[2:3, :])
    g_norm[0:1, :] = grad_gain
    g_norm[1:2, :] = grad_shift
    grad_self[...] = grad_pre
    low = grad_pre.astype(bf16)
    g_out[...] = dot_tn(ctx[...], low).astype(bf16)
    grad_ctx[...] = dot_nt(low, w_out[...]).astype(bf16).astype(f32)
    wide[...] = query[...].astype(f32)
    pause()

    def one(item):
        rows = pl.ds(pl.multiple_of(item * TEXT, 8), TEXT)
        every = pl.ds(item, slots, stride=items)

        def put_q(j, value):
            grad_q[rows, pair_cols(j)] = value

        def put(start):
            def store(j, value):
                flat[start + j, every, :] = value
            return store

        attend_backward(
            lambda j: wide[rows, pair_cols(j)],
            lambda j: memory[item, :, pair_cols(j)],
            lambda j: memory[item, :, pair_cols(j, D)],
            probs, item, lambda j: grad_ctx[rows, pair_cols(j)],
            put_q, put(0), put(PAIRS),
        )

    chunks_of(items, parts, one, pause)
    low_q = grad_q[...].astype(bf16)
    after = (normed_one[...] * norms[0:1, :] + norms[1:2, :]).astype(bf16)
    g_q[...] = dot_tn(after, low_q).astype(bf16)
    grad_self[...] += dot_nt(low_q, w_q[...])


def memory_backward(image, w_kv, flat, g_kv, image_grad, grad_mem, pause=quiet, wide=1):
    for j in range(2 * PAIRS):
        grad_mem[:, pair_cols(j)] = flat[j].astype(bf16)
    step = 4 * PAIR

    def weights(k):
        cols = pl.ds(pl.multiple_of(k * step, step), step)
        g_kv[:, cols] = dot_tn(image[...], grad_mem[:, cols]).astype(bf16)

    chunks_of(2 * D // step, wide, weights, pause)
    pause()

    def back(k):
        cols = pl.ds(pl.multiple_of(k * step, step), step)
        image_grad[:, cols] = dot_nt(grad_mem[...], w_kv[cols, :]).astype(bf16)

    chunks_of(ENC // step, 1, back, pause)


def feed_forward(normed_two, cotangent, w_inner, w_outer, norms,
                 block_output, g_inner, g_outer, grad_after, g_norm, low_in, hidden, slope, total, grad_low,
                 inner_in, outer_in, inner_out, outer_out, load, store):
    step = D
    count = w_inner.shape[1] // step

    def part(k):
        return pl.ds(pl.multiple_of(k * step, step), step)

    def loads(k):
        cols = part(k)
        return (
            pltpu.make_async_copy(w_inner.at[:, cols], inner_in.at[:, cols], load.at[0, k]),
            pltpu.make_async_copy(w_outer.at[cols], outer_in.at[cols], load.at[1, k]),
        )

    def stores(k):
        cols = part(k)
        return (
            pltpu.make_async_copy(inner_out.at[:, cols], g_inner.at[:, cols], store.at[0, k]),
            pltpu.make_async_copy(outer_out.at[cols], g_outer.at[cols], store.at[1, k]),
        )

    for k in range(count):
        for copy in loads(k):
            copy.start()
    after = normed_two[...] * norms[2:3, :] + norms[3:4, :]
    low_in[...] = after.astype(bf16)
    total[...] = after

    def up(k):
        cols = part(k)
        for copy in loads(k):
            copy.wait()
        pre = dot(low_in[...], inner_in[:, cols])
        bell = 0.5 * (1.0 + lax.erf(pre * (0.5 ** 0.5)))
        low = (pre * bell).astype(bf16)
        hidden[:, cols] = low
        slope[:, cols] = bell + pre * jnp.exp(-0.5 * pre * pre) * 0.3989422804014327
        total[...] += dot(low, outer_in[cols, :])

    chunks_of(count, 1, up, quiet)
    n, r = norm_forward(total[...])
    gain = norms[4:5, :]
    block_output[...] = (n * gain + norms[5:6, :]).astype(bf16)
    grad_pre, grad_gain, grad_shift = norm_backward(cotangent[...].astype(f32), n, r, gain)
    g_norm[0:1, :] = grad_gain
    g_norm[1:2, :] = grad_shift
    grad_after[...] = grad_pre
    grad_low[...] = grad_pre.astype(bf16)

    def down(k):
        cols = part(k)
        low = (dot_nt(grad_low[...], outer_in[cols, :]) * slope[:, cols]).astype(bf16)
        inner_out[:, cols] = dot_tn(low_in[...], low).astype(bf16)
        outer_out[cols, :] = dot_tn(hidden[:, cols], grad_low[...]).astype(bf16)
        for copy in stores(k):
            copy.start()
        grad_after[...] += dot_nt(low, inner_in[:, cols])

    chunks_of(count, 1, down, quiet)
    for k in range(count):
        for copy in stores(k):
            copy.wait()


VM = pl.BlockSpec(memory_space=pltpu.VMEM)


def call(body, args, outs, scratch, name, smem=0, limit=60 << 20, left=(), sems=()):
    def where(k):
        return pl.BlockSpec(memory_space=pl.ANY) if k in left else VM

    return pl.pallas_call(
        body,
        out_shape=[jax.ShapeDtypeStruct(s, k) for s, k in outs],
        in_specs=[pl.BlockSpec(memory_space=pltpu.SMEM)] * smem + [where(k) for k in range(smem, len(args))],
        out_specs=[where(len(args) + k) for k in range(len(outs))],
        scratch_shapes=[pltpu.VMEM(s, k) for s, k in scratch] + [pltpu.SemaphoreType.DMA(s) for s in sems],
        compiler_params=pltpu.CompilerParams(vmem_limit_bytes=limit),
        name=name,
    )(*args)


def adamw(count, decays, rates, *refs):
    masters, firsts, seconds, grads = (refs[count * i : count * (i + 1)] for i in range(4))
    image_low = refs[4 * count]
    new_m, new_f, new_s = (refs[4 * count + 1 + count * i : 4 * count + 1 + count * (i + 1)] for i in range(3))
    image_grad = refs[7 * count + 1]
    for k in range(count):
        rows, cols = masters[k].shape
        gradient = grads[k][:rows, :cols]
        first = 0.9 * firsts[k][...] + 0.1 * gradient
        second = 0.999 * seconds[k][...] + 0.001 * gradient * gradient
        step = first / (1.0 - 0.9**10) / (jnp.sqrt(second / (1.0 - 0.999**10)) + 1e-08)
        master = masters[k][...]
        new_m[k][...] = master - rates[k] * (step + decays[k] * master)
        new_f[k][...] = first
        new_s[k][...] = second
    image_grad[...] = image_low[...].astype(f32)


def forward_local(text, lengths, image, masks, ws, blocks):
    w_qkv, w_out, w_cq, w_kv, w_co = ws[:5]
    rows = text.shape[0]
    items = rows // TEXT
    slots = image.shape[0] // items
    pairs = HEADS * TEXT
    row = ((rows, D), f32)
    rowl = ((rows, D), bf16)
    one = ((rows, 1), f32)
    *first, norms = call(
        self_forward, (lengths, text, w_qkv, w_out, blocks),
        [((rows, 3 * D), bf16), ((items, pairs, TEXT), f32), rowl, row, one, ((8, D), f32)],
        [((rows, 3 * D), f32), row], "self_forward", smem=1)
    second = call(
        cross_forward, (image, masks, w_kv, w_cq, w_co, norms, first[3]),
        [((items, slots, 2 * D), bf16), rowl, ((items, pairs, slots), f32), rowl, row, one],
        [((items, slots), f32), row, row, ((2 * PAIRS, items * slots, PAIR), f32)], "cross_forward")
    return norms, [*first, *second]


def feed_forward_call(cotangent, ws, norms, n2):
    w_in, w_outer = ws
    rows, ff = n2.shape[0], w_in.shape[1]
    row = ((rows, D), f32)
    rowl = ((rows, D), bf16)
    return call(
        feed_forward, (n2, cotangent, w_in, w_outer, norms),
        [rowl, ((D, ff), bf16), ((ff, D), bf16), row, ((2, D), f32)],
        [rowl, ((rows, ff), bf16), ((rows, ff), f32), row, rowl, *[(w.shape, bf16) for w in (w_in, w_outer)] * 2],
        "feed_forward", left=(2, 3, 6, 7), sems=[(2, ff // D)] * 2)


def backward_local(text, image, ws, norms, saved, grad_after, gn3, count):
    w_qkv, w_out, w_cq, w_kv, w_co = ws
    mixed, probs, ctx, n1, r1, memory, query, cprobs, cctx, n2, r2 = saved
    rows = text.shape[0]
    row = ((rows, D), f32)
    flat = (2 * PAIRS, image.shape[0], PAIR)
    g_cq, g_co, grad_self, gn2, flat_grad = call(
        cross_backward, (memory, query, cprobs, cctx, n2, r2, n1, grad_after, w_cq, w_co, norms),
        [((D, D), bf16), ((D, D), bf16), row, ((2, D), f32), (flat, f32)], [row, row, row], "cross_backward")
    g_kv, image_grad = call(
        memory_backward, (image, w_kv, flat_grad), [((ENC, 2 * D), bf16), (image.shape, bf16)],
        [((image.shape[0], 2 * D), bf16)], "memory_backward")
    g_qkv, g_out, text_grad, g_blocks = call(
        self_backward, (text, mixed, probs, ctx, n1, r1, grad_self, w_qkv, w_out, norms, gn2, gn3),
        [((D, 3 * D), bf16), ((D, D), bf16), row, ((count * 8, 128), f32)],
        [((rows, 3 * D), f32), row, ((rows, 3 * D), f32), ((rows, 3 * D), bf16)], "self_backward")
    return text_grad, image_grad, (g_qkv, g_out, g_cq, g_kv, g_co), g_blocks


MESH = pl.DeviceIdType.MESH
Z, X, Y, C = 4, 2, 2, 2
PLANE_FIRST, TURNED = (0,), (6,)
SETS = ((0, 1, 7, 3, 2, 4), (5, 6))
PLAN = (
    ("0", "00", "01", "1", "02", "swap", "03", "10", "04", "11", "05", "06", "swapped"),
    (("12",),),
    (),
    (("13",), (), ("14",), ("15",)),
    ("16",),
)
PLANE_LAST, TURNED_BACK = (3,), (6,)
ROUNDS = tuple((k, ws) for ws in ((6, 5), (3, 2, 4), (0, 1, 7)) for k in range(4))
BACK_PLAN = (
    ("b0", "b1", "c0", "b2"),
    ("c1", "b3"),
    ("c2", "a0"),
    ("c3", "a1"),
    ("a2",),
    ("d0", "a3"),
    ("d1",),
    ("b4", "b5", "s", "d2"),
    ("c4", "e4", "b6"),
    ("c5", "e5", "a4", "b7"),
    ("c6", "e6", "a5", "d3"),
    ("c7", "a6", "m4"),
    ("b8", "b9", "c8", "b10", "c9", "b11", "a7", "a8", "c10", "d4", "m5", "d5", "a9", "c11", "m6", "d6", "d8", "a10", "p7", "d7", "d9", "a11", "q7", "d10", "d11"),
)
bf16, f32 = jnp.bfloat16, jnp.float32


class Place:
    def __init__(self):
        item, self.me = lax.axis_index("items"), lax.axis_index("patch")
        self.z, self.x, self.y, self.c = item // X, item % X, self.me // C, self.me % C
        z, x, y, c = self.z, self.x, self.y, self.c
        self.left = (item - X, self.me)
        self.right = (item + X, self.me)
        self.xdev = (z * X + (1 - x), self.me)
        self.ypeer, self.cpeer, self.dpeer = (1 - y) * C + c, y * C + (1 - c), (1 - y) * C + (1 - c)
        self.ydev, self.cdev, self.ddev = (item, self.ypeer), (item, self.cpeer), (item, self.dpeer)

    def at(self, zz, xx, yy, cc):
        return ((zz * X + xx) * Y + yy) * C + cc

    def greet(self, barrier):
        for dev in (self.xdev, self.ydev, self.cdev, self.ddev):
            pl.semaphore_signal(barrier, inc=1, device_id=dev, device_id_type=MESH)

        @pl.when(self.z > 0)
        def _():
            pl.semaphore_signal(barrier, inc=1, device_id=self.left, device_id_type=MESH)

        @pl.when(self.z < Z - 1)
        def _():
            pl.semaphore_signal(barrier, inc=1, device_id=self.right, device_id_type=MESH)

    def met(self, barrier):
        pl.semaphore_wait(barrier, 4 + (self.z > 0).astype(jnp.int32) + (self.z < Z - 1).astype(jnp.int32))

    def both(self, d, step):
        if d == 0:
            step(self.z, None)
            return

        @pl.when(self.z >= d)
        def _():
            step(self.z - d, True)

        @pl.when(self.z + d < Z)
        def _():
            step(self.z + d, False)


def patch_bias(mask, first, valid):
    index = first + lax.broadcasted_iota(jnp.int32, mask.shape, 1)
    return jnp.where((mask > 0) & (index < valid), 0.0, -10000.0).astype(f32)


class Gather:
    def __init__(self, place, plane_first, turned, low, outs, recv, to_x, to_y, to_c, to_l, to_r, local):
        self.place, self.plane_first, self.turned = place, plane_first, turned
        self.low, self.outs, self.recv, self.local = low, outs, recv, local
        self.sems = {"x": to_x, "y": to_y, "c": to_c, "l": to_l, "r": to_r}
        self.devs = {"x": place.xdev, "y": place.ydev, "c": place.cdev, "l": place.left, "r": place.right}
        self.mine = place.at(place.z, place.x, place.y, place.c)

    def blocks(self, w, first, count=1):
        rows = self.low[w].shape[0]
        return self.outs[w].at[pl.ds(pl.multiple_of(first * rows, rows), count * rows)]

    def copy(self, w, block, way, own=False):
        return pltpu.make_async_remote_copy(
            src_ref=self.low[w] if own else self.blocks(w, block),
            dst_ref=self.blocks(w, block),
            send_sem=self.sems[way].at[w],
            recv_sem=self.recv.at[w, block],
            device_id=self.devs[way],
            device_id_type=MESH,
        )

    def send(self, w, block, ways, own=False):
        z = self.place.z
        for way in ways:
            if way == "l":
                @pl.when(z > 0)
                def _():
                    self.copy(w, block, "l", own).start()
            elif way == "r":
                @pl.when(z < Z - 1)
                def _():
                    self.copy(w, block, "r", own).start()
            else:
                self.copy(w, block, way, own).start()

    def arrived(self, w, block):
        self.copy(w, block, "x").wait_recv()

    def pass_on(self, w, block, ways):
        self.arrived(w, block)
        self.send(w, block, ways)

    def keep(self, w):
        return pltpu.make_async_copy(self.low[w], self.blocks(w, self.mine), self.local.at[w])

    def start(self, ws):
        for w in ws:
            self.send(w, self.mine, "xylr" if w in self.plane_first else "lryx", True)
        for w in ws:
            self.send(w, self.mine, "c", True)
            self.keep(w).start()

    def stages(self, ws):
        p = self.place
        x, y, c = p.x, p.y, p.c
        line = [w for w in ws if w not in self.plane_first]
        plane = [w for w in ws if w in self.plane_first]

        def plane_x():
            for w in plane:
                self.pass_on(w, p.at(p.z, 1 - x, y, c), "ylrc")

        def plane_y():
            for xx in (x, 1 - x):
                for w in plane:
                    self.pass_on(w, p.at(p.z, xx, 1 - y, c), "lrc")

        def plane_z(zz, from_left):
            for xx, yy in ((x, y), (1 - x, y), (x, 1 - y), (1 - x, 1 - y)):
                for w in plane:
                    self.pass_on(w, p.at(zz, xx, yy, c), "rc" if from_left else "lc")

        def line_z(zz, from_left):
            for w in line:
                self.pass_on(w, p.at(zz, x, y, c), "ryxc" if from_left else "lyxc")

        def line_y(zz, _):
            for w in line:
                if w in self.turned:
                    self.pass_on(w, p.at(zz, 1 - x, y, c), "yc")
                else:
                    self.pass_on(w, p.at(zz, x, 1 - y, c), "xc")

        def line_x(zz, _):
            for near in (True, False):
                for w in line:
                    if w in self.turned:
                        self.pass_on(w, p.at(zz, x if near else 1 - x, 1 - y, c), "c")
                    else:
                        self.pass_on(w, p.at(zz, 1 - x, y if near else 1 - y, c), "c")

        def from_core():
            for zz in range(Z):
                for xx in range(X):
                    for yy in range(Y):
                        for w in ws:
                            self.arrived(w, p.at(zz, xx, yy, 1 - c))
            for w in ws:
                self.keep(w).wait()

        def steps(*pairs):
            def run():
                for d, step in pairs:
                    if d is None:
                        step()
                    else:
                        p.both(d, step)
            return run

        first = [(None, plane_x)] if plane else []
        second = [(None, plane_y)] if plane else []

        def deep(d):
            return [(d, plane_z)] if plane else []

        if not line:
            return [steps(*first), steps(*second), steps(*deep(1)), steps(*deep(2)), steps(*deep(3)), quiet, from_core]
        return [
            steps(*first, (1, line_z)),
            steps(*second, (0, line_y)),
            steps(*deep(1), (2, line_z), (1, line_y), (0, line_x)),
            steps(*deep(2), (3, line_z), (2, line_y), (1, line_x)),
            steps(*deep(3), (3, line_y), (2, line_x)),
            steps((3, line_x)),
            from_core,
        ]

    def finish(self):
        z = self.place.z
        for w in range(len(self.low)):
            def sent(count, way):
                span = self.blocks(w, 0, count)
                pltpu.make_async_copy(span, span, self.sems[way].at[w]).wait()

            plane = w in self.plane_first
            wide = X * Y if plane else 1
            turned = w in self.turned
            sent(1 if plane else Z if turned else Z * Y, "x")
            sent(X if plane else Z * X if turned else Z, "y")
            sent(Z * X * Y, "c")
            for k in range(Z):
                @pl.when(z == k)
                def _():
                    if k > 0:
                        sent(wide * (Z - k), "l")
                    if k < Z - 1:
                        sent(wide * (k + 1), "r")


def forward_kernel(plane_first, turned, sets, plan, valid, *refs):
    nw = 8
    refs = list(refs)

    def take(count):
        got = refs[:count]
        del refs[:count]
        return got

    (lengths,), shards, (image, mask, text) = take(1), take(nw), take(3)
    whole, (image_out, norms) = take(nw - 1), take(2)
    saved = take(11)
    low, (blocks, masks, bias_here) = take(nw), take(3)
    w_qkv, w_out, w_cq, w_kv, w_co = take(5)
    image_in, mix, context, bias, wide, flat = take(6)
    kept = take(11)
    recv, to_x, to_y, to_c, to_l, to_r, local, psend, precv, plocal, load, save = take(12)
    p = Place()
    me = p.me
    barrier = pltpu.get_barrier_semaphore()
    p.greet(barrier)
    for w in range(nw - 1):
        low[w][...] = shards[w][...].astype(low[w].dtype)
    low[nw - 1][...] = jnp.zeros(low[nw - 1].shape, f32)
    rows, cols = shards[nw - 1].shape
    low[nw - 1][:rows, :cols] = shards[nw - 1][...].astype(bf16).astype(f32)
    slots = mask.shape[1]
    bias_here[...] = jnp.zeros(bias_here.shape, f32)
    bias_here[:, :slots] = patch_bias(mask[...], me * slots, valid)
    here = mask.shape[0] // (Y * C)
    peers = ((p.ydev, p.ypeer), (p.cdev, p.cpeer), (p.ddev, p.dpeer))
    swaps = (image_out, masks)

    def part(s, peer):
        rows = pl.ds(pl.multiple_of(peer * here, here), here)
        return bias_here.at[rows] if s else image.at[:, rows]

    def swap(s, k):
        dev, peer = peers[k]
        return pltpu.make_async_remote_copy(
            src_ref=part(s, peer),
            dst_ref=swaps[s].at[me],
            send_sem=psend.at[s, k],
            recv_sem=precv.at[s, k],
            device_id=dev,
            device_id_type=MESH,
        )

    def stay(s):
        return pltpu.make_async_copy(part(s, me), swaps[s].at[me], plocal.at[s])

    gather = Gather(p, plane_first, turned, low, [*whole, blocks], recv, to_x, to_y, to_c, to_l, to_r, local)
    staged = [gather.stages(ws) for ws in sets]
    p.met(barrier)

    def start_swaps():
        for s in range(2):
            for k in range(3):
                swap(s, k).start()
            stay(s).start()

    def end_swaps():
        for s in range(2):
            for k in range(3):
                swap(s, k).wait()
            stay(s).wait()

    def loads(pairs):
        return [pltpu.make_async_copy(src, dst, load.at[k]) for k, src, dst in pairs]

    early = loads([(0, whole[0], w_qkv), (1, whole[1], w_out)])
    late = loads([(2, whole[2], w_cq), (3, whole[3], w_kv), (4, whole[4], w_co)])

    def flatten(k, carry):
        rows = pl.ds(pl.multiple_of(k * here, here), here)
        pltpu.make_async_copy(image_out.at[k // slots, k % slots], image_in.at[rows], load.at[5]).start()
        return carry
    saves = [pltpu.make_async_copy(src, dst, save.at[k]) for k, (src, dst) in enumerate(zip(kept, saved))]

    def run(tokens):
        for token in tokens:
            if token == "swap":
                start_swaps()
            elif token == "swapped":
                end_swaps()
            elif len(token) == 1:
                gather.start(sets[int(token)])
            else:
                staged[int(token[0])][int(token[1])]()

    def queue(events):
        left = list(events)

        def pause():
            if left:
                run(left.pop(0))

        return pause

    before, during_self, between, during_cross, after = plan
    run(before)
    for copy in early:
        copy.start()
    for copy in early:
        copy.wait()
    mixed, probs, ctx, normed, inverse, memory, query, cross_probs, cross_ctx, normed_two, inverse_two = kept
    self_forward(
        lengths, text, w_qkv, w_out, blocks, mixed, probs, ctx, normed, inverse, norms, mix, context,
        queue(during_self), 2,
    )
    for copy in saves[:5]:
        copy.start()
    run(between)
    for copy in late:
        copy.start()
    lax.fori_loop(0, Y * C * slots, flatten, 0)
    for copy in late:
        copy.wait()
    pltpu.make_async_copy(image_in, image_in, load.at[5]).wait()
    cross_forward(
        image_in, masks, w_kv, w_cq, w_co, norms, normed,
        memory, query, cross_probs, cross_ctx, normed_two, inverse_two, bias, context, wide, flat,
        queue(during_cross), 2, 4,
    )
    for copy in saves[5:]:
        copy.start()
    run(after)
    gather.finish()
    for copy in saves:
        copy.wait()


def forward_all(text, lengths, shards, image, mask, valid, plane_first=PLANE_FIRST, turned=TURNED, sets=SETS, plan=PLAN, collective=0):
    nw = len(shards)
    n = Z * X * Y * C
    shapes = [s.shape for s in shards[:-1]] + [(8, 128)]
    kinds = [bf16] * (nw - 1) + [f32]
    slots, group, width = image.shape
    items = group // (Y * C)
    rows = text.shape[0]
    every = slots * Y * C
    pairs = HEADS * TEXT
    row, low_row, one = ((rows, D), f32), ((rows, D), bf16), ((rows, 1), f32)
    keep = [
        ((rows, 3 * D), bf16), ((items, pairs, TEXT), f32), low_row, row, one,
        ((items, every, 2 * D), bf16), low_row, ((items, pairs, every), f32), low_row, row, one,
    ]
    anyspec = pl.BlockSpec(memory_space=pl.ANY)
    dma = pltpu.SemaphoreType.DMA
    shape = jax.ShapeDtypeStruct
    out = pl.pallas_call(
        functools.partial(forward_kernel, plane_first, turned, sets, plan, valid),
        out_shape=[shape((n * s[0], s[1]), bf16) for s in shapes[:-1]]
        + [shape((Y * C, slots, items, width), image.dtype), shape((8, D), f32)]
        + [shape(*k) for k in keep],
        in_specs=[pl.BlockSpec(memory_space=pltpu.SMEM)] + [VM] * nw + [anyspec, VM, VM],
        out_specs=[anyspec] * nw + [VM] + [anyspec] * len(keep),
        scratch_shapes=[pltpu.VMEM(s, k) for s, k in zip(shapes, kinds)]
        + [pltpu.VMEM((n * 8, 128), f32), pltpu.VMEM((Y * C, items, 128), f32), pltpu.VMEM((group, 128), f32)]
        + [pltpu.VMEM((n * shapes[w][0], shapes[w][1]), bf16) for w in range(5)]
        + [pltpu.VMEM(s, k) for s, k in (
            ((every * items, width), bf16), ((rows, 3 * D), f32), row, ((items, every), f32), row,
            ((2 * PAIRS, items * every, PAIR), f32), *keep)]
        + [dma((nw, n))] + [dma((nw,))] * 6 + [dma((2, 3)), dma((2, 3)), dma((2,)), dma((6,)), dma((len(keep),))],
        compiler_params=pltpu.CompilerParams(collective_id=collective, has_side_effects=True, vmem_limit_bytes=60 << 20),
        name="forward",
    )(lengths, *shards, image, mask, text)
    return out[: nw - 1], out[nw - 1].reshape(every * items, width), out[nw], out[nw + 1 :]


class Scatter:
    def __init__(self, place, plane_first, turned, grads, own, from_core, from_x, from_y, from_z, sems):
        self.place, self.plane_first, self.turned, self.grads, self.own = place, plane_first, turned, grads, own
        self.from_core, self.from_x, self.from_y, self.from_z = from_core, from_x, from_y, from_z
        self.load, self.rcore, self.rx, self.ry, self.rl, self.rr, self.score, self.sx, self.sy, self.sl, self.sr = sems

    def target(self, k):
        half = self.place.z // 2
        near = self.place.z * (1 - half) + (Z - 1 - self.place.z) * half
        return half * (Z - 1) + (1 - 2 * half) * (Z - 1, 2 - 2 * near, 1 + near, near)[k]

    def copy(self, src, dst, send_sem, recv_sem, dev):
        return pltpu.make_async_remote_copy(
            src_ref=src, dst_ref=dst, send_sem=send_sem, recv_sem=recv_sem, device_id=dev, device_id_type=MESH
        )

    def arrived(self, dst, sem):
        self.copy(dst, dst, self.score.at[0], sem, self.place.cdev).wait_recv()

    def block(self, w, b):
        rows = self.own[w].shape[1]
        return self.grads[w].at[pl.ds(pl.multiple_of(b * rows, rows), rows)]

    def add(self, w, at, count, ref, start):
        mine = self.own[w]

        def one(i, carry):
            mine[at + i] = (mine[at + i].astype(f32) + ref[start + i].astype(f32)).astype(mine.dtype)
            return carry

        if count == 1:
            one(0, 0)
        else:
            lax.fori_loop(0, count, one, 0)

    def begin(self, k, ws):
        t, c = self.target(k), self.place.c
        for w in ws:
            for s in range(X * Y):
                q = t * X * Y + s
                pltpu.make_async_copy(self.block(w, q * C + c), self.own[w].at[q], self.load.at[w, t]).start()
                self.copy(
                    self.block(w, q * C + 1 - c), self.from_core[w].at[q], self.score.at[w], self.rcore.at[w, t], self.place.cdev
                ).start()

    def core(self, k, ws):
        t, p = self.target(k), self.place
        span = pl.ds(t * X * Y, X * Y)
        for w in ws:
            mine = self.own[w].at[span]
            pltpu.make_async_copy(mine, mine, self.load.at[w, t]).wait()
            self.arrived(self.from_core[w].at[span], self.rcore.at[w, t])
            self.add(w, t * X * Y, X * Y, self.from_core[w], t * X * Y)
            if w in self.turned:
                for xx in range(X):
                    self.copy(
                        self.own[w].at[(t * X + xx) * Y + 1 - p.y], self.from_y[w].at[t * X + xx],
                        self.sy.at[w], self.ry.at[w, t], p.ydev,
                    ).start()
            elif w not in self.plane_first:
                self.copy(
                    self.own[w].at[pl.ds((t * X + 1 - p.x) * Y, Y)], self.from_x[w].at[pl.ds(t * Y, Y)],
                    self.sx.at[w], self.rx.at[w, t], p.xdev,
                ).start()

    def across(self, k, ws):
        t, p = self.target(k), self.place
        for w in ws:
            if w in self.turned:
                self.arrived(self.from_y[w].at[pl.ds(t * X, X)], self.ry.at[w, t])
                for xx in range(X):
                    self.add(w, (t * X + xx) * Y + p.y, 1, self.from_y[w], t * X + xx)
                self.copy(
                    self.own[w].at[(t * X + 1 - p.x) * Y + p.y], self.from_x[w].at[t], self.sx.at[w], self.rx.at[w, t], p.xdev
                ).start()
                continue
            self.arrived(self.from_x[w].at[pl.ds(t * Y, Y)], self.rx.at[w, t])
            self.add(w, (t * X + p.x) * Y, Y, self.from_x[w], t * Y)
            self.copy(
                self.own[w].at[(t * X + p.x) * Y + 1 - p.y], self.from_y[w].at[t], self.sy.at[w], self.ry.at[w, t], p.ydev
            ).start()

    def along(self, k, ws, first, count):
        t, z = self.target(k), self.place.z

        def span(w):
            return self.own[w].at[pl.ds(first(t), count)]

        def slot(w, s):
            return self.from_z[w].at[pl.ds(s * count, count)]

        def take(w, s, sem):
            self.arrived(slot(w, s), sem.at[w, t])
            self.add(w, first(t), count, self.from_z[w], s * count)

        if k < Z - 1:
            @pl.when(t > z)
            def _():
                for w in ws:
                    @pl.when(z > 0)
                    def _():
                        take(w, t, self.rl)

                    self.copy(span(w), slot(w, t), self.sr.at[w], self.rl.at[w, t], self.place.right).start()

            @pl.when(t < z)
            def _():
                there = t + (Z - t) * (t == z - 1).astype(jnp.int32)
                for w in ws:
                    @pl.when(z < Z - 1)
                    def _():
                        take(w, t, self.rr)

                    self.copy(span(w), slot(w, there), self.sl.at[w], self.rr.at[w, t], self.place.left).start()
        else:
            for w in ws:
                @pl.when(z > 0)
                def _():
                    take(w, t, self.rl)

                @pl.when(z < Z - 1)
                def _():
                    take(w, Z, self.rr)

    def down(self, k, ws):
        t, p = self.target(k), self.place
        for w in ws:
            ref, sem = (self.from_x, self.rx) if w in self.turned else (self.from_y, self.ry)
            self.arrived(ref[w].at[t], sem.at[w, t])
            self.add(w, (t * X + p.x) * Y + p.y, 1, ref[w], t)
        self.along(k, ws, lambda t: (t * X + p.x) * Y + p.y, 1)

    def plane(self, k, ws):
        p = self.place
        self.along(k, ws, lambda t: t * X * Y, X * Y)
        if k == Z - 1:
            for w in ws:
                for xx in range(X):
                    self.copy(
                        self.own[w].at[(p.z * X + xx) * Y + 1 - p.y], self.from_y[w].at[xx], self.sy.at[w], self.ry.at[w, xx], p.ydev
                    ).start()

    def plane_across(self, ws):
        p = self.place
        for w in ws:
            for xx in range(X):
                self.arrived(self.from_y[w].at[xx], self.ry.at[w, xx])
                self.add(w, (p.z * X + xx) * Y + p.y, 1, self.from_y[w], xx)
            self.copy(
                self.own[w].at[(p.z * X + 1 - p.x) * Y + p.y], self.from_x[w].at[0], self.sx.at[w], self.rx.at[w, 0], p.xdev
            ).start()

    def act(self, name, k, ws):
        line = [w for w in ws if w not in self.plane_first]
        plane = [w for w in ws if w in self.plane_first]
        z = self.place.z
        if name == "b":
            self.begin(k, ws)
        elif name == "c":
            self.core(k, ws)
        elif name == "a":
            self.across(k, line)
        elif name == "d":
            self.down(k, line)
        elif name == "e":
            @pl.when((z == 0) | (z == Z - 1))
            def _():
                self.plane(k, plane)
        elif name == "m":
            @pl.when((z > 0) & (z < Z - 1))
            def _():
                self.plane(k, plane)
        elif name == "p":
            self.plane(k, plane)
        elif name == "q":
            self.plane_across(plane)

    def finish(self, outs):
        p = self.place
        at = (p.z * X + p.x) * Y + p.y
        for w, out in enumerate(outs):
            plane = w in self.plane_first
            total = self.own[w][at].astype(f32)
            if plane:
                self.arrived(self.from_x[w].at[0], self.rx.at[w, 0])
                total = total + self.from_x[w][0].astype(f32)
            out[...] = total

            def sent(count, sem):
                span = self.own[w].at[pl.ds(0, count)]
                pltpu.make_async_copy(span, span, sem.at[w]).wait()

            sent(Z * X * Y, self.score)
            turned = w in self.turned
            sent(1 if plane else Z if turned else Z * Y, self.sx)
            sent(X if plane else Z * X if turned else Z, self.sy)
            per = X * Y if plane else 1
            for k in range(Z):
                @pl.when(p.z == k)
                def _():
                    if k > 0:
                        sent(per * k, self.sl)
                    if k < Z - 1:
                        sent(per * (Z - 1 - k), self.sr)


def backward_kernel(plane_first, turned, rounds, plan, *refs):
    nw = 8
    refs = list(refs)

    def take(count):
        got = refs[:count]
        del refs[:count]
        return got

    norms, g_third = take(2)
    text, image, w_qkv, w_out, w_cq, w_kv, w_co = take(7)
    mixed, probs, ctx, n1, r1, memory, query, cprobs, cctx, n2, r2 = take(11)
    grad_after, g_in, g_outer = take(3)
    outs, (swapped, text_grad) = take(nw), take(2)
    g_qkv, g_out, g_cq, g_kv, g_co, image_grad = take(6)
    own, from_core, from_x, from_y, from_z = (take(nw) for _ in range(5))
    g_blocks, grad_self, g_second = take(3)
    sems = take(11)
    psend, precv, plocal, fetch, store = take(5)
    p = Place()
    me = p.me
    barrier = pltpu.get_barrier_semaphore()
    p.greet(barrier)
    scatter = Scatter(
        p, plane_first, turned, [g_qkv, g_out, g_cq, g_kv, g_co, g_in, g_outer, g_blocks], own, from_core, from_x, from_y, from_z, sems
    )
    here = swapped.shape[1] // (Y * C)
    place = swapped.at[:, pl.ds(pl.multiple_of(me * here, here), here)]
    peers = ((p.ydev, p.ypeer), (p.cdev, p.cpeer), (p.ddev, p.dpeer))

    def swap(k):
        return scatter.copy(image_grad.at[peers[k][1]], place, psend.at[k], precv.at[k], peers[k][0])

    def stay():
        return pltpu.make_async_copy(image_grad.at[me], place, plocal)

    def run(tokens):
        for token in tokens:
            if token == "s":
                for k in range(3):
                    swap(k).start()
                stay().start()
            else:
                scatter.act(token[0], *rounds[int(token[1:])])

    left = list(plan)

    def pause():
        run(left.pop(0))

    def copies(pairs, sem):
        made = [pltpu.make_async_copy(src, dst, sem.at[k]) for k, (src, dst) in enumerate(pairs)]
        for copy in made:
            copy.start()
        return made

    def done(made):
        for copy in made:
            copy.wait()

    p.met(barrier)

    def cross(flat):
        def attention(*scope):
            made = copies(list(zip((memory, query, cprobs, cctx, n2, r2, n1, grad_after, w_cq, w_co), scope)), fetch)
            pause()
            done(made)
            cross_backward(*scope[:10], norms, *scope[10:12], grad_self, g_second, flat, *scope[12:], scope[7], pause, 2)
            made = copies([(scope[10], g_cq), (scope[11], g_co)], store)
            pause()
            done(made)

        row = pltpu.VMEM(n1.shape, f32)
        pl.run_scoped(
            attention,
            *[pltpu.VMEM(r.shape, r.dtype) for r in (memory, query, cprobs, cctx, n2, r2, n1, grad_after, w_cq, w_co, g_cq, g_co)],
            row, row,
        )

        def weights(image_in, w_in, g_low, back, grad_mem):
            made = copies([(image, image_in), (w_kv, w_in)], fetch)
            pause()
            done(made)
            memory_backward(image_in, w_in, flat, g_low, back, grad_mem, pause, 1)
            made = copies([(g_low, g_kv)], store)
            count = image_grad.shape[1]

            def out(k, carry):
                rows = pl.ds(pl.multiple_of(k * here, here), here)
                pltpu.make_async_copy(back.at[rows], image_grad.at[k // count, k % count], store.at[1]).start()
                return carry

            lax.fori_loop(0, Y * C * count, out, 0)
            pause()
            done(made)
            pltpu.make_async_copy(back, back, store.at[1]).wait()

        pl.run_scoped(
            weights, pltpu.VMEM(image.shape, bf16), pltpu.VMEM(w_kv.shape, bf16), pltpu.VMEM(g_kv.shape, bf16),
            pltpu.VMEM(image.shape, bf16), pltpu.VMEM((image.shape[0], 2 * D), bf16),
        )

    pl.run_scoped(cross, pltpu.VMEM((2 * PAIRS, image.shape[0], PAIR), f32))

    def alone(*scope):
        made = copies(list(zip((text, mixed, probs, ctx, n1, r1, w_qkv, w_out), scope)), fetch)
        pause()
        done(made)
        text_in, mixed_in, probs_in, ctx_in, normed, inverse, w_mix, w_ctx, g_mix, g_ctx, back, *work = scope
        self_backward(
            text_in, mixed_in, probs_in, ctx_in, normed, inverse, grad_self, w_mix, w_ctx, norms, g_second, g_third,
            g_mix, g_ctx, back, g_blocks, *work, pause, 2, 1,
        )
        made = copies([(g_mix, g_qkv), (g_ctx, g_out), (back, text_grad)], store)
        pause()
        done(made)

    rows = text.shape[0]
    pl.run_scoped(
        alone, *[pltpu.VMEM(r.shape, r.dtype) for r in (text, mixed, probs, ctx, n1, r1, w_qkv, w_out, g_qkv, g_out, text_grad)],
        pltpu.VMEM((rows, 3 * D), f32), pltpu.VMEM((rows, D), f32), pltpu.VMEM((rows, 3 * D), f32), pltpu.VMEM((rows, 3 * D), bf16),
    )
    while left:
        pause()
    scatter.finish(outs)
    for k in range(3):
        swap(k).wait()
    stay().wait()


def backward_all(text, image, ws, norms, saved, grad_after, g_third, g_in, g_outer, slots,
                 plane_first=PLANE_LAST, turned=TURNED_BACK, rounds=ROUNDS, plan=BACK_PLAN, collective=1):
    nw = 8
    n = Z * X * Y * C
    every = Z * X * Y
    items = image.shape[0] // slots
    shapes = [w.shape for w in ws] + [g_in.shape, g_outer.shape, (n * 8, 128)]
    blocks = [(s[0] // n, s[1]) for s in shapes]
    kinds = [bf16] * (nw - 1) + [f32]
    anyspec = pl.BlockSpec(memory_space=pl.ANY)
    dma = pltpu.SemaphoreType.DMA
    shape = jax.ShapeDtypeStruct

    def room(line, plane, other=None):
        return [
            pltpu.VMEM((plane if w in plane_first else other or line if w in turned else line,) + b, k)
            for w, (b, k) in enumerate(zip(blocks, kinds))
        ]

    out = pl.pallas_call(
        functools.partial(backward_kernel, plane_first, turned, rounds, plan),
        out_shape=[shape(b, f32) for b in blocks]
        + [shape((slots // (Y * C), items * Y * C, ENC), bf16), shape(text.shape, f32)]
        + [shape(s, bf16) for s in shapes[:5]] + [shape((Y * C, slots // (Y * C), items, ENC), bf16)],
        in_specs=[VM] * 2 + [anyspec] * 21,
        out_specs=[VM] * nw + [anyspec] * 8,
        scratch_shapes=room(every, every) + room(every, every) + room(Z * Y, 1, Z) + room(Z, X, Z * X) + room(Z + 1, (Z + 1) * X * Y)
        + [pltpu.VMEM((n * 8, 128), f32), pltpu.VMEM(text.shape, f32), pltpu.VMEM((2, D), f32)]
        + [dma((nw, Z))] * 6 + [dma((nw,))] * 5 + [dma((3,)), dma((3,)), dma, dma((12,)), dma((4,))],
        compiler_params=pltpu.CompilerParams(collective_id=collective, has_side_effects=True, vmem_limit_bytes=60 << 20),
        name="backward",
    )(norms, g_third, text, image, *ws, *saved, grad_after, g_in, g_outer)
    return list(out[:nw]), out[nw], out[nw + 1]


step_rates = (0.05, 0.15, 0.05, 0.05, 0.3, 0.05, 0.05, 0.5)
step_decays = (0.01, 0.01, 0.01, 0.01, 0.01, 0.01, 0.01, 0.0)
BOTH = ("items", "patch")


def in_blocks(norms, count):
    width = D // count
    return jnp.pad(norms.reshape(6, count, width).transpose(1, 0, 2), ((0, 0), (0, 2), (0, 128 - width))).reshape(8 * count, 128)


def on_device(direct, text, cotangent, patches, text_lengths, patch_mask, *state):
    masters, firsts, seconds = state[:8], state[8:16], state[16:]
    group, local = patch_mask.shape
    chunks = lax.axis_size("patch")
    items = group // chunks
    devices = chunks * lax.axis_size("items")
    by_slot = patches.transpose(1, 0, 2)
    if direct:
        weights, image, norms, saved = forward_all(text, text_lengths, masters, by_slot, patch_mask, VALID)
    else:
        weights = [lax.all_gather(m.astype(bf16), BOTH, axis=0, tiled=True) for m in masters[:7]]
        blocks = in_blocks(lax.all_gather(masters[7].astype(bf16), BOTH, axis=1, tiled=True).astype(f32), devices)
        image = lax.all_to_all(by_slot.reshape(local, chunks, items, ENC), "patch", 1, 0)
        image = image.reshape(chunks * local * items, ENC)
        masks = patch_bias(patch_mask, lax.axis_index("patch") * local, VALID)
        masks = jnp.pad(masks, ((0, 0), (0, 128 - local))).reshape(chunks, items, 128)
        masks = lax.all_to_all(masks, "patch", 0, 0)
        norms, saved = forward_local(text, text_lengths, image, masks, weights, blocks)
    block_output, g_in, g_outer, grad_after, g_third = feed_forward_call(cotangent, weights[5:7], norms, saved[9])
    if direct:
        reduced, image_grad, text_grad = backward_all(
            text, image, weights[:5], norms, saved, grad_after, g_third, g_in, g_outer, chunks * local
        )
    else:
        text_grad, image_grad, grads, grad_blocks = backward_local(
            text, image, weights[:5], norms, saved, grad_after, g_third, devices
        )
        grads = (*grads, g_in, g_outer)
        reduced = [lax.psum_scatter(g, BOTH, scatter_dimension=0, tiled=True).astype(f32) for g in grads]
        reduced.append(lax.psum_scatter(grad_blocks, BOTH, scatter_dimension=0, tiled=True))
        image_grad = lax.all_to_all(image_grad.reshape(chunks, local, items, ENC), "patch", 0, 1)
        image_grad = image_grad.reshape(local, group, ENC)
    state_shapes = [(m.shape, f32) for m in masters]
    *updated, patch_grad = call(
        functools.partial(adamw, 8, step_decays, step_rates),
        (*masters, *firsts, *seconds, *reduced, image_grad),
        [*state_shapes * 3, (image_grad.shape, f32)], [], "adamw",
    )
    return (block_output, text_grad, patch_grad.transpose(1, 0, 2), *updated)


def solution(mesh):
    rows, cols = P(BOTH, None), P(None, BOTH)
    state = (*[rows] * 7, cols)
    direct = dict(mesh.shape) == {"items": Z * X, "patch": Y * C}
    return jax.shard_map(
        functools.partial(on_device, direct),
        mesh=mesh,
        in_specs=(rows, rows, P("items", "patch", None), P(BOTH), P("items", "patch"), *state * 3),
        out_specs=(rows, rows, P("items", "patch", None), *state * 3),
        check_vma=False,
    )
```

```python
import functools

import jax
import jax.numpy as jnp
from jax import lax
from jax.experimental import pallas as pl
from jax.experimental.pallas import tpu as pltpu
from jax.sharding import PartitionSpec as P

D = 768
HEADS = 12
HEAD_DIM = 64
ENC = 1024
TEXT = 40
VALID = 145
PAIR = 2 * HEAD_DIM
PAIRS = HEADS // 2
SCALE = HEAD_DIM ** (-0.5)
OUTSIDE = -1e30
bf16, f32 = jnp.bfloat16, jnp.float32


def dot(a, b):
    return jnp.dot(a, b, preferred_element_type=f32)


def dot_nt(a, b):
    return lax.dot_general(a, b, (((1,), (1,)), ((), ())), preferred_element_type=f32)


def dot_tn(a, b):
    return lax.dot_general(a, b, (((0,), (0,)), ((), ())), preferred_element_type=f32)


def quiet():
    pass


def chunks_of(count, parts, body, pause):
    def run(k, carry):
        body(k)
        return carry

    for part in range(parts):
        lax.fori_loop(count * part // parts, count * (part + 1) // parts, run, 0)
        if part < parts - 1:
            pause()


def tiles(total, step, body):
    def run(k, carry):
        body(pl.ds(pl.multiple_of(k * step, step), step))
        return carry

    lax.fori_loop(0, total // step, run, 0)


def norm_forward(values):
    center = values - jnp.mean(values, axis=-1, keepdims=True)
    inverse = lax.rsqrt(jnp.mean(center * center, axis=-1, keepdims=True) + 1e-12)
    return center * inverse, inverse


def norm_backward(grad_out, normed, inverse, gain):
    grad_gain = jnp.sum(grad_out * normed, axis=0, keepdims=True)
    grad_shift = jnp.sum(grad_out, axis=0, keepdims=True)
    scaled = grad_out * gain
    grad_values = inverse * (
        scaled
        - jnp.mean(scaled, axis=-1, keepdims=True)
        - normed * jnp.mean(scaled * normed, axis=-1, keepdims=True)
    )
    return grad_values, grad_gain, grad_shift


def low_half():
    return lax.broadcasted_iota(jnp.int32, (TEXT, PAIR), 1) < HEAD_DIM


def expand(rows):
    low = low_half()
    return jnp.concatenate(
        [jnp.where(low, rows, 0.0), jnp.where(low, 0.0, rows)], axis=0
    ).astype(bf16)


def fold(rows):
    return jnp.where(low_half(), rows[:TEXT], rows[TEXT:])


def softmax(scores):
    top = jnp.max(scores, axis=-1, keepdims=True)
    powers = jnp.exp(scores - top)
    return powers / jnp.sum(powers, axis=-1, keepdims=True)


def pair_cols(j, start=0):
    return slice(start + PAIR * j, start + PAIR * (j + 1))


def pair_rows(j):
    return slice(2 * TEXT * j, 2 * TEXT * (j + 1))


def attend_forward(query, keys, values, bias, probs, item, context, rows):
    js = range(PAIRS)
    scores = [dot_nt(expand(query(j)), keys(j)) * SCALE + bias for j in js]
    weights = [softmax(s) for s in scores]
    for j in js:
        probs[item, pair_rows(j), :] = weights[j]
    parts = [dot(weights[j].astype(bf16), values(j)) for j in js]
    for j in js:
        context[rows, pair_cols(j)] = fold(parts[j])


def attend_backward(query, keys, values, probs, item, grad_context, put_q, put_k, put_v):
    js = range(PAIRS)
    outer = [expand(grad_context(j)) for j in js]
    grads = [dot_nt(outer[j], values(j)) for j in js]
    inner = []
    for j in js:
        weights = probs[item, pair_rows(j), :]
        delta = jnp.sum(weights * grads[j], axis=-1, keepdims=True)
        inner.append((weights * (grads[j] - delta)).astype(bf16))
    for j in js:
        put_v(j, dot_tn(probs[item, pair_rows(j), :].astype(bf16), outer[j]))
    for j in js:
        put_q(j, fold(dot(inner[j], keys(j))) * SCALE)
    for j in js:
        put_k(j, dot_tn(inner[j], expand(query(j))) * SCALE)


def self_forward(lengths, text, w_qkv, w_out, blocks, mixed, probs, ctx, normed, inverse, norms, mix, context,
                 pause=quiet, parts=1):
    spread(blocks, norms)

    def project(cols):
        got = dot(text[...], w_qkv[:, cols]).astype(bf16)
        mixed[:, cols] = got
        mix[:, cols] = got.astype(f32)

    tiles(3 * D, 768, project)
    pause()
    position = lax.broadcasted_iota(jnp.int32, (1, TEXT), 1)

    def one(item):
        rows = pl.ds(pl.multiple_of(item * TEXT, 8), TEXT)
        bias = jnp.where(position < lengths[item], 0.0, -10000.0).astype(f32)
        attend_forward(
            lambda j: mix[rows, pair_cols(j)],
            lambda j: mix[rows, pair_cols(j, D)].astype(bf16),
            lambda j: mix[rows, pair_cols(j, 2 * D)].astype(bf16),
            bias, probs, item, context, rows,
        )

    chunks_of(probs.shape[0], parts, one, pause)
    pause()
    ctx[...] = context[...].astype(bf16)
    pre = text[...].astype(f32) + dot(ctx[...], w_out[...])
    n, r = norm_forward(pre)
    normed[...] = n
    inverse[...] = r


def self_backward(text, mixed, probs, ctx, normed, inverse, grad_after, w_qkv, w_out, norms, g_second, g_third,
                  g_qkv, g_out, text_grad, g_blocks, mix, grad_ctx, grad_mix, low_mix,
                  pause=quiet, parts=1, wide=1):
    grad_pre, grad_gain, grad_shift = norm_backward(grad_after[...], normed[...], inverse[...], norms[0:1, :])
    rows = jnp.concatenate([grad_gain, grad_shift, g_second[...], g_third[...], jnp.zeros((2, D), f32)], axis=0)
    count = g_blocks.shape[0] // 8
    width = D // count
    g_blocks[...] = jnp.zeros(g_blocks.shape, f32)
    for b in range(count):
        g_blocks[8 * b : 8 * b + 8, :width] = rows[:, width * b : width * (b + 1)]
    low = grad_pre.astype(bf16)
    g_out[...] = dot_tn(ctx[...], low).astype(bf16)
    grad_ctx[...] = dot_nt(low, w_out[...]).astype(bf16).astype(f32)
    text_grad[...] = grad_pre
    mix[...] = mixed[...].astype(f32)
    pause()

    def one(item):
        rows = pl.ds(pl.multiple_of(item * TEXT, 8), TEXT)

        def put(start):
            def store(j, value):
                grad_mix[rows, pair_cols(j, start)] = value
            return store

        attend_backward(
            lambda j: mix[rows, pair_cols(j)],
            lambda j: mix[rows, pair_cols(j, D)].astype(bf16),
            lambda j: mix[rows, pair_cols(j, 2 * D)].astype(bf16),
            probs, item, lambda j: grad_ctx[rows, pair_cols(j)],
            put(0), put(D), put(2 * D),
        )

    chunks_of(probs.shape[0], parts, one, pause)
    pause()
    low_mix[...] = grad_mix[...].astype(bf16)

    def weights(k):
        cols = pl.ds(pl.multiple_of(k * D, D), D)
        g_qkv[:, cols] = dot_tn(text[...], low_mix[:, cols]).astype(bf16)
        text_grad[...] += dot_nt(low_mix[:, cols], w_qkv[:, cols])

    chunks_of(3, wide, weights, pause)


def spread(blocks, norms):
    count = blocks.shape[0] // 8
    width = D // count
    for b in range(count):
        norms[:, width * b : width * (b + 1)] = blocks[8 * b : 8 * b + 8, :width]


def cross_forward(image, masks, w_kv, w_q, w_out, norms, normed_one,
                  memory, query, probs, ctx, normed, inverse, bias, context, wide, flat,
                  pause=quiet, tall=1, parts=1):
    items = masks.shape[1]
    slots = bias.shape[1]
    local = slots // masks.shape[0]
    for c in range(masks.shape[0]):
        bias[:, local * c : local * (c + 1)] = masks[c, :, :local]

    def project(k):
        got = dot(image[...], w_kv[:, pl.ds(pl.multiple_of(4 * PAIR * k, 4 * PAIR), 4 * PAIR)]).astype(bf16).astype(f32)
        for j in range(4):
            flat[4 * k + j] = got[:, pair_cols(j)]

    chunks_of(PAIRS // 2, tall, project, pause)
    pause()
    after = normed_one[...] * norms[0:1, :] + norms[1:2, :]
    low = dot(after.astype(bf16), w_q[...]).astype(bf16)
    query[...] = low
    wide[...] = low.astype(f32)

    def one(item):
        rows = pl.ds(pl.multiple_of(item * TEXT, 8), TEXT)
        every = pl.ds(item, slots, stride=items)
        for j in range(2 * PAIRS):
            memory[item, :, pair_cols(j)] = flat[j, every, :].astype(bf16)
        attend_forward(
            lambda j: wide[rows, pair_cols(j)],
            lambda j: memory[item, :, pair_cols(j)],
            lambda j: memory[item, :, pair_cols(j, D)],
            bias[pl.ds(item, 1), :], probs, item, context, rows,
        )

    chunks_of(items, parts, one, pause)
    pause()
    ctx[...] = context[...].astype(bf16)
    pre = after + dot(ctx[...], w_out[...])
    n, r = norm_forward(pre)
    normed[...] = n
    inverse[...] = r


def cross_backward(memory, query, probs, ctx, normed, inverse, normed_one, grad_after, w_q, w_out, norms,
                   g_q, g_out, grad_self, g_norm, flat, wide, grad_ctx, grad_q, pause=quiet, parts=1):
    items, slots = memory.shape[:2]
    grad_pre, grad_gain, grad_shift = norm_backward(grad_after[...], normed[...], inverse[...], norms[2:3, :])
    g_norm[0:1, :] = grad_gain
    g_norm[1:2, :] = grad_shift
    grad_self[...] = grad_pre
    low = grad_pre.astype(bf16)
    g_out[...] = dot_tn(ctx[...], low).astype(bf16)
    grad_ctx[...] = dot_nt(low, w_out[...]).astype(bf16).astype(f32)
    wide[...] = query[...].astype(f32)
    pause()

    def one(item):
        rows = pl.ds(pl.multiple_of(item * TEXT, 8), TEXT)
        every = pl.ds(item, slots, stride=items)

        def put_q(j, value):
            grad_q[rows, pair_cols(j)] = value

        def put(start):
            def store(j, value):
                flat[start + j, every, :] = value
            return store

        attend_backward(
            lambda j: wide[rows, pair_cols(j)],
            lambda j: memory[item, :, pair_cols(j)],
            lambda j: memory[item, :, pair_cols(j, D)],
            probs, item, lambda j: grad_ctx[rows, pair_cols(j)],
            put_q, put(0), put(PAIRS),
        )

    chunks_of(items, parts, one, pause)
    low_q = grad_q[...].astype(bf16)
    after = (normed_one[...] * norms[0:1, :] + norms[1:2, :]).astype(bf16)
    g_q[...] = dot_tn(after, low_q).astype(bf16)
    grad_self[...] += dot_nt(low_q, w_q[...])


def memory_backward(image, w_kv, flat, g_kv, image_grad, grad_mem, pause=quiet, wide=1):
    for j in range(2 * PAIRS):
        grad_mem[:, pair_cols(j)] = flat[j].astype(bf16)
    step = 4 * PAIR

    def weights(k):
        cols = pl.ds(pl.multiple_of(k * step, step), step)
        g_kv[:, cols] = dot_tn(image[...], grad_mem[:, cols]).astype(bf16)

    chunks_of(2 * D // step, wide, weights, pause)
    pause()

    def back(k):
        cols = pl.ds(pl.multiple_of(k * step, step), step)
        image_grad[:, cols] = dot_nt(grad_mem[...], w_kv[cols, :]).astype(bf16)

    chunks_of(ENC // step, 1, back, pause)


def feed_forward(normed_two, cotangent, w_inner, w_outer, norms,
                 block_output, g_inner, g_outer, grad_after, g_norm, low_in, hidden, slope, total, grad_low,
                 inner_in, outer_in, inner_out, outer_out, load, store):
    step = D
    count = w_inner.shape[1] // step

    def part(k):
        return pl.ds(pl.multiple_of(k * step, step), step)

    def loads(k):
        cols = part(k)
        return (
            pltpu.make_async_copy(w_inner.at[:, cols], inner_in.at[:, cols], load.at[0, k]),
            pltpu.make_async_copy(w_outer.at[cols], outer_in.at[cols], load.at[1, k]),
        )

    def stores(k):
        cols = part(k)
        return (
            pltpu.make_async_copy(inner_out.at[:, cols], g_inner.at[:, cols], store.at[0, k]),
            pltpu.make_async_copy(outer_out.at[cols], g_outer.at[cols], store.at[1, k]),
        )

    for k in range(count):
        for copy in loads(k):
            copy.start()
    after = normed_two[...] * norms[2:3, :] + norms[3:4, :]
    low_in[...] = after.astype(bf16)
    total[...] = after

    def up(k):
        cols = part(k)
        for copy in loads(k):
            copy.wait()
        pre = dot(low_in[...], inner_in[:, cols])
        bell = 0.5 * (1.0 + lax.erf(pre * (0.5 ** 0.5)))
        low = (pre * bell).astype(bf16)
        hidden[:, cols] = low
        slope[:, cols] = bell + pre * jnp.exp(-0.5 * pre * pre) * 0.3989422804014327
        total[...] += dot(low, outer_in[cols, :])

    chunks_of(count, 1, up, quiet)
    n, r = norm_forward(total[...])
    gain = norms[4:5, :]
    block_output[...] = (n * gain + norms[5:6, :]).astype(bf16)
    grad_pre, grad_gain, grad_shift = norm_backward(cotangent[...].astype(f32), n, r, gain)
    g_norm[0:1, :] = grad_gain
    g_norm[1:2, :] = grad_shift
    grad_after[...] = grad_pre
    grad_low[...] = grad_pre.astype(bf16)

    def down(k):
        cols = part(k)
        low = (dot_nt(grad_low[...], outer_in[cols, :]) * slope[:, cols]).astype(bf16)
        inner_out[:, cols] = dot_tn(low_in[...], low).astype(bf16)
        outer_out[cols, :] = dot_tn(hidden[:, cols], grad_low[...]).astype(bf16)
        for copy in stores(k):
            copy.start()
        grad_after[...] += dot_nt(low, inner_in[:, cols])

    chunks_of(count, 1, down, quiet)
    for k in range(count):
        for copy in stores(k):
            copy.wait()


VM = pl.BlockSpec(memory_space=pltpu.VMEM)


def call(body, args, outs, scratch, name, smem=0, limit=60 << 20, left=(), sems=()):
    def where(k):
        return pl.BlockSpec(memory_space=pl.ANY) if k in left else VM

    return pl.pallas_call(
        body,
        out_shape=[jax.ShapeDtypeStruct(s, k) for s, k in outs],
        in_specs=[pl.BlockSpec(memory_space=pltpu.SMEM)] * smem + [where(k) for k in range(smem, len(args))],
        out_specs=[where(len(args) + k) for k in range(len(outs))],
        scratch_shapes=[pltpu.VMEM(s, k) for s, k in scratch] + [pltpu.SemaphoreType.DMA(s) for s in sems],
        compiler_params=pltpu.CompilerParams(vmem_limit_bytes=limit),
        name=name,
    )(*args)


def adamw(count, decays, rates, *refs):
    masters, firsts, seconds, grads = (refs[count * i : count * (i + 1)] for i in range(4))
    image_low = refs[4 * count]
    new_m, new_f, new_s = (refs[4 * count + 1 + count * i : 4 * count + 1 + count * (i + 1)] for i in range(3))
    image_grad = refs[7 * count + 1]
    for k in range(count):
        rows, cols = masters[k].shape
        gradient = grads[k][:rows, :cols]
        first = 0.9 * firsts[k][...] + 0.1 * gradient
        second = 0.999 * seconds[k][...] + 0.001 * gradient * gradient
        step = first / (1.0 - 0.9**10) / (jnp.sqrt(second / (1.0 - 0.999**10)) + 1e-08)
        master = masters[k][...]
        new_m[k][...] = master - rates[k] * (step + decays[k] * master)
        new_f[k][...] = first
        new_s[k][...] = second
    image_grad[...] = image_low[...].astype(f32)


def forward_local(text, lengths, image, masks, ws, blocks):
    w_qkv, w_out, w_cq, w_kv, w_co = ws[:5]
    rows = text.shape[0]
    items = rows // TEXT
    slots = image.shape[0] // items
    pairs = HEADS * TEXT
    row = ((rows, D), f32)
    rowl = ((rows, D), bf16)
    one = ((rows, 1), f32)
    *first, norms = call(
        self_forward, (lengths, text, w_qkv, w_out, blocks),
        [((rows, 3 * D), bf16), ((items, pairs, TEXT), f32), rowl, row, one, ((8, D), f32)],
        [((rows, 3 * D), f32), row], "self_forward", smem=1)
    second = call(
        cross_forward, (image, masks, w_kv, w_cq, w_co, norms, first[3]),
        [((items, slots, 2 * D), bf16), rowl, ((items, pairs, slots), f32), rowl, row, one],
        [((items, slots), f32), row, row, ((2 * PAIRS, items * slots, PAIR), f32)], "cross_forward")
    return norms, [*first, *second]


def feed_forward_call(cotangent, ws, norms, n2):
    w_in, w_outer = ws
    rows, ff = n2.shape[0], w_in.shape[1]
    row = ((rows, D), f32)
    rowl = ((rows, D), bf16)
    return call(
        feed_forward, (n2, cotangent, w_in, w_outer, norms),
        [rowl, ((D, ff), bf16), ((ff, D), bf16), row, ((2, D), f32)],
        [rowl, ((rows, ff), bf16), ((rows, ff), f32), row, rowl, *[(w.shape, bf16) for w in (w_in, w_outer)] * 2],
        "feed_forward", left=(2, 3, 6, 7), sems=[(2, ff // D)] * 2)


def backward_local(text, image, ws, norms, saved, grad_after, gn3, count):
    w_qkv, w_out, w_cq, w_kv, w_co = ws
    mixed, probs, ctx, n1, r1, memory, query, cprobs, cctx, n2, r2 = saved
    rows = text.shape[0]
    row = ((rows, D), f32)
    flat = (2 * PAIRS, image.shape[0], PAIR)
    g_cq, g_co, grad_self, gn2, flat_grad = call(
        cross_backward, (memory, query, cprobs, cctx, n2, r2, n1, grad_after, w_cq, w_co, norms),
        [((D, D), bf16), ((D, D), bf16), row, ((2, D), f32), (flat, f32)], [row, row, row], "cross_backward")
    g_kv, image_grad = call(
        memory_backward, (image, w_kv, flat_grad), [((ENC, 2 * D), bf16), (image.shape, bf16)],
        [((image.shape[0], 2 * D), bf16)], "memory_backward")
    g_qkv, g_out, text_grad, g_blocks = call(
        self_backward, (text, mixed, probs, ctx, n1, r1, grad_self, w_qkv, w_out, norms, gn2, gn3),
        [((D, 3 * D), bf16), ((D, D), bf16), row, ((count * 8, 128), f32)],
        [((rows, 3 * D), f32), row, ((rows, 3 * D), f32), ((rows, 3 * D), bf16)], "self_backward")
    return text_grad, image_grad, (g_qkv, g_out, g_cq, g_kv, g_co), g_blocks


MESH = pl.DeviceIdType.MESH
Z, X, Y, C = 4, 2, 2, 2
PLANE_FIRST, TURNED = (0,), (6,)
SETS = ((0, 1, 7, 3, 2, 4), (5, 6))
PLAN = (
    ("0", "00", "01", "1", "02", "swap", "03", "10", "04", "11", "05", "06", "swapped"),
    (("12",),),
    (),
    (("13",), (), ("14",), ("15",)),
    ("16",),
)
PLANE_LAST, TURNED_BACK = (3,), (6,)
ROUNDS = tuple((k, ws) for ws in ((5, 6), (3, 2, 4), (0, 1, 7)) for k in range(4))
BACK_PLAN = (
    ("b0", "b1", "c0", "b2"),
    ("c1", "b3"),
    ("c2", "a0"),
    ("c3", "a1"),
    ("a2",),
    ("d0", "a3"),
    ("d1",),
    ("b4", "b5", "s", "d2"),
    ("c4", "e4", "b6"),
    ("c5", "e5", "a4", "b7"),
    ("c6", "e6", "a5", "d3"),
    ("c7", "a6", "m4"),
    ("b8", "b9", "c8", "b10", "c9", "b11", "a7", "a8", "c10", "d4", "m5", "d5", "a9", "c11", "m6", "d6", "d8", "a10", "p7", "d7", "d9", "a11", "q7", "d10", "d11"),
)
bf16, f32 = jnp.bfloat16, jnp.float32


class Place:
    def __init__(self):
        item, self.me = lax.axis_index("items"), lax.axis_index("patch")
        self.z, self.x, self.y, self.c = item // X, item % X, self.me // C, self.me % C
        z, x, y, c = self.z, self.x, self.y, self.c
        self.left = (item - X, self.me)
        self.right = (item + X, self.me)
        self.xdev = (z * X + (1 - x), self.me)
        self.ypeer, self.cpeer, self.dpeer = (1 - y) * C + c, y * C + (1 - c), (1 - y) * C + (1 - c)
        self.ydev, self.cdev, self.ddev = (item, self.ypeer), (item, self.cpeer), (item, self.dpeer)

    def at(self, zz, xx, yy, cc):
        return ((zz * X + xx) * Y + yy) * C + cc

    def greet(self, barrier):
        for dev in (self.xdev, self.ydev, self.cdev, self.ddev):
            pl.semaphore_signal(barrier, inc=1, device_id=dev, device_id_type=MESH)

        @pl.when(self.z > 0)
        def _():
            pl.semaphore_signal(barrier, inc=1, device_id=self.left, device_id_type=MESH)

        @pl.when(self.z < Z - 1)
        def _():
            pl.semaphore_signal(barrier, inc=1, device_id=self.right, device_id_type=MESH)

    def met(self, barrier):
        pl.semaphore_wait(barrier, 4 + (self.z > 0).astype(jnp.int32) + (self.z < Z - 1).astype(jnp.int32))

    def both(self, d, step):
        if d == 0:
            step(self.z, None)
            return

        @pl.when(self.z >= d)
        def _():
            step(self.z - d, True)

        @pl.when(self.z + d < Z)
        def _():
            step(self.z + d, False)


def patch_bias(mask, first, valid):
    index = first + lax.broadcasted_iota(jnp.int32, mask.shape, 1)
    return jnp.where((mask > 0) & (index < valid), 0.0, -10000.0).astype(f32)


class Gather:
    def __init__(self, place, plane_first, turned, low, outs, recv, to_x, to_y, to_c, to_l, to_r, local):
        self.place, self.plane_first, self.turned = place, plane_first, turned
        self.low, self.outs, self.recv, self.local = low, outs, recv, local
        self.sems = {"x": to_x, "y": to_y, "c": to_c, "l": to_l, "r": to_r}
        self.devs = {"x": place.xdev, "y": place.ydev, "c": place.cdev, "l": place.left, "r": place.right}
        self.mine = place.at(place.z, place.x, place.y, place.c)

    def blocks(self, w, first, count=1):
        rows = self.low[w].shape[0]
        return self.outs[w].at[pl.ds(pl.multiple_of(first * rows, rows), count * rows)]

    def copy(self, w, block, way, own=False):
        return pltpu.make_async_remote_copy(
            src_ref=self.low[w] if own else self.blocks(w, block),
            dst_ref=self.blocks(w, block),
            send_sem=self.sems[way].at[w],
            recv_sem=self.recv.at[w, block],
            device_id=self.devs[way],
            device_id_type=MESH,
        )

    def send(self, w, block, ways, own=False):
        z = self.place.z
        for way in ways:
            if way == "l":
                @pl.when(z > 0)
                def _():
                    self.copy(w, block, "l", own).start()
            elif way == "r":
                @pl.when(z < Z - 1)
                def _():
                    self.copy(w, block, "r", own).start()
            else:
                self.copy(w, block, way, own).start()

    def arrived(self, w, block):
        self.copy(w, block, "x").wait_recv()

    def pass_on(self, w, block, ways):
        self.arrived(w, block)
        self.send(w, block, ways)

    def keep(self, w):
        return pltpu.make_async_copy(self.low[w], self.blocks(w, self.mine), self.local.at[w])

    def start(self, ws):
        for w in ws:
            self.send(w, self.mine, "xylr" if w in self.plane_first else "lryx", True)
        for w in ws:
            self.send(w, self.mine, "c", True)
            self.keep(w).start()

    def stages(self, ws):
        p = self.place
        x, y, c = p.x, p.y, p.c
        line = [w for w in ws if w not in self.plane_first]
        plane = [w for w in ws if w in self.plane_first]

        def plane_x():
            for w in plane:
                self.pass_on(w, p.at(p.z, 1 - x, y, c), "ylrc")

        def plane_y():
            for xx in (x, 1 - x):
                for w in plane:
                    self.pass_on(w, p.at(p.z, xx, 1 - y, c), "lrc")

        def plane_z(zz, from_left):
            for xx, yy in ((x, y), (1 - x, y), (x, 1 - y), (1 - x, 1 - y)):
                for w in plane:
                    self.pass_on(w, p.at(zz, xx, yy, c), "rc" if from_left else "lc")

        def line_z(zz, from_left):
            for w in line:
                self.pass_on(w, p.at(zz, x, y, c), "ryxc" if from_left else "lyxc")

        def line_y(zz, _):
            for w in line:
                if w in self.turned:
                    self.pass_on(w, p.at(zz, 1 - x, y, c), "yc")
                else:
                    self.pass_on(w, p.at(zz, x, 1 - y, c), "xc")

        def line_x(zz, _):
            for near in (True, False):
                for w in line:
                    if w in self.turned:
                        self.pass_on(w, p.at(zz, x if near else 1 - x, 1 - y, c), "c")
                    else:
                        self.pass_on(w, p.at(zz, 1 - x, y if near else 1 - y, c), "c")

        def from_core():
            for zz in range(Z):
                for xx in range(X):
                    for yy in range(Y):
                        for w in ws:
                            self.arrived(w, p.at(zz, xx, yy, 1 - c))
            for w in ws:
                self.keep(w).wait()

        def steps(*pairs):
            def run():
                for d, step in pairs:
                    if d is None:
                        step()
                    else:
                        p.both(d, step)
            return run

        first = [(None, plane_x)] if plane else []
        second = [(None, plane_y)] if plane else []

        def deep(d):
            return [(d, plane_z)] if plane else []

        if not line:
            return [steps(*first), steps(*second), steps(*deep(1)), steps(*deep(2)), steps(*deep(3)), quiet, from_core]
        return [
            steps(*first, (1, line_z)),
            steps(*second, (0, line_y)),
            steps(*deep(1), (2, line_z), (1, line_y), (0, line_x)),
            steps(*deep(2), (3, line_z), (2, line_y), (1, line_x)),
            steps(*deep(3), (3, line_y), (2, line_x)),
            steps((3, line_x)),
            from_core,
        ]

    def finish(self):
        z = self.place.z
        for w in range(len(self.low)):
            def sent(count, way):
                span = self.blocks(w, 0, count)
                pltpu.make_async_copy(span, span, self.sems[way].at[w]).wait()

            plane = w in self.plane_first
            wide = X * Y if plane else 1
            turned = w in self.turned
            sent(1 if plane else Z if turned else Z * Y, "x")
            sent(X if plane else Z * X if turned else Z, "y")
            sent(Z * X * Y, "c")
            for k in range(Z):
                @pl.when(z == k)
                def _():
                    if k > 0:
                        sent(wide * (Z - k), "l")
                    if k < Z - 1:
                        sent(wide * (k + 1), "r")


def forward_kernel(plane_first, turned, sets, plan, valid, *refs):
    nw = 8
    refs = list(refs)

    def take(count):
        got = refs[:count]
        del refs[:count]
        return got

    (lengths,), shards, (image, mask, text) = take(1), take(nw), take(3)
    whole, (image_out, norms) = take(nw - 1), take(2)
    saved = take(11)
    low, (blocks, masks, bias_here) = take(nw), take(3)
    w_qkv, w_out, w_cq, w_kv, w_co = take(5)
    image_in, mix, context, bias, wide, flat = take(6)
    kept = take(11)
    recv, to_x, to_y, to_c, to_l, to_r, local, psend, precv, plocal, load, save = take(12)
    p = Place()
    me = p.me
    barrier = pltpu.get_barrier_semaphore()
    p.greet(barrier)
    for w in range(nw - 1):
        low[w][...] = shards[w][...].astype(low[w].dtype)
    low[nw - 1][...] = jnp.zeros(low[nw - 1].shape, f32)
    rows, cols = shards[nw - 1].shape
    low[nw - 1][:rows, :cols] = shards[nw - 1][...].astype(bf16).astype(f32)
    slots = mask.shape[1]
    bias_here[...] = jnp.zeros(bias_here.shape, f32)
    bias_here[:, :slots] = patch_bias(mask[...], me * slots, valid)
    here = mask.shape[0] // (Y * C)
    peers = ((p.ydev, p.ypeer), (p.cdev, p.cpeer), (p.ddev, p.dpeer))
    swaps = (image_out, masks)

    def part(s, peer):
        rows = pl.ds(pl.multiple_of(peer * here, here), here)
        return bias_here.at[rows] if s else image.at[:, rows]

    def swap(s, k):
        dev, peer = peers[k]
        return pltpu.make_async_remote_copy(
            src_ref=part(s, peer),
            dst_ref=swaps[s].at[me],
            send_sem=psend.at[s, k],
            recv_sem=precv.at[s, k],
            device_id=dev,
            device_id_type=MESH,
        )

    def stay(s):
        return pltpu.make_async_copy(part(s, me), swaps[s].at[me], plocal.at[s])

    gather = Gather(p, plane_first, turned, low, [*whole, blocks], recv, to_x, to_y, to_c, to_l, to_r, local)
    staged = [gather.stages(ws) for ws in sets]
    p.met(barrier)

    def start_swaps():
        for s in range(2):
            for k in range(3):
                swap(s, k).start()
            stay(s).start()

    def end_swaps():
        for s in range(2):
            for k in range(3):
                swap(s, k).wait()
            stay(s).wait()

    def loads(pairs):
        return [pltpu.make_async_copy(src, dst, load.at[k]) for k, src, dst in pairs]

    early = loads([(0, whole[0], w_qkv), (1, whole[1], w_out)])
    late = loads([(2, whole[2], w_cq), (3, whole[3], w_kv), (4, whole[4], w_co)])

    def flatten(k, carry):
        rows = pl.ds(pl.multiple_of(k * here, here), here)
        pltpu.make_async_copy(image_out.at[k // slots, k % slots], image_in.at[rows], load.at[5]).start()
        return carry
    saves = [pltpu.make_async_copy(src, dst, save.at[k]) for k, (src, dst) in enumerate(zip(kept, saved))]

    def run(tokens):
        for token in tokens:
            if token == "swap":
                start_swaps()
            elif token == "swapped":
                end_swaps()
            elif len(token) == 1:
                gather.start(sets[int(token)])
            else:
                staged[int(token[0])][int(token[1])]()

    def queue(events):
        left = list(events)

        def pause():
            if left:
                run(left.pop(0))

        return pause

    before, during_self, between, during_cross, after = plan
    run(before)
    for copy in early:
        copy.start()
    for copy in early:
        copy.wait()
    mixed, probs, ctx, normed, inverse, memory, query, cross_probs, cross_ctx, normed_two, inverse_two = kept
    self_forward(
        lengths, text, w_qkv, w_out, blocks, mixed, probs, ctx, normed, inverse, norms, mix, context,
        queue(during_self), 2,
    )
    for copy in saves[:5]:
        copy.start()
    run(between)
    for copy in late:
        copy.start()
    lax.fori_loop(0, Y * C * slots, flatten, 0)
    for copy in late:
        copy.wait()
    pltpu.make_async_copy(image_in, image_in, load.at[5]).wait()
    cross_forward(
        image_in, masks, w_kv, w_cq, w_co, norms, normed,
        memory, query, cross_probs, cross_ctx, normed_two, inverse_two, bias, context, wide, flat,
        queue(during_cross), 2, 4,
    )
    for copy in saves[5:]:
        copy.start()
    run(after)
    gather.finish()
    for copy in saves:
        copy.wait()


def forward_all(text, lengths, shards, image, mask, valid, plane_first=PLANE_FIRST, turned=TURNED, sets=SETS, plan=PLAN, collective=0):
    nw = len(shards)
    n = Z * X * Y * C
    shapes = [s.shape for s in shards[:-1]] + [(8, 128)]
    kinds = [bf16] * (nw - 1) + [f32]
    slots, group, width = image.shape
    items = group // (Y * C)
    rows = text.shape[0]
    every = slots * Y * C
    pairs = HEADS * TEXT
    row, low_row, one = ((rows, D), f32), ((rows, D), bf16), ((rows, 1), f32)
    keep = [
        ((rows, 3 * D), bf16), ((items, pairs, TEXT), f32), low_row, row, one,
        ((items, every, 2 * D), bf16), low_row, ((items, pairs, every), f32), low_row, row, one,
    ]
    anyspec = pl.BlockSpec(memory_space=pl.ANY)
    dma = pltpu.SemaphoreType.DMA
    shape = jax.ShapeDtypeStruct
    out = pl.pallas_call(
        functools.partial(forward_kernel, plane_first, turned, sets, plan, valid),
        out_shape=[shape((n * s[0], s[1]), bf16) for s in shapes[:-1]]
        + [shape((Y * C, slots, items, width), image.dtype), shape((8, D), f32)]
        + [shape(*k) for k in keep],
        in_specs=[pl.BlockSpec(memory_space=pltpu.SMEM)] + [VM] * nw + [anyspec, VM, VM],
        out_specs=[anyspec] * nw + [VM] + [anyspec] * len(keep),
        scratch_shapes=[pltpu.VMEM(s, k) for s, k in zip(shapes, kinds)]
        + [pltpu.VMEM((n * 8, 128), f32), pltpu.VMEM((Y * C, items, 128), f32), pltpu.VMEM((group, 128), f32)]
        + [pltpu.VMEM((n * shapes[w][0], shapes[w][1]), bf16) for w in range(5)]
        + [pltpu.VMEM(s, k) for s, k in (
            ((every * items, width), bf16), ((rows, 3 * D), f32), row, ((items, every), f32), row,
            ((2 * PAIRS, items * every, PAIR), f32), *keep)]
        + [dma((nw, n))] + [dma((nw,))] * 6 + [dma((2, 3)), dma((2, 3)), dma((2,)), dma((6,)), dma((len(keep),))],
        compiler_params=pltpu.CompilerParams(collective_id=collective, has_side_effects=True, vmem_limit_bytes=60 << 20),
        name="forward",
    )(lengths, *shards, image, mask, text)
    return out[: nw - 1], out[nw - 1].reshape(every * items, width), out[nw], out[nw + 1 :]


class Scatter:
    def __init__(self, place, plane_first, turned, grads, own, from_core, from_x, from_y, from_z, sems):
        self.place, self.plane_first, self.turned, self.grads, self.own = place, plane_first, turned, grads, own
        self.from_core, self.from_x, self.from_y, self.from_z = from_core, from_x, from_y, from_z
        self.load, self.rcore, self.rx, self.ry, self.rl, self.rr, self.score, self.sx, self.sy, self.sl, self.sr = sems

    def target(self, k):
        half = self.place.z // 2
        near = self.place.z * (1 - half) + (Z - 1 - self.place.z) * half
        return half * (Z - 1) + (1 - 2 * half) * (Z - 1, 2 - 2 * near, 1 + near, near)[k]

    def copy(self, src, dst, send_sem, recv_sem, dev):
        return pltpu.make_async_remote_copy(
            src_ref=src, dst_ref=dst, send_sem=send_sem, recv_sem=recv_sem, device_id=dev, device_id_type=MESH
        )

    def arrived(self, dst, sem):
        self.copy(dst, dst, self.score.at[0], sem, self.place.cdev).wait_recv()

    def block(self, w, b):
        rows = self.own[w].shape[1]
        return self.grads[w].at[pl.ds(pl.multiple_of(b * rows, rows), rows)]

    def add(self, w, at, count, ref, start):
        mine = self.own[w]

        def one(i, carry):
            mine[at + i] = (mine[at + i].astype(f32) + ref[start + i].astype(f32)).astype(mine.dtype)
            return carry

        if count == 1:
            one(0, 0)
        else:
            lax.fori_loop(0, count, one, 0)

    def begin(self, k, ws):
        t, c = self.target(k), self.place.c
        for w in ws:
            for s in range(X * Y):
                q = t * X * Y + s
                pltpu.make_async_copy(self.block(w, q * C + c), self.own[w].at[q], self.load.at[w, t]).start()
                self.copy(
                    self.block(w, q * C + 1 - c), self.from_core[w].at[q], self.score.at[w], self.rcore.at[w, t], self.place.cdev
                ).start()

    def core(self, k, ws):
        t, p = self.target(k), self.place
        span = pl.ds(t * X * Y, X * Y)
        for w in ws:
            mine = self.own[w].at[span]
            pltpu.make_async_copy(mine, mine, self.load.at[w, t]).wait()
            self.arrived(self.from_core[w].at[span], self.rcore.at[w, t])
            self.add(w, t * X * Y, X * Y, self.from_core[w], t * X * Y)
            if w in self.turned:
                for xx in range(X):
                    self.copy(
                        self.own[w].at[(t * X + xx) * Y + 1 - p.y], self.from_y[w].at[t * X + xx],
                        self.sy.at[w], self.ry.at[w, t], p.ydev,
                    ).start()
            elif w not in self.plane_first:
                self.copy(
                    self.own[w].at[pl.ds((t * X + 1 - p.x) * Y, Y)], self.from_x[w].at[pl.ds(t * Y, Y)],
                    self.sx.at[w], self.rx.at[w, t], p.xdev,
                ).start()

    def across(self, k, ws):
        t, p = self.target(k), self.place
        for w in ws:
            if w in self.turned:
                self.arrived(self.from_y[w].at[pl.ds(t * X, X)], self.ry.at[w, t])
                for xx in range(X):
                    self.add(w, (t * X + xx) * Y + p.y, 1, self.from_y[w], t * X + xx)
                self.copy(
                    self.own[w].at[(t * X + 1 - p.x) * Y + p.y], self.from_x[w].at[t], self.sx.at[w], self.rx.at[w, t], p.xdev
                ).start()
                continue
            self.arrived(self.from_x[w].at[pl.ds(t * Y, Y)], self.rx.at[w, t])
            self.add(w, (t * X + p.x) * Y, Y, self.from_x[w], t * Y)
            self.copy(
                self.own[w].at[(t * X + p.x) * Y + 1 - p.y], self.from_y[w].at[t], self.sy.at[w], self.ry.at[w, t], p.ydev
            ).start()

    def along(self, k, ws, first, count):
        t, z = self.target(k), self.place.z

        def span(w):
            return self.own[w].at[pl.ds(first(t), count)]

        def slot(w, s):
            return self.from_z[w].at[pl.ds(s * count, count)]

        def take(w, s, sem):
            self.arrived(slot(w, s), sem.at[w, t])
            self.add(w, first(t), count, self.from_z[w], s * count)

        if k < Z - 1:
            @pl.when(t > z)
            def _():
                for w in ws:
                    @pl.when(z > 0)
                    def _():
                        take(w, t, self.rl)

                    self.copy(span(w), slot(w, t), self.sr.at[w], self.rl.at[w, t], self.place.right).start()

            @pl.when(t < z)
            def _():
                there = t + (Z - t) * (t == z - 1).astype(jnp.int32)
                for w in ws:
                    @pl.when(z < Z - 1)
                    def _():
                        take(w, t, self.rr)

                    self.copy(span(w), slot(w, there), self.sl.at[w], self.rr.at[w, t], self.place.left).start()
        else:
            for w in ws:
                @pl.when(z > 0)
                def _():
                    take(w, t, self.rl)

                @pl.when(z < Z - 1)
                def _():
                    take(w, Z, self.rr)

    def down(self, k, ws):
        t, p = self.target(k), self.place
        for w in ws:
            ref, sem = (self.from_x, self.rx) if w in self.turned else (self.from_y, self.ry)
            self.arrived(ref[w].at[t], sem.at[w, t])
            self.add(w, (t * X + p.x) * Y + p.y, 1, ref[w], t)
        self.along(k, ws, lambda t: (t * X + p.x) * Y + p.y, 1)

    def plane(self, k, ws):
        p = self.place
        self.along(k, ws, lambda t: t * X * Y, X * Y)
        if k == Z - 1:
            for w in ws:
                for xx in range(X):
                    self.copy(
                        self.own[w].at[(p.z * X + xx) * Y + 1 - p.y], self.from_y[w].at[xx], self.sy.at[w], self.ry.at[w, xx], p.ydev
                    ).start()

    def plane_across(self, ws):
        p = self.place
        for w in ws:
            for xx in range(X):
                self.arrived(self.from_y[w].at[xx], self.ry.at[w, xx])
                self.add(w, (p.z * X + xx) * Y + p.y, 1, self.from_y[w], xx)
            self.copy(
                self.own[w].at[(p.z * X + 1 - p.x) * Y + p.y], self.from_x[w].at[0], self.sx.at[w], self.rx.at[w, 0], p.xdev
            ).start()

    def act(self, name, k, ws):
        line = [w for w in ws if w not in self.plane_first]
        plane = [w for w in ws if w in self.plane_first]
        z = self.place.z
        if name == "b":
            self.begin(k, ws)
        elif name == "c":
            self.core(k, ws)
        elif name == "a":
            self.across(k, line)
        elif name == "d":
            self.down(k, line)
        elif name == "e":
            @pl.when((z == 0) | (z == Z - 1))
            def _():
                self.plane(k, plane)
        elif name == "m":
            @pl.when((z > 0) & (z < Z - 1))
            def _():
                self.plane(k, plane)
        elif name == "p":
            self.plane(k, plane)
        elif name == "q":
            self.plane_across(plane)

    def finish(self, outs):
        p = self.place
        at = (p.z * X + p.x) * Y + p.y
        for w, out in enumerate(outs):
            plane = w in self.plane_first
            total = self.own[w][at].astype(f32)
            if plane:
                self.arrived(self.from_x[w].at[0], self.rx.at[w, 0])
                total = total + self.from_x[w][0].astype(f32)
            out[...] = total

            def sent(count, sem):
                span = self.own[w].at[pl.ds(0, count)]
                pltpu.make_async_copy(span, span, sem.at[w]).wait()

            sent(Z * X * Y, self.score)
            turned = w in self.turned
            sent(1 if plane else Z if turned else Z * Y, self.sx)
            sent(X if plane else Z * X if turned else Z, self.sy)
            per = X * Y if plane else 1
            for k in range(Z):
                @pl.when(p.z == k)
                def _():
                    if k > 0:
                        sent(per * k, self.sl)
                    if k < Z - 1:
                        sent(per * (Z - 1 - k), self.sr)


def backward_kernel(plane_first, turned, rounds, plan, *refs):
    nw = 8
    refs = list(refs)

    def take(count):
        got = refs[:count]
        del refs[:count]
        return got

    norms, g_third = take(2)
    text, image, w_qkv, w_out, w_cq, w_kv, w_co = take(7)
    mixed, probs, ctx, n1, r1, memory, query, cprobs, cctx, n2, r2 = take(11)
    grad_after, g_in, g_outer = take(3)
    outs, (swapped, text_grad) = take(nw), take(2)
    g_qkv, g_out, g_cq, g_kv, g_co, image_grad = take(6)
    own, from_core, from_x, from_y, from_z = (take(nw) for _ in range(5))
    g_blocks, grad_self, g_second = take(3)
    sems = take(11)
    psend, precv, plocal, fetch, store = take(5)
    p = Place()
    me = p.me
    barrier = pltpu.get_barrier_semaphore()
    p.greet(barrier)
    scatter = Scatter(
        p, plane_first, turned, [g_qkv, g_out, g_cq, g_kv, g_co, g_in, g_outer, g_blocks], own, from_core, from_x, from_y, from_z, sems
    )
    here = swapped.shape[1] // (Y * C)
    place = swapped.at[:, pl.ds(pl.multiple_of(me * here, here), here)]
    peers = ((p.ydev, p.ypeer), (p.cdev, p.cpeer), (p.ddev, p.dpeer))

    def swap(k):
        return scatter.copy(image_grad.at[peers[k][1]], place, psend.at[k], precv.at[k], peers[k][0])

    def stay():
        return pltpu.make_async_copy(image_grad.at[me], place, plocal)

    def run(tokens):
        for token in tokens:
            if token == "s":
                for k in range(3):
                    swap(k).start()
                stay().start()
            else:
                scatter.act(token[0], *rounds[int(token[1:])])

    left = list(plan)

    def pause():
        run(left.pop(0))

    def copies(pairs, sem):
        made = [pltpu.make_async_copy(src, dst, sem.at[k]) for k, (src, dst) in enumerate(pairs)]
        for copy in made:
            copy.start()
        return made

    def done(made):
        for copy in made:
            copy.wait()

    p.met(barrier)

    def cross(flat):
        def attention(*scope):
            made = copies(list(zip((memory, query, cprobs, cctx, n2, r2, n1, grad_after, w_cq, w_co), scope)), fetch)
            pause()
            done(made)
            cross_backward(*scope[:10], norms, *scope[10:12], grad_self, g_second, flat, *scope[12:], scope[7], pause, 2)
            made = copies([(scope[10], g_cq), (scope[11], g_co)], store)
            pause()
            done(made)

        row = pltpu.VMEM(n1.shape, f32)
        pl.run_scoped(
            attention,
            *[pltpu.VMEM(r.shape, r.dtype) for r in (memory, query, cprobs, cctx, n2, r2, n1, grad_after, w_cq, w_co, g_cq, g_co)],
            row, row,
        )

        def weights(image_in, w_in, g_low, back, grad_mem):
            made = copies([(image, image_in), (w_kv, w_in)], fetch)
            pause()
            done(made)
            memory_backward(image_in, w_in, flat, g_low, back, grad_mem, pause, 1)
            made = copies([(g_low, g_kv)], store)
            count = image_grad.shape[1]

            def out(k, carry):
                rows = pl.ds(pl.multiple_of(k * here, here), here)
                pltpu.make_async_copy(back.at[rows], image_grad.at[k // count, k % count], store.at[1]).start()
                return carry

            lax.fori_loop(0, Y * C * count, out, 0)
            pause()
            done(made)
            pltpu.make_async_copy(back, back, store.at[1]).wait()

        pl.run_scoped(
            weights, pltpu.VMEM(image.shape, bf16), pltpu.VMEM(w_kv.shape, bf16), pltpu.VMEM(g_kv.shape, bf16),
            pltpu.VMEM(image.shape, bf16), pltpu.VMEM((image.shape[0], 2 * D), bf16),
        )

    pl.run_scoped(cross, pltpu.VMEM((2 * PAIRS, image.shape[0], PAIR), f32))

    def alone(*scope):
        made = copies(list(zip((text, mixed, probs, ctx, n1, r1, w_qkv, w_out), scope)), fetch)
        pause()
        done(made)
        text_in, mixed_in, probs_in, ctx_in, normed, inverse, w_mix, w_ctx, g_mix, g_ctx, back, *work = scope
        self_backward(
            text_in, mixed_in, probs_in, ctx_in, normed, inverse, grad_self, w_mix, w_ctx, norms, g_second, g_third,
            g_mix, g_ctx, back, g_blocks, *work, pause, 2, 1,
        )
        made = copies([(g_mix, g_qkv), (g_ctx, g_out), (back, text_grad)], store)
        pause()
        done(made)

    rows = text.shape[0]
    pl.run_scoped(
        alone, *[pltpu.VMEM(r.shape, r.dtype) for r in (text, mixed, probs, ctx, n1, r1, w_qkv, w_out, g_qkv, g_out, text_grad)],
        pltpu.VMEM((rows, 3 * D), f32), pltpu.VMEM((rows, D), f32), pltpu.VMEM((rows, 3 * D), f32), pltpu.VMEM((rows, 3 * D), bf16),
    )
    while left:
        pause()
    scatter.finish(outs)
    for k in range(3):
        swap(k).wait()
    stay().wait()


def backward_all(text, image, ws, norms, saved, grad_after, g_third, g_in, g_outer, slots,
                 plane_first=PLANE_LAST, turned=TURNED_BACK, rounds=ROUNDS, plan=BACK_PLAN, collective=1):
    nw = 8
    n = Z * X * Y * C
    every = Z * X * Y
    items = image.shape[0] // slots
    shapes = [w.shape for w in ws] + [g_in.shape, g_outer.shape, (n * 8, 128)]
    blocks = [(s[0] // n, s[1]) for s in shapes]
    kinds = [bf16] * (nw - 1) + [f32]
    anyspec = pl.BlockSpec(memory_space=pl.ANY)
    dma = pltpu.SemaphoreType.DMA
    shape = jax.ShapeDtypeStruct

    def room(line, plane, other=None):
        return [
            pltpu.VMEM((plane if w in plane_first else other or line if w in turned else line,) + b, k)
            for w, (b, k) in enumerate(zip(blocks, kinds))
        ]

    out = pl.pallas_call(
        functools.partial(backward_kernel, plane_first, turned, rounds, plan),
        out_shape=[shape(b, f32) for b in blocks]
        + [shape((slots // (Y * C), items * Y * C, ENC), bf16), shape(text.shape, f32)]
        + [shape(s, bf16) for s in shapes[:5]] + [shape((Y * C, slots // (Y * C), items, ENC), bf16)],
        in_specs=[VM] * 2 + [anyspec] * 21,
        out_specs=[VM] * nw + [anyspec] * 8,
        scratch_shapes=room(every, every) + room(every, every) + room(Z * Y, 1, Z) + room(Z, X, Z * X) + room(Z + 1, (Z + 1) * X * Y)
        + [pltpu.VMEM((n * 8, 128), f32), pltpu.VMEM(text.shape, f32), pltpu.VMEM((2, D), f32)]
        + [dma((nw, Z))] * 6 + [dma((nw,))] * 5 + [dma((3,)), dma((3,)), dma, dma((12,)), dma((4,))],
        compiler_params=pltpu.CompilerParams(collective_id=collective, has_side_effects=True, vmem_limit_bytes=60 << 20),
        name="backward",
    )(norms, g_third, text, image, *ws, *saved, grad_after, g_in, g_outer)
    return list(out[:nw]), out[nw], out[nw + 1]


step_rates = (0.05, 0.15, 0.05, 0.05, 0.3, 0.05, 0.05, 0.5)
step_decays = (0.01, 0.01, 0.01, 0.01, 0.01, 0.01, 0.01, 0.0)
BOTH = ("items", "patch")


def in_blocks(norms, count):
    width = D // count
    return jnp.pad(norms.reshape(6, count, width).transpose(1, 0, 2), ((0, 0), (0, 2), (0, 128 - width))).reshape(8 * count, 128)


def on_device(direct, text, cotangent, patches, text_lengths, patch_mask, *state):
    masters, firsts, seconds = state[:8], state[8:16], state[16:]
    group, local = patch_mask.shape
    chunks = lax.axis_size("patch")
    items = group // chunks
    devices = chunks * lax.axis_size("items")
    by_slot = patches.transpose(1, 0, 2)
    if direct:
        weights, image, norms, saved = forward_all(text, text_lengths, masters, by_slot, patch_mask, VALID)
    else:
        weights = [lax.all_gather(m.astype(bf16), BOTH, axis=0, tiled=True) for m in masters[:7]]
        blocks = in_blocks(lax.all_gather(masters[7].astype(bf16), BOTH, axis=1, tiled=True).astype(f32), devices)
        image = lax.all_to_all(by_slot.reshape(local, chunks, items, ENC), "patch", 1, 0)
        image = image.reshape(chunks * local * items, ENC)
        masks = patch_bias(patch_mask, lax.axis_index("patch") * local, VALID)
        masks = jnp.pad(masks, ((0, 0), (0, 128 - local))).reshape(chunks, items, 128)
        masks = lax.all_to_all(masks, "patch", 0, 0)
        norms, saved = forward_local(text, text_lengths, image, masks, weights, blocks)
    block_output, g_in, g_outer, grad_after, g_third = feed_forward_call(cotangent, weights[5:7], norms, saved[9])
    if direct:
        reduced, image_grad, text_grad = backward_all(
            text, image, weights[:5], norms, saved, grad_after, g_third, g_in, g_outer, chunks * local
        )
    else:
        text_grad, image_grad, grads, grad_blocks = backward_local(
            text, image, weights[:5], norms, saved, grad_after, g_third, devices
        )
        grads = (*grads, g_in, g_outer)
        reduced = [lax.psum_scatter(g, BOTH, scatter_dimension=0, tiled=True).astype(f32) for g in grads]
        reduced.append(lax.psum_scatter(grad_blocks, BOTH, scatter_dimension=0, tiled=True))
        image_grad = lax.all_to_all(image_grad.reshape(chunks, local, items, ENC), "patch", 0, 1)
        image_grad = image_grad.reshape(local, group, ENC)
    state_shapes = [(m.shape, f32) for m in masters]
    *updated, patch_grad = call(
        functools.partial(adamw, 8, step_decays, step_rates),
        (*masters, *firsts, *seconds, *reduced, image_grad),
        [*state_shapes * 3, (image_grad.shape, f32)], [], "adamw",
    )
    return (block_output, text_grad, patch_grad.transpose(1, 0, 2), *updated)


def solution(mesh):
    rows, cols = P(BOTH, None), P(None, BOTH)
    state = (*[rows] * 7, cols)
    direct = dict(mesh.shape) == {"items": Z * X, "patch": Y * C}
    return jax.shard_map(
        functools.partial(on_device, direct),
        mesh=mesh,
        in_specs=(rows, rows, P("items", "patch", None), P(BOTH), P("items", "patch"), *state * 3),
        out_specs=(rows, rows, P("items", "patch", None), *state * 3),
        check_vma=False,
    )
```
